32 devices in a mesh: section: 2 (over x), tensor: 2 (over core), dp: 8 (over z, y).
Axes of the slice: x: 2, y: 2, z: 4, core: 2. Of those that a mesh axis runs over, the one named last changes fastest.
Arguments:
- inputs: bfloat16 [2, 1024, 2048], P(None, 'dp'), may hold values from -6 to 6
- cotangent: bfloat16 [2, 1024, 2048], P(None, 'dp'), may hold values from -6 to 6
- segments: int32 [2, 1024], P(None, 'dp'), may hold values from 0 to 3, never falling along the last dimension, each value on 1 to 512 neighbouring positions
- w_query: bfloat16 [2, 2048, 2048], P('section', 'dp', 'tensor'), may hold values from -0.125 to 0.125
- key_weight: bfloat16 [2, 2048, 1024], P('section', 'dp', 'tensor'), may hold values from -0.125 to 0.125
- value_weight: bfloat16 [2, 2048, 1024], P('section', 'dp', 'tensor'), may hold values from -0.125 to 0.125
- w_output: bfloat16 [2, 2048, 2048], P('section', 'dp', 'tensor'), may hold values from -0.5 to 0.5
- w_gate: bfloat16 [2, 2048, 6144], P('section', 'dp', 'tensor'), may hold values from -0.125 to 0.125
- w_up: bfloat16 [2, 2048, 6144], P('section', 'dp', 'tensor'), may hold values from -0.125 to 0.125
- w_down: bfloat16 [2, 2048, 6144], P('section', 'dp', 'tensor'), may hold values from -0.078125 to 0.078125
- attn_gain: bfloat16 [2, 2048], P('section', 'dp'), may hold values from 0.5 to 1.5
- mlp_gain: bfloat16 [2, 2048], P('section', 'dp'), may hold values from 0.5 to 1.5
- query_gain: bfloat16 [2, 128], P('section'), may hold values from 0.5 to 1.5
- key_gain: bfloat16 [2, 128], P('section'), may hold values from 0.5 to 1.5
Outputs:
- section_outputs: bfloat16 [2, 2, 1024, 2048], P('section', None, 'dp')
- input_grads: bfloat16 [2, 2, 1024, 2048], P('section', None, 'dp')
- grad_query: float32 [2, 2048, 2048], P('section', 'dp', 'tensor')
- grad_key: float32 [2, 2048, 1024], P('section', 'dp', 'tensor')
- grad_value: float32 [2, 2048, 1024], P('section', 'dp', 'tensor')
- grad_output: float32 [2, 2048, 2048], P('section', 'dp', 'tensor')
- grad_gate: float32 [2, 2048, 6144], P('section', 'dp', 'tensor')
- up_weight_grad: float32 [2, 2048, 6144], P('section', 'dp', 'tensor')
- grad_down: float32 [2, 2048, 6144], P('section', 'dp', 'tensor')
- grad_attn_gain: float32 [2, 2048], P('section', 'dp')
- grad_mlp_gain: float32 [2, 2048], P('section', 'dp')
- grad_query_gain: float32 [2, 128], P('section')
- grad_key_gain: float32 [2, 128], P('section')
The draws below stay inside these ranges and needn't reach their ends.
Inputs may be any that keep to these rules, and one draw needn't show every extreme that they name: `segments`: segment numbers never fall along a micro-batch; each document holds 1 to 512 tokens of a micro-batch.
All inputs are finite; a program needn't handle non-finite values.
Results may differ from the reference program's by a relative error of at most 0.03.
Values may be sent and summed in bfloat16 or wider, within the bound.
No kernel may reach another device: no remote copies, remote signals or barrier semaphores. Data moves between devices by JAX's collectives and lax.ppermute only.
A program may use at most 320 MiB of HBM per device.

```python
import math
from functools import partial
import jax
import jax.numpy as jnp
import numpy as np
from jax import lax

MODEL_DIM = 2048
FF = 6144
NQ = 16
KEY_VALUE_HEADS = 8
HEAD_DIM = 128
MB = 2
LAYER_SECTIONS = 2
TOK_MB = 1024


def block_levels(key, dims, shards, least, largest):
    gain, own = 1.0, jax.random.fold_in(key, 6)
    for axis_at, parts in shards:
        heights = jnp.exp(jax.random.uniform(jax.random.fold_in(own, axis_at), (parts,), jnp.float32, least / len(shards), largest / len(shards)))
        gain = gain * jnp.repeat(heights, dims[axis_at] // parts).reshape([-1 if axis == axis_at else 1 for axis in range(len(dims))])
    return gain


def length_profile(amount, total, most, slope):
    loads = [(1 << 20) // math.isqrt(standing ** slope) + 1 for standing in range(2, amount + 1)]
    spare, counts = total - most - (amount - 1), [1] * (amount - 1)
    while spare > 0:
        movable = [i for i in range(amount - 1) if counts[i] < most]
        whole, budget = sum([loads[i] for i in movable]), spare
        for i in movable:
            addition = min(most - counts[i], max(1, budget * loads[i] // whole), spare)
            counts[i] = counts[i] + addition
            spare = spare - addition
    return np.array([most] + counts)


def ragged(stream_key, amount, total, limit, skew):
    if amount == 2:
        one = jax.random.randint(stream_key, (), max(1, total - limit), min(limit, total - 1) + 1)
        return jnp.stack([one, total - one])
    lengths = jnp.asarray(length_profile(amount, total, limit, skew), jnp.int32)
    twos = (amount - 1) // 2
    giver, taker = lengths[1:1 + 2 * twos:2], lengths[2:2 + 2 * twos:2]
    slack = jnp.minimum(giver - 1, limit - taker)
    shifted = jax.random.randint(jax.random.fold_in(stream_key, 1), (twos,), 0, 1 << 20) % (slack + 1)
    lengths = lengths.at[1:1 + 2 * twos:2].set(giver - shifted).at[2:2 + 2 * twos:2].set(taker + shifted)
    return lengths[jax.random.permutation(jax.random.fold_in(stream_key, 2), amount)]


def bell_draw(own_key, shape, deviation, reach, pieces=(), kind=jnp.bfloat16):
    array = jax.random.normal(own_key, shape, jnp.float32) * deviation
    if len(pieces) > 0:
        array = block_levels(own_key, shape, pieces, -0.22, 0.18) * array
    return jnp.clip(array, min=-reach, max=reach).astype(kind)


def setup_inputs(seed: int = 0) -> dict:
    seeds = jax.random.split(jax.random.key(seed), 15)
    inputs = bell_draw(seeds[0], (MB, TOK_MB, MODEL_DIM), 1.0, 6.0, ((1, 8),))
    cotangent = bell_draw(seeds[1], (MB, TOK_MB, MODEL_DIM), 1.0, 6.0, ((1, 8),))
    segments = jax.vmap(lambda own: jnp.searchsorted(jnp.cumsum(ragged(own, max(3, TOK_MB // 256), TOK_MB, TOK_MB // 2, 1)), jnp.arange(TOK_MB), side="right"))(jax.random.split(seeds[2], MB)).reshape((MB, TOK_MB)).astype(jnp.int32)
    w_query = bell_draw(seeds[3], (LAYER_SECTIONS, MODEL_DIM, NQ * HEAD_DIM), MODEL_DIM ** -0.5, 0.125, ((0, 2), (1, 8), (2, 2)))
    key_weight = bell_draw(seeds[4], (LAYER_SECTIONS, MODEL_DIM, KEY_VALUE_HEADS * HEAD_DIM), MODEL_DIM ** -0.5, 0.125, ((0, 2), (1, 8), (2, 2)))
    value_weight = bell_draw(seeds[5], (LAYER_SECTIONS, MODEL_DIM, KEY_VALUE_HEADS * HEAD_DIM), MODEL_DIM ** -0.5, 0.125, ((0, 2), (1, 8), (2, 2)))
    w_output = bell_draw(seeds[6], (LAYER_SECTIONS, MODEL_DIM, NQ * HEAD_DIM), (NQ * HEAD_DIM // 16) ** -0.5, 0.5, ((0, 2), (1, 8), (2, 2)))
    w_gate = bell_draw(seeds[7], (LAYER_SECTIONS, MODEL_DIM, FF), MODEL_DIM ** -0.5, 0.125, ((0, 2), (1, 8), (2, 2)))
    w_up = bell_draw(seeds[8], (LAYER_SECTIONS, MODEL_DIM, FF), MODEL_DIM ** -0.5, 0.125, ((0, 2), (1, 8), (2, 2)))
    w_down = bell_draw(seeds[9], (LAYER_SECTIONS, MODEL_DIM, FF), FF ** -0.5, 0.078125, ((0, 2), (1, 8), (2, 2)))
    attn_gain = jnp.clip(1.0 + 0.1 * jax.random.normal(seeds[10], (LAYER_SECTIONS, MODEL_DIM), jnp.float32), 0.5, 1.5).astype(jnp.bfloat16)
    mlp_gain = jnp.clip(1.0 + 0.1 * jax.random.normal(seeds[11], (LAYER_SECTIONS, MODEL_DIM), jnp.float32), 0.5, 1.5).astype(jnp.bfloat16)
    query_gain = jnp.clip(1.0 + 0.1 * jax.random.normal(seeds[12], (LAYER_SECTIONS, HEAD_DIM), jnp.float32), 0.5, 1.5).astype(jnp.bfloat16)
    key_gain = jnp.clip(1.0 + 0.1 * jax.random.normal(seeds[13], (LAYER_SECTIONS, HEAD_DIM), jnp.float32), 0.5, 1.5).astype(jnp.bfloat16)
    return {"inputs": inputs, "cotangent": cotangent, "segments": segments, "w_query": w_query, "key_weight": key_weight, "value_weight": value_weight, "w_output": w_output, "w_gate": w_gate, "w_up": w_up, "w_down": w_down, "attn_gain": attn_gain, "mlp_gain": mlp_gain, "query_gain": query_gain, "key_gain": key_gain}


@jax.custom_vjp
def low(v):
    return lax.optimization_barrier(v.astype(jnp.bfloat16)).astype(jnp.float32)

@jax.custom_vjp
def low_back(v):
    return v

def low_keep(v):
    return (low(v), None)

def low_pass(kept, grad):
    return (grad,)

def back_keep(v):
    return (v, None)

def back_low(kept, grad):
    return (low(grad),)
low.defvjp(low_keep, low_pass)
low_back.defvjp(back_keep, back_low)
HIGHEST = lax.Precision.HIGHEST
EPSILON = 1e-06
MASKED = -1e+30

def matmul_plain(left, right):
    return jnp.dot(left, right, precision=HIGHEST, preferred_element_type=jnp.float32)

def matmul_last(left, right):
    return lax.dot_general(left, right, (((1,), (1,)), ((), ())), precision=HIGHEST, preferred_element_type=jnp.float32)

def rms_scale(values, norm_gain):
    return values * lax.rsqrt(lax.optimization_barrier(jnp.mean(values * values, axis=-1, keepdims=True)) + EPSILON) * norm_gain

def rope_tables(positions, head_size):
    half_size = head_size // 2
    freqs = jnp.power(jnp.float32(1000000.0), -jnp.arange(half_size, dtype=jnp.float32) * 2.0 / head_size)
    angles = positions.astype(jnp.float32)[:, None] * freqs[None, :]
    angles = jnp.concatenate([angles, angles], axis=-1)
    return (jnp.cos(angles), jnp.sin(angles))

def rotate_norm(raw_proj, norm_gain, cosine, sine_table):
    head_size = norm_gain.shape[0]
    token_count = raw_proj.shape[0]
    heads = raw_proj.reshape(token_count, -1, head_size)
    normed = rms_scale(heads, norm_gain)
    half_size = head_size // 2
    turned = jnp.concatenate([-normed[..., half_size:], normed[..., :half_size]], axis=-1)
    rotated = normed * cosine[:, None, :] + turned * sine_table[:, None, :]
    return rotated.reshape(token_count, -1)

def attend_block(block_in, keys_all, values_all, key_segs, head_size):
    query_block, block_start = block_in
    row_count = query_block.shape[0]
    kv_heads = keys_all.shape[1] // head_size
    group_size = query_block.shape[1] // keys_all.shape[1]
    query_heads = query_block.reshape(row_count, kv_heads, group_size, head_size)
    key_heads = keys_all.reshape(-1, kv_heads, head_size)
    value_heads = values_all.reshape(-1, kv_heads, head_size)
    scores = jnp.einsum('bngd,snd->ngbs', query_heads, key_heads, precision=HIGHEST) * head_size ** (-0.5)
    scores = low_back(scores)
    query_pos = block_start + jnp.arange(row_count, dtype=jnp.int32)
    key_pos = jnp.arange(keys_all.shape[0], dtype=jnp.int32)
    query_segs = lax.dynamic_slice_in_dim(key_segs, block_start, row_count)
    allowed = (key_pos[None, :] <= query_pos[:, None]) & (query_segs[:, None] == key_segs[None, :])
    scores = jnp.where(allowed[None, None], scores, MASKED)
    highest = lax.optimization_barrier(jnp.max(scores, axis=-1, keepdims=True))
    weights = jnp.exp(scores - highest)
    probs = weights / lax.optimization_barrier(jnp.sum(weights, axis=-1, keepdims=True))
    mixed = jnp.einsum('ngbs,snd->bngd', low(probs), value_heads, precision=HIGHEST)
    return mixed.reshape(row_count, -1)

def layer(layer_in, params, segs, cosine, sine_table):
    w_q, w_k, w_v, w_o, w_g, w_u, w_d, gain_attn, gain_mlp, gain_q, gain_k = params
    token_count = layer_in.shape[0]
    head_size = gain_q.shape[0]
    normed = low(rms_scale(layer_in, gain_attn))
    queries = low_back(matmul_plain(normed, w_q))
    key_raw = low_back(matmul_plain(normed, w_k))
    value_raw = low(low_back(matmul_plain(normed, w_v)))
    query_rot = low(rotate_norm(queries, gain_q, cosine, sine_table))
    key_rot = low(rotate_norm(key_raw, gain_k, cosine, sine_table))
    block_rows = min(512, token_count)
    blocks = token_count // block_rows
    starts = jnp.arange(blocks, dtype=jnp.int32) * block_rows
    attend = jax.checkpoint(partial(attend_block, keys_all=key_rot, values_all=value_raw, key_segs=segs, head_size=head_size))
    attn = lax.map(attend, (query_rot.reshape(blocks, block_rows, -1), starts)).reshape(token_count, -1)
    attn = low(low_back(attn))
    mixed = layer_in + low_back(matmul_last(attn, w_o))
    normed_mlp = low(rms_scale(mixed, gain_mlp))
    gate_raw = low_back(matmul_plain(normed_mlp, w_g))
    up_raw = low_back(matmul_plain(normed_mlp, w_u))
    activated = low(jax.nn.silu(gate_raw) * up_raw)
    return mixed + low_back(matmul_last(activated, w_d))

def reference(inputs, cotangent, segments, w_query, key_weight, value_weight, w_output, w_gate, w_up, w_down, attn_gain, mlp_gain, query_gain, key_gain):
    stacked = (w_query, key_weight, value_weight, w_output, w_gate, w_up, w_down, attn_gain, mlp_gain, query_gain, key_gain)
    first_params = tuple((member[0].astype(jnp.float32) for member in stacked))
    second_params = tuple((member[1].astype(jnp.float32) for member in stacked))
    cosine, sine_table = rope_tables(jnp.arange(TOK_MB, dtype=jnp.int32), HEAD_DIM)

    def full(layer_input, first_set, second_set, joint_zero):
        finals, middles = ([], [])
        for batch_index in range(MB):
            middle = layer(layer_input[batch_index], first_set, segments[batch_index], cosine, sine_table)
            passed = low(low_back(middle)) + joint_zero[batch_index]
            finals.append(layer(passed, second_set, segments[batch_index], cosine, sine_table))
            middles.append(middle)
        return (jnp.stack(finals), jnp.stack(middles))
    start_value = inputs.astype(jnp.float32)
    joint_value = jnp.zeros_like(start_value)
    final_out, backward, middle_out = jax.vjp(full, start_value, first_params, second_params, joint_value, has_aux=True)
    grad_in, grad_first, grad_second, grad_joint = backward(cotangent.astype(jnp.float32))
    outputs = jnp.stack([middle_out, final_out]).astype(jnp.bfloat16)
    in_grads = jnp.stack([grad_in, grad_joint]).astype(jnp.bfloat16)
    weight_grads = [jnp.stack([grad_first[index], grad_second[index]]) for index in range(11)]
    return (outputs, in_grads, weight_grads[0], weight_grads[1], weight_grads[2], weight_grads[3], weight_grads[4], weight_grads[5], weight_grads[6], weight_grads[7], weight_grads[8], weight_grads[9], weight_grads[10])
```

```python
from functools import partial

import jax
import jax.numpy as jnp
from jax import lax
from jax.experimental import pallas as pl
from jax.experimental.pallas import tpu as pltpu
from jax.sharding import PartitionSpec as P

EPSILON = 1e-06
MASKED = -1e30


def shifted(x, axis, by):
    count = lax.axis_size(axis)
    pairs = [(i, i + by) for i in range(count) if 0 <= i + by < count]
    return lax.ppermute(x, axis, pairs)


def as_sent(x):

    def short(part):
        return part.astype(jnp.bfloat16) if part.dtype == jnp.float32 else part

    return jax.tree.map(short, x)


def dot_plain(left, right):
    return jnp.dot(left, right, preferred_element_type=jnp.float32)


def dot_last(left, right):
    return lax.dot_general(
        left, right, (((1,), (1,)), ((), ())), preferred_element_type=jnp.float32
    )


def dot_first(left, right):
    return lax.dot_general(
        left, right, (((0,), (0,)), ((), ())), preferred_element_type=jnp.float32
    )


def rms_scale(values, norm_gain):
    return (
        values * lax.rsqrt(jnp.mean(values * values, axis=-1, keepdims=True) + EPSILON) * norm_gain
    )


def swiglu(gate_raw, up_raw):
    return jax.nn.silu(gate_raw) * up_raw


def rope_tables(positions, head_size):
    half_size = head_size // 2
    freqs = jnp.power(
        jnp.float32(1000000.0), -jnp.arange(half_size, dtype=jnp.float32) * 2.0 / head_size
    )
    angles = positions.astype(jnp.float32)[:, None] * freqs[None, :]
    angles = jnp.concatenate([angles, angles], axis=-1)
    return (jnp.cos(angles), jnp.sin(angles))


def rotate_norm(raw_proj, norm_gain, cosine, sine_table):
    head_size = norm_gain.shape[0]
    token_count = raw_proj.shape[0]
    heads = raw_proj.reshape(token_count, -1, head_size)
    normed = rms_scale(heads, norm_gain)
    half_size = head_size // 2
    turned = jnp.concatenate([-normed[..., half_size:], normed[..., :half_size]], axis=-1)
    rotated = normed * cosine[:, None, :] + turned * sine_table[:, None, :]
    return rotated.reshape(token_count, -1)


def scores_for(queries, keys_all, allowed, head_size):
    row_count = queries.shape[0]
    kv_heads = keys_all.shape[1] // head_size
    group_size = queries.shape[1] // keys_all.shape[1]
    query_heads = queries.reshape(row_count, kv_heads, group_size, head_size)
    key_heads = keys_all.reshape(keys_all.shape[0], kv_heads, head_size)
    scores = jnp.einsum(
        "bngd,snd->ngbs", query_heads, key_heads, preferred_element_type=jnp.float32
    ) * head_size ** (-0.5)
    return (jnp.where(allowed[None, None], scores, MASKED), query_heads, key_heads)


def attend(queries, keys_all, values_all, allowed, head_size):
    scores, query_heads, key_heads = scores_for(queries, keys_all, allowed, head_size)
    highest = jnp.max(scores, axis=-1, keepdims=True)
    weights = jnp.exp(scores - highest)
    total = jnp.sum(weights, axis=-1, keepdims=True)
    probs = (weights / total).astype(jnp.bfloat16)
    value_heads = values_all.reshape(key_heads.shape)
    mixed = jnp.einsum("ngbs,snd->bngd", probs, value_heads, preferred_element_type=jnp.float32)
    return (mixed.reshape(queries.shape[0], -1).astype(jnp.bfloat16), highest + jnp.log(total))


def attend_back(queries, keys_all, values_all, allowed, log_total, attn_grad, head_size):
    scores, query_heads, key_heads = scores_for(queries, keys_all, allowed, head_size)
    probs = jnp.exp(scores - log_total)
    value_heads = values_all.reshape(key_heads.shape)
    grad_heads = attn_grad.reshape(query_heads.shape)
    prob_grad = jnp.einsum(
        "bngd,snd->ngbs", grad_heads, value_heads, preferred_element_type=jnp.float32
    )
    delta = jnp.sum(probs * prob_grad, axis=-1, keepdims=True)
    score_grad = (probs * (prob_grad - delta)).astype(jnp.bfloat16)
    scale = head_size ** (-0.5)
    query_back = jnp.einsum(
        "ngbs,snd->bngd", score_grad, key_heads, preferred_element_type=jnp.float32
    )
    key_back = jnp.einsum(
        "ngbs,bngd->snd", score_grad, query_heads, preferred_element_type=jnp.float32
    )
    value_back = jnp.einsum(
        "ngbs,bngd->snd", probs.astype(jnp.bfloat16), grad_heads, preferred_element_type=jnp.float32
    )
    key_count = keys_all.shape[0]
    return (
        query_back.reshape(queries.shape[0], -1) * scale,
        key_back.reshape(key_count, -1) * scale,
        value_back.reshape(key_count, -1),
    )


def per_device_wide(
    inputs,
    cotangent,
    segments,
    w_query,
    key_weight,
    value_weight,
    w_output,
    w_gate,
    w_up,
    w_down,
    attn_gain,
    mlp_gain,
    query_gain,
    key_gain,
):
    section_first = lax.axis_index("section") == 0
    gathered = (
        lax.all_gather(w_query[0], "dp", axis=0, tiled=True),
        lax.all_gather(key_weight[0], "dp", axis=0, tiled=True),
        lax.all_gather(value_weight[0], "dp", axis=0, tiled=True),
        lax.all_gather(w_output[0], "dp", axis=0, tiled=True),
        lax.all_gather(w_gate[0], "dp", axis=0, tiled=True),
        lax.all_gather(w_up[0], "dp", axis=0, tiled=True),
        lax.all_gather(w_down[0], "dp", axis=0, tiled=True),
        lax.all_gather(attn_gain[0], "dp", axis=0, tiled=True),
        lax.all_gather(mlp_gain[0], "dp", axis=0, tiled=True),
    )
    w_q, w_k, w_v, w_o, w_g, w_u, w_d = gathered[:7]
    gain_attn = gathered[7].astype(jnp.float32)
    gain_mlp = gathered[8].astype(jnp.float32)
    gain_q = query_gain[0].astype(jnp.float32)
    gain_k = key_gain[0].astype(jnp.float32)
    head_size = gain_q.shape[0]
    doc_table = lax.all_gather(segments, "dp", axis=1, tiled=True)
    batch_count, row_count, model_width = inputs.shape
    token_count = doc_table.shape[1]
    positions = lax.axis_index("dp") * row_count + jnp.arange(row_count, dtype=jnp.int32)
    key_pos = jnp.arange(token_count, dtype=jnp.int32)
    cosine, sine_table = rope_tables(positions, head_size)
    rope_query = partial(rotate_norm, cosine=cosine, sine_table=sine_table)
    arrived = jnp.zeros((row_count, model_width), jnp.bfloat16)
    stored_steps, outgoing_steps = ([], [])
    for step_index in range(batch_count + 1):
        early = min(step_index, batch_count - 1)
        late = max(step_index - 1, 0)
        layer_in = jnp.where(
            section_first, inputs[early].astype(jnp.float32), arrived.astype(jnp.float32)
        )
        own_segs = jnp.where(section_first, segments[early], segments[late])
        doc_row = jnp.where(section_first, doc_table[early], doc_table[late])
        forward_normed = rms_scale(layer_in, gain_attn).astype(jnp.bfloat16)
        forward_queries = dot_plain(forward_normed, w_q)
        forward_key_raw = dot_plain(forward_normed, w_k)
        forward_value_raw = dot_plain(forward_normed, w_v).astype(jnp.bfloat16)
        forward_query_rot = rope_query(forward_queries, gain_q).astype(jnp.bfloat16)
        forward_key_rot = rope_query(forward_key_raw, gain_k).astype(jnp.bfloat16)
        forward_keys_all = lax.all_gather(forward_key_rot, "dp", axis=0, tiled=True)
        forward_values_all = lax.all_gather(forward_value_raw, "dp", axis=0, tiled=True)
        forward_allowed = (key_pos[None, :] <= positions[:, None]) & (
            own_segs[:, None] == doc_row[None, :]
        )
        forward_attn, forward_log_total = attend(
            forward_query_rot, forward_keys_all, forward_values_all, forward_allowed, head_size
        )
        forward_mixed = layer_in + lax.psum(dot_last(forward_attn, w_o), "tensor")
        forward_normed_mlp = rms_scale(forward_mixed, gain_mlp).astype(jnp.bfloat16)
        forward_gate_raw = dot_plain(forward_normed_mlp, w_g)
        forward_up_raw = dot_plain(forward_normed_mlp, w_u)
        forward_activated = swiglu(forward_gate_raw, forward_up_raw).astype(jnp.bfloat16)
        layer_out = forward_mixed + lax.psum(dot_last(forward_activated, w_d), "tensor")
        forward_stored = (
            layer_in,
            forward_normed,
            forward_queries,
            forward_key_raw,
            forward_query_rot,
            forward_key_rot,
            forward_value_raw,
            forward_attn,
            forward_log_total,
            forward_mixed,
            forward_normed_mlp,
            forward_gate_raw,
            forward_up_raw,
            forward_activated,
            forward_allowed,
        )
        layer_out, stored = (layer_out, forward_stored)
        outgoing = layer_out.astype(jnp.bfloat16)
        stored_steps.append(stored)
        outgoing_steps.append(outgoing)
        if step_index < batch_count:
            arrived = shifted(outgoing, "section", 1)
    section_out = jnp.stack(
        [
            jnp.where(section_first, outgoing_steps[batch_index], outgoing_steps[batch_index + 1])
            for batch_index in range(batch_count)
        ]
    )
    back_arrived = jnp.zeros((row_count, model_width), jnp.bfloat16)
    grad_steps = []
    totals = None
    norm_totals = None
    for step_index in range(batch_count + 1):
        early_batch = min(batch_count - step_index, batch_count - 1)
        late_batch = max(batch_count - 1 - step_index, 0)
        stored = jax.tree.map(
            lambda a, b: jnp.where(section_first, a, b),
            stored_steps[early_batch],
            stored_steps[late_batch + 1],
        )
        valid = jnp.where(
            section_first,
            jnp.float32(1.0 if step_index >= 1 else 0.0),
            jnp.float32(1.0 if step_index < batch_count else 0.0),
        )
        grad_out = (
            jnp.where(
                section_first,
                back_arrived.astype(jnp.float32),
                cotangent[late_batch].astype(jnp.float32),
            )
            * valid
        )
        (
            backward_layer_in,
            normed,
            queries,
            key_raw,
            query_rot,
            key_rot,
            value_raw,
            attn,
            log_total,
            mixed,
            normed_mlp,
            gate_raw,
            up_raw,
            activated,
            allowed,
        ) = stored[:15]
        keys_all = lax.all_gather(key_rot, "dp", axis=0, tiled=True)
        values_all = lax.all_gather(value_raw, "dp", axis=0, tiled=True)
        mlp_grad = grad_out.astype(jnp.bfloat16)
        act_grad = dot_plain(mlp_grad, w_d)
        grad_wd = dot_first(mlp_grad, activated)
        unused, swiglu_back = jax.vjp(swiglu, gate_raw, up_raw)
        gate_grad, up_grad = swiglu_back(act_grad)
        gate_grad = gate_grad.astype(jnp.bfloat16)
        up_grad = up_grad.astype(jnp.bfloat16)
        grad_wg = dot_first(normed_mlp, gate_grad)
        grad_wu = dot_first(normed_mlp, up_grad)
        normed_mlp_grad = lax.psum(
            (dot_last(gate_grad, w_g) + dot_last(up_grad, w_u)).astype(jnp.bfloat16), "tensor"
        ).astype(jnp.float32)
        unused, mlp_norm_back = jax.vjp(rms_scale, mixed, gain_mlp)
        mixed_part, grad_gain_mlp = mlp_norm_back(normed_mlp_grad)
        mixed_grad = grad_out + mixed_part
        branch_low = mixed_grad.astype(jnp.bfloat16)
        attn_grad = dot_plain(branch_low, w_o).astype(jnp.bfloat16)
        grad_wo = dot_first(branch_low, attn)
        query_back, key_back, value_back = attend_back(
            query_rot, keys_all, values_all, allowed, log_total, attn_grad, head_size
        )
        backward_key_total = lax.psum_scatter(
            key_back.astype(jnp.bfloat16), "dp", scatter_dimension=0, tiled=True
        ).astype(jnp.float32)
        value_total = lax.psum_scatter(
            value_back.astype(jnp.bfloat16), "dp", scatter_dimension=0, tiled=True
        )
        unused, key_rope_back = jax.vjp(rope_query, key_raw, gain_k)
        key_gradient, grad_gain_k = key_rope_back(backward_key_total)
        key_gradient = key_gradient.astype(jnp.bfloat16)
        unused, query_rope_back = jax.vjp(rope_query, queries, gain_q)
        query_grad, grad_gain_q = query_rope_back(query_back)
        query_grad = query_grad.astype(jnp.bfloat16)
        grad_wq = dot_first(normed, query_grad)
        grad_wk = dot_first(normed, key_gradient)
        grad_wv = dot_first(normed, value_total)
        normed_grad = lax.psum(
            (
                dot_last(query_grad, w_q) + dot_last(key_gradient, w_k) + dot_last(value_total, w_v)
            ).astype(jnp.bfloat16),
            "tensor",
        ).astype(jnp.float32)
        unused, attn_norm_back = jax.vjp(rms_scale, backward_layer_in, gain_attn)
        input_part, grad_gain_attn = attn_norm_back(normed_grad)
        weight_part = (
            grad_wq,
            grad_wk,
            grad_wv,
            grad_wo,
            grad_wg,
            grad_wu,
            grad_wd,
            grad_gain_attn,
            grad_gain_mlp,
        )
        input_grad, weight_part, norm_part = (
            mixed_grad + input_part,
            weight_part,
            (grad_gain_q, grad_gain_k),
        )
        outgoing = input_grad.astype(jnp.bfloat16)
        grad_steps.append(outgoing)
        if step_index < batch_count:
            back_arrived = shifted(outgoing, "section", -1)
        totals = (
            weight_part if totals is None else tuple((a + b for a, b in zip(totals, weight_part)))
        )
        norm_totals = (
            norm_part
            if norm_totals is None
            else tuple((a + b for a, b in zip(norm_totals, norm_part)))
        )
    shards = jax.tree.map(
        lambda part: part.astype(jnp.float32),
        lax.psum_scatter(as_sent(totals), "dp", scatter_dimension=0, tiled=True),
    )
    query_total, key_total = lax.psum(norm_totals, ("tensor", "dp"))
    input_grads = jnp.stack(
        [
            jnp.where(
                section_first,
                grad_steps[batch_count - batch_index],
                grad_steps[batch_count - 1 - batch_index],
            )
            for batch_index in range(batch_count)
        ]
    )
    return (
        (section_out[None], input_grads[None])
        + tuple((member[None] for member in shards))
        + (query_total[None], key_total[None])
    )


def paired(x, axis, flip):
    count = lax.axis_size(axis)
    return lax.ppermute(x, axis, [(i, i ^ flip) for i in range(count)])


def ring_order(count):
    return list(range(0, count, 2)) + list(range(count - 1, 0, -2))


def ring(x, by):
    order = ring_order(lax.axis_size("dp"))
    count = len(order)
    return lax.ppermute(x, "dp", [(order[i], order[(i + by) % count]) for i in range(count)])


def far_order(count):
    order = [0]
    for step in range(1, count // 2):
        order += [step, count - step]
    return order + [count // 2]


def gather_ring(chunk):
    count = lax.axis_size("dp")
    half = count // 2
    mid = chunk.shape[0] // 2
    held = {0: chunk}
    down = up = chunk
    for step in range(1, half):
        down, up = ring(down, 1), ring(up, -1)
        held[count - step], held[step] = down, up
    last = [ring(down[:mid], 1), ring(up[mid:], -1)]
    pieces = [held[k] for k in far_order(count)[:-1]] + last
    others = [paired(piece, "tensor", 1) for piece in pieces]
    return jnp.concatenate(pieces + others, axis=0)


def scatter_ring(own, other):
    count = lax.axis_size("dp")
    half = count // 2
    order = far_order(count)
    rows = own.shape[0] // count
    mid = rows // 2
    near = (count - 3) * rows
    arrived = jnp.concatenate(
        [paired(other[:near], "tensor", 1), paired(other[near:], "tensor", 1)], axis=0
    )
    total = own + arrived.astype(jnp.float32)
    part = {k: total[i * rows : (i + 1) * rows] for i, k in enumerate(order)}
    plus = ring(part[half][:mid].astype(jnp.bfloat16), 1).astype(jnp.float32)
    minus = ring(part[half][mid:].astype(jnp.bfloat16), -1).astype(jnp.float32)
    for step in range(half - 1, 0, -1):
        ahead, behind = part[step], part[count - step]
        if step == half - 1:
            ahead = jnp.concatenate([ahead[:mid] + plus, ahead[mid:]], axis=0)
            behind = jnp.concatenate([behind[:mid], behind[mid:] + minus], axis=0)
        else:
            ahead, behind = ahead + plus, behind + minus
        plus = ring(ahead.astype(jnp.bfloat16), 1).astype(jnp.float32)
        minus = ring(behind.astype(jnp.bfloat16), -1).astype(jnp.float32)
    return part[0] + plus + minus


def product_scattered(acts, weights, contract):
    top = acts[0].shape[0] // 2

    def product(rows):
        return sum(contract(a[rows], w) for a, w in zip(acts, weights))

    other = product(slice(top, None)).astype(jnp.bfloat16)
    return scatter_ring(product(slice(0, top)), other)


def place_rows(mine, theirs, flags, widths):
    count = len(mine)
    rows = mine[0].shape[0]

    def kernel(flags_ref, *refs):
        ins, outs = refs[: 2 * count], refs[2 * count :]
        me = flags_ref[0]

        def fill(blocks):
            for s in range(count):
                at = pl.multiple_of((me ^ s) * rows, rows)
                left = 0
                for out, width in zip(outs, widths):
                    out[pl.ds(at, rows), :] = blocks[s][:, left : left + width]
                    left += width

        @pl.when(flags_ref[1] == 0)
        def _():
            fill(ins[:count])

        @pl.when(flags_ref[1] != 0)
        def _():
            fill(ins[count:])

    whole = pl.BlockSpec(memory_space=pltpu.VMEM)
    size = 2 * count * rows * sum(widths)
    return pl.pallas_call(
        kernel,
        out_shape=[jax.ShapeDtypeStruct((count * rows, w), mine[0].dtype) for w in widths],
        in_specs=[pl.BlockSpec(memory_space=pltpu.SMEM)] + [whole] * (2 * count),
        out_specs=[whole] * len(widths),
        cost_estimate=pl.CostEstimate(flops=0, bytes_accessed=3 * size, transcendentals=0),
    )(flags, *mine, *theirs)


def place_columns(firsts, seconds, flags, widths, shared):
    count = len(firsts[0])
    rows = firsts[0][0].shape[0]

    def kernel(flags_ref, *refs):
        ins, outs = refs[: 4 * count], refs[4 * count :]
        me = flags_ref[0]
        plane = flags_ref[1]

        def fill(low, high):
            left = 0
            for out, width, wide in zip(outs, widths, shared):
                for s in range(0, count, 1 if not wide else 2):
                    column = (me ^ s) * width if not wide else ((me ^ s) // 2) * width
                    column = pl.multiple_of(column, width)
                    for blocks, at in ((low, 0), (high, rows)):
                        value = blocks[s][:, left : left + width].astype(jnp.float32)
                        if wide:
                            value += blocks[s + 1][:, left : left + width].astype(jnp.float32)
                        out[at : at + rows, pl.ds(column, width)] = value
                left += width

        @pl.when(plane == 0)
        def _():
            fill(ins[:count], ins[2 * count : 3 * count])

        @pl.when(plane != 0)
        def _():
            fill(ins[3 * count :], ins[count : 2 * count])

    whole = pl.BlockSpec(memory_space=pltpu.VMEM)
    columns = [w * count // (2 if wide else 1) for w, wide in zip(widths, shared)]
    size = 4 * 2 * rows * sum(columns) + 8 * count * rows * sum(widths)
    return pl.pallas_call(
        kernel,
        out_shape=[jax.ShapeDtypeStruct((2 * rows, c), jnp.float32) for c in columns],
        in_specs=[pl.BlockSpec(memory_space=pltpu.SMEM)] + [whole] * (4 * count),
        out_specs=[whole] * len(widths),
        cost_estimate=pl.CostEstimate(flops=0, bytes_accessed=size, transcendentals=0),
    )(flags, *firsts[0], *firsts[1], *seconds[0], *seconds[1])


def head_attend(query, key, value, allowed):
    scores = dot_last(query, key) * query.shape[1] ** (-0.5)
    scores = jnp.where(allowed, scores, MASKED)
    highest = jnp.max(scores, axis=-1, keepdims=True)
    weights = jnp.exp(scores - highest)
    total = jnp.sum(weights, axis=-1, keepdims=True)
    probs = (weights / total).astype(jnp.bfloat16)
    return dot_plain(probs, value).astype(jnp.bfloat16), highest + jnp.log(total)


def head_attend_back(query, key, value, allowed, log_total, grad):
    scale = query.shape[1] ** (-0.5)
    scores = jnp.where(allowed, dot_last(query, key) * scale, MASKED)
    probs = jnp.exp(scores - log_total)
    prob_grad = dot_last(grad, value)
    delta = jnp.sum(probs * prob_grad, axis=-1, keepdims=True)
    score_grad = (probs * (prob_grad - delta)).astype(jnp.bfloat16)
    return (
        dot_plain(score_grad, key) * scale,
        dot_first(score_grad, query) * scale,
        dot_first(probs.astype(jnp.bfloat16), grad),
    )


def per_device(
    inputs,
    cotangent,
    segments,
    w_query,
    key_weight,
    value_weight,
    w_output,
    w_gate,
    w_up,
    w_down,
    attn_gain,
    mlp_gain,
    query_gain,
    key_gain,
):
    count = lax.axis_size("dp")
    plane = lax.axis_index("section")
    me = lax.axis_index("dp")
    core = lax.axis_index("tensor")
    flags = [jnp.stack([me, plane ^ layer]).astype(jnp.int32) for layer in range(2)]
    model_width = inputs.shape[2]
    rows = inputs.shape[1] // 2
    head_size = query_gain.shape[1]
    ff_width = w_gate.shape[2] // count
    group_size = w_query.shape[2] // key_weight.shape[2]
    gain_width = attn_gain.shape[1]

    def by_layer(own):
        theirs = paired(own, "section", 1)
        first = plane == 0
        return [jnp.where(first, own, theirs), jnp.where(first, theirs, own)]

    def own_rows(array):
        return lax.dynamic_slice(array, (plane, core * rows, 0), (1, rows, model_width))[0]

    gains = jnp.concatenate([attn_gain[0], mlp_gain[0], query_gain[0], key_gain[0]])
    gains = jnp.concatenate(by_layer(gains.astype(jnp.float32)))
    docs = lax.dynamic_index_in_dim(segments, plane, 0, keepdims=False).astype(jnp.float32)
    note = jnp.concatenate([gains, docs])
    notes = jnp.stack([note] + [paired(note, "dp", s) for s in range(1, count)])
    notes = jnp.concatenate(
        [lax.dynamic_slice_in_dim(notes, me ^ j, 1, axis=0) for j in range(count)], axis=0
    )
    per_layer = gains.shape[0] // 2
    layer_gains = []
    for layer in range(2):
        at = layer * per_layer
        layer_gains.append(
            (
                notes[:, at : at + gain_width].reshape(-1),
                notes[:, at + gain_width : at + 2 * gain_width].reshape(-1),
                gains[at + 2 * gain_width : at + 2 * gain_width + head_size],
                gains[at + 2 * gain_width + head_size : at + per_layer],
            )
        )
    doc_table = notes[:, 2 * per_layer :].reshape(count, 2, rows)

    place = jnp.where(me % 2 == 0, me // 2, count - 1 - me // 2)
    docs_near, docs_far, pos_near, pos_far = [], [], [], []
    for distance in far_order(count):
        spot = (place + distance) % count
        owner = jnp.where(spot < count // 2, 2 * spot, 2 * (count - 1 - spot) + 1)
        block = lax.dynamic_index_in_dim(doc_table, owner, 0, keepdims=False)
        docs_near.append(lax.dynamic_index_in_dim(block, core, 0, keepdims=False))
        docs_far.append(lax.dynamic_index_in_dim(block, 1 - core, 0, keepdims=False))
        start = owner * 2 * rows
        pos_near.append(start + core * rows + jnp.arange(rows, dtype=jnp.int32))
        pos_far.append(start + (1 - core) * rows + jnp.arange(rows, dtype=jnp.int32))
    docs_all = jnp.concatenate(docs_near + docs_far)
    positions = jnp.concatenate(pos_near + pos_far)
    allowed = (positions[None, :] <= positions[:, None]) & (docs_all[:, None] == docs_all[None, :])
    cosine, sine_table = rope_tables(positions, head_size)
    rope = partial(rotate_norm, cosine=cosine, sine_table=sine_table)

    def turned(pieces, after):
        def block(to):
            return jnp.concatenate(
                [
                    lax.dynamic_slice_in_dim(
                        array, (to // share) * width, width, axis=1
                    )
                    for array, width, share in pieces
                ],
                axis=1,
            )

        def late(x):
            return x if after is None else lax.optimization_barrier((x, after))[0]

        mine = [block(me)] + [paired(late(block(me ^ s)), "dp", s) for s in range(1, count)]
        theirs = [paired(x, "section", 1) for x in mine]
        return mine, theirs

    attn_pieces = (
        (w_query[0], head_size, 1),
        (key_weight[0], head_size, group_size),
        (value_weight[0], head_size, group_size),
        (w_output[0], head_size, 1),
    )
    mlp_pieces = ((w_gate[0], ff_width, 1), (w_up[0], ff_width, 1), (w_down[0], ff_width, 1))
    attn_blocks = turned(attn_pieces, None)
    mlp_blocks = turned(mlp_pieces, attn_blocks[0][-1])
    weights = []
    for layer in range(2):
        w_qkv, w_o = place_rows(*attn_blocks, flags[layer], (3 * head_size, head_size))
        w_gu, w_d = place_rows(*mlp_blocks, flags[layer], (2 * ff_width, ff_width))
        weights.append((w_qkv, w_o, w_gu, w_d))

    def forward(layer_in, layer):
        w_qkv, w_o, w_gu, w_d = weights[layer]
        gain_attn, gain_mlp, gain_q, gain_k = layer_gains[layer]
        normed = gather_ring(rms_scale(layer_in, gain_attn).astype(jnp.bfloat16))
        raw = dot_plain(normed, w_qkv)
        queries, key_raw = raw[:, :head_size], raw[:, head_size : 2 * head_size]
        value = raw[:, 2 * head_size :].astype(jnp.bfloat16)
        query_rot = rope(queries, gain_q).astype(jnp.bfloat16)
        key_rot = rope(key_raw, gain_k).astype(jnp.bfloat16)
        attn, log_total = head_attend(query_rot, key_rot, value, allowed)
        mixed = layer_in + product_scattered([attn], [w_o], dot_last)
        normed_mlp = gather_ring(rms_scale(mixed, gain_mlp).astype(jnp.bfloat16))
        raw_mlp = dot_plain(normed_mlp, w_gu)
        gate_raw, up_raw = raw_mlp[:, :ff_width], raw_mlp[:, ff_width:]
        activated = swiglu(gate_raw, up_raw).astype(jnp.bfloat16)
        layer_out = mixed + product_scattered([activated], [w_d], dot_last)
        stored = (
            layer_in, normed, queries, key_raw, value, query_rot, key_rot, attn, log_total,
            mixed, normed_mlp, gate_raw, up_raw, activated,
        )
        return layer_out, stored

    def halves_sum(grad):
        wide = grad.astype(jnp.bfloat16).reshape(count, 2, -1, grad.shape[1])
        sent = lax.dynamic_index_in_dim(wide, 1 - plane, 1, keepdims=False)
        kept = lax.dynamic_index_in_dim(
            grad.reshape(count, 2, -1, grad.shape[1]), plane, 1, keepdims=False
        )
        total = (kept + paired(sent, "section", 1).astype(jnp.float32)).astype(jnp.bfloat16)

        def block(to):
            return lax.dynamic_index_in_dim(total, to, 0, keepdims=False)

        return [block(me)] + [paired(block(me ^ s), "dp", s) for s in range(1, count)]

    def to_owner(blocks, layer):
        return [lax.ppermute(x, "section", [(1 - layer, layer)]) for x in blocks]

    def backward(grad_out, stored, layer):
        (
            layer_in, normed, queries, key_raw, value, query_rot, key_rot, attn, log_total,
            mixed, normed_mlp, gate_raw, up_raw, activated,
        ) = stored
        w_qkv, w_o, w_gu, w_d = weights[layer]
        gain_attn, gain_mlp, gain_q, gain_k = layer_gains[layer]
        out_low = gather_ring(grad_out.astype(jnp.bfloat16))
        act_grad = dot_plain(out_low, w_d)
        unused, swiglu_back = jax.vjp(swiglu, gate_raw, up_raw)
        gate_grad, up_grad = swiglu_back(act_grad)
        raw_grad = jnp.concatenate([gate_grad, up_grad], axis=1).astype(jnp.bfloat16)
        normed_mlp_grad = product_scattered([raw_grad], [w_gu], dot_last)
        grad_mlp = jnp.concatenate(
            [dot_first(normed_mlp, raw_grad), dot_first(out_low, activated)], axis=1
        )
        mlp_sent = halves_sum(grad_mlp)
        mlp_done = to_owner(mlp_sent, layer)
        unused, mlp_norm_back = jax.vjp(rms_scale, mixed, gain_mlp)
        mixed_part, grad_gain_mlp = mlp_norm_back(normed_mlp_grad)
        mixed_grad = grad_out + mixed_part
        branch_low = gather_ring(mixed_grad.astype(jnp.bfloat16))
        attn_grad = dot_plain(branch_low, w_o).astype(jnp.bfloat16)
        query_back, key_back, value_back = head_attend_back(
            query_rot, key_rot, value, allowed, log_total, attn_grad
        )
        unused, key_rope_back = jax.vjp(rope, key_raw, gain_k)
        key_grad, grad_gain_k = key_rope_back(key_back)
        unused, query_rope_back = jax.vjp(rope, queries, gain_q)
        query_grad, grad_gain_q = query_rope_back(query_back)
        qkv_grad = jnp.concatenate([query_grad, key_grad, value_back], axis=1).astype(jnp.bfloat16)
        normed_grad = product_scattered([qkv_grad], [w_qkv], dot_last)
        grad_attn = jnp.concatenate(
            [dot_first(normed, qkv_grad), dot_first(branch_low, attn)], axis=1
        )
        attn_sent = halves_sum(grad_attn)
        attn_done = to_owner(attn_sent, layer)
        unused, attn_norm_back = jax.vjp(rms_scale, layer_in, gain_attn)
        input_part, grad_gain_attn = attn_norm_back(normed_grad)
        small = (grad_gain_attn, grad_gain_mlp, grad_gain_q, grad_gain_k)
        return mixed_grad + input_part, (mlp_sent, mlp_done, attn_sent, attn_done), small

    out_first, stored_first = forward(own_rows(inputs).astype(jnp.float32), 0)
    out_first = out_first.astype(jnp.bfloat16)
    out_second, stored_second = forward(out_first.astype(jnp.float32), 1)
    out_second = out_second.astype(jnp.bfloat16)
    grad_second, big_second, small_second = backward(
        own_rows(cotangent).astype(jnp.float32), stored_second, 1
    )
    grad_second = grad_second.astype(jnp.bfloat16)
    grad_first, big_first, small_first = backward(grad_second.astype(jnp.float32), stored_first, 0)
    grad_first = grad_first.astype(jnp.bfloat16)

    def by_section(first, second):
        kept = jnp.where(plane == 0, first, second)
        taken = paired(jnp.where(plane == 0, second, first), "section", 1)
        both = jnp.where(plane == 0, jnp.stack([kept, taken]), jnp.stack([taken, kept]))
        facing = paired(both, "tensor", 1)
        return jnp.where(
            core == 0,
            jnp.concatenate([both, facing], axis=1),
            jnp.concatenate([facing, both], axis=1),
        )[None]

    section_out = by_section(out_first, out_second)
    input_grads = by_section(grad_first, grad_second)

    flag = flags[0]
    attn_grads = place_columns(
        (big_first[2], big_second[2]),
        (big_first[3], big_second[3]),
        flag,
        (head_size,) * 4,
        (False, True, True, False),
    )
    mlp_grads = place_columns(
        (big_first[0], big_second[0]),
        (big_first[1], big_second[1]),
        flag,
        (ff_width,) * 3,
        (False,) * 3,
    )

    rows_of = jnp.concatenate(
        [
            part.reshape(count, -1)
            for small in (small_first, small_second)
            for part in (
                small[0],
                small[1],
                jnp.tile(small[2], count),
                jnp.tile(small[3], count),
            )
        ],
        axis=1,
    )

    def row(to):
        return lax.dynamic_index_in_dim(rows_of, to, 0, keepdims=False)

    gain_sum = row(me)
    for s in range(1, count):
        gain_sum = gain_sum + paired(row(me ^ s), "dp", s)
    gain_sum = gain_sum + paired(gain_sum, "tensor", 1)
    gain_sum = gain_sum + paired(gain_sum, "section", 1)
    mine = jnp.where(plane == 0, gain_sum[:per_layer], gain_sum[per_layer:])
    grad_gain_attn = mine[:gain_width]
    grad_gain_mlp = mine[gain_width : 2 * gain_width]
    grad_gain_q = mine[2 * gain_width : 2 * gain_width + head_size]
    grad_gain_k = mine[2 * gain_width + head_size :]
    shards = (
        attn_grads[0], attn_grads[1], attn_grads[2], attn_grads[3],
        mlp_grads[0], mlp_grads[1], mlp_grads[2],
        grad_gain_attn, grad_gain_mlp, grad_gain_q, grad_gain_k,
    )
    return (section_out, input_grads) + tuple(part[None] for part in shards)


def fits(mesh):
    sizes = dict(mesh.shape)
    return sizes["dp"] == 8 and sizes["tensor"] == 2 and sizes["section"] == 2


def solution(mesh):
    return jax.shard_map(
        per_device if fits(mesh) else per_device_wide,
        mesh=mesh,
        in_specs=(
            P(None, "dp", None),
            P(None, "dp", None),
            P(None, "dp"),
            P("section", "dp", "tensor"),
            P("section", "dp", "tensor"),
            P("section", "dp", "tensor"),
            P("section", "dp", "tensor"),
            P("section", "dp", "tensor"),
            P("section", "dp", "tensor"),
            P("section", "dp", "tensor"),
            P("section", "dp"),
            P("section", "dp"),
            P("section", None),
            P("section", None),
        ),
        out_specs=(
            P("section", None, "dp", None),
            P("section", None, "dp", None),
            P("section", "dp", "tensor"),
            P("section", "dp", "tensor"),
            P("section", "dp", "tensor"),
            P("section", "dp", "tensor"),
            P("section", "dp", "tensor"),
            P("section", "dp", "tensor"),
            P("section", "dp", "tensor"),
            P("section", "dp"),
            P("section", "dp"),
            P("section", None),
            P("section", None),
        ),
        check_vma=False,
    )
```

```python
from functools import partial

import jax
import jax.numpy as jnp
from jax import lax
from jax.experimental import pallas as pl
from jax.experimental.pallas import tpu as pltpu
from jax.sharding import PartitionSpec as P

EPSILON = 1e-06
MASKED = -1e30


def shifted(x, axis, by):
    count = lax.axis_size(axis)
    pairs = [(i, i + by) for i in range(count) if 0 <= i + by < count]
    return lax.ppermute(x, axis, pairs)


def as_sent(x):

    def short(part):
        return part.astype(jnp.bfloat16) if part.dtype == jnp.float32 else part

    return jax.tree.map(short, x)


def dot_plain(left, right):
    return jnp.dot(left, right, preferred_element_type=jnp.float32)


def dot_last(left, right):
    return lax.dot_general(
        left, right, (((1,), (1,)), ((), ())), preferred_element_type=jnp.float32
    )


def dot_first(left, right):
    return lax.dot_general(
        left, right, (((0,), (0,)), ((), ())), preferred_element_type=jnp.float32
    )


def rms_scale(values, norm_gain):
    return (
        values * lax.rsqrt(jnp.mean(values * values, axis=-1, keepdims=True) + EPSILON) * norm_gain
    )


def swiglu(gate_raw, up_raw):
    return jax.nn.silu(gate_raw) * up_raw


def rope_tables(positions, head_size):
    half_size = head_size // 2
    freqs = jnp.power(
        jnp.float32(1000000.0), -jnp.arange(half_size, dtype=jnp.float32) * 2.0 / head_size
    )
    angles = positions.astype(jnp.float32)[:, None] * freqs[None, :]
    angles = jnp.concatenate([angles, angles], axis=-1)
    return (jnp.cos(angles), jnp.sin(angles))


def rotate_norm(raw_proj, norm_gain, cosine, sine_table):
    head_size = norm_gain.shape[0]
    token_count = raw_proj.shape[0]
    heads = raw_proj.reshape(token_count, -1, head_size)
    normed = rms_scale(heads, norm_gain)
    half_size = head_size // 2
    turned = jnp.concatenate([-normed[..., half_size:], normed[..., :half_size]], axis=-1)
    rotated = normed * cosine[:, None, :] + turned * sine_table[:, None, :]
    return rotated.reshape(token_count, -1)


def scores_for(queries, keys_all, allowed, head_size):
    row_count = queries.shape[0]
    kv_heads = keys_all.shape[1] // head_size
    group_size = queries.shape[1] // keys_all.shape[1]
    query_heads = queries.reshape(row_count, kv_heads, group_size, head_size)
    key_heads = keys_all.reshape(keys_all.shape[0], kv_heads, head_size)
    scores = jnp.einsum(
        "bngd,snd->ngbs", query_heads, key_heads, preferred_element_type=jnp.float32
    ) * head_size ** (-0.5)
    return (jnp.where(allowed[None, None], scores, MASKED), query_heads, key_heads)


def attend(queries, keys_all, values_all, allowed, head_size):
    scores, _, key_heads = scores_for(queries, keys_all, allowed, head_size)
    highest = jnp.max(scores, axis=-1, keepdims=True)
    weights = jnp.exp(scores - highest)
    total = jnp.sum(weights, axis=-1, keepdims=True)
    probs = (weights / total).astype(jnp.bfloat16)
    value_heads = values_all.reshape(key_heads.shape)
    mixed = jnp.einsum("ngbs,snd->bngd", probs, value_heads, preferred_element_type=jnp.float32)
    return (mixed.reshape(queries.shape[0], -1).astype(jnp.bfloat16), highest + jnp.log(total))


def attend_back(queries, keys_all, values_all, allowed, log_total, attn_grad, head_size):
    scores, query_heads, key_heads = scores_for(queries, keys_all, allowed, head_size)
    probs = jnp.exp(scores - log_total)
    value_heads = values_all.reshape(key_heads.shape)
    grad_heads = attn_grad.reshape(query_heads.shape)
    prob_grad = jnp.einsum(
        "bngd,snd->ngbs", grad_heads, value_heads, preferred_element_type=jnp.float32
    )
    delta = jnp.sum(probs * prob_grad, axis=-1, keepdims=True)
    score_grad = (probs * (prob_grad - delta)).astype(jnp.bfloat16)
    scale = head_size ** (-0.5)
    query_back = jnp.einsum(
        "ngbs,snd->bngd", score_grad, key_heads, preferred_element_type=jnp.float32
    )
    key_back = jnp.einsum(
        "ngbs,bngd->snd", score_grad, query_heads, preferred_element_type=jnp.float32
    )
    value_back = jnp.einsum(
        "ngbs,bngd->snd", probs.astype(jnp.bfloat16), grad_heads, preferred_element_type=jnp.float32
    )
    key_count = keys_all.shape[0]
    return (
        query_back.reshape(queries.shape[0], -1) * scale,
        key_back.reshape(key_count, -1) * scale,
        value_back.reshape(key_count, -1),
    )


def per_device_wide(
    inputs,
    cotangent,
    segments,
    w_query,
    key_weight,
    value_weight,
    w_output,
    w_gate,
    w_up,
    w_down,
    attn_gain,
    mlp_gain,
    query_gain,
    key_gain,
):
    section_first = lax.axis_index("section") == 0
    gathered = (
        lax.all_gather(w_query[0], "dp", axis=0, tiled=True),
        lax.all_gather(key_weight[0], "dp", axis=0, tiled=True),
        lax.all_gather(value_weight[0], "dp", axis=0, tiled=True),
        lax.all_gather(w_output[0], "dp", axis=0, tiled=True),
        lax.all_gather(w_gate[0], "dp", axis=0, tiled=True),
        lax.all_gather(w_up[0], "dp", axis=0, tiled=True),
        lax.all_gather(w_down[0], "dp", axis=0, tiled=True),
        lax.all_gather(attn_gain[0], "dp", axis=0, tiled=True),
        lax.all_gather(mlp_gain[0], "dp", axis=0, tiled=True),
    )
    w_q, w_k, w_v, w_o, w_g, w_u, w_d = gathered[:7]
    gain_attn = gathered[7].astype(jnp.float32)
    gain_mlp = gathered[8].astype(jnp.float32)
    gain_q = query_gain[0].astype(jnp.float32)
    gain_k = key_gain[0].astype(jnp.float32)
    head_size = gain_q.shape[0]
    doc_table = lax.all_gather(segments, "dp", axis=1, tiled=True)
    batch_count, row_count, model_width = inputs.shape
    token_count = doc_table.shape[1]
    positions = lax.axis_index("dp") * row_count + jnp.arange(row_count, dtype=jnp.int32)
    key_pos = jnp.arange(token_count, dtype=jnp.int32)
    cosine, sine_table = rope_tables(positions, head_size)
    rope_query = partial(rotate_norm, cosine=cosine, sine_table=sine_table)
    arrived = jnp.zeros((row_count, model_width), jnp.bfloat16)
    stored_steps, outgoing_steps = ([], [])
    for step_index in range(batch_count + 1):
        early = min(step_index, batch_count - 1)
        late = max(step_index - 1, 0)
        layer_in = jnp.where(
            section_first, inputs[early].astype(jnp.float32), arrived.astype(jnp.float32)
        )
        own_segs = jnp.where(section_first, segments[early], segments[late])
        doc_row = jnp.where(section_first, doc_table[early], doc_table[late])
        forward_normed = rms_scale(layer_in, gain_attn).astype(jnp.bfloat16)
        forward_queries = dot_plain(forward_normed, w_q)
        forward_key_raw = dot_plain(forward_normed, w_k)
        forward_value_raw = dot_plain(forward_normed, w_v).astype(jnp.bfloat16)
        forward_query_rot = rope_query(forward_queries, gain_q).astype(jnp.bfloat16)
        forward_key_rot = rope_query(forward_key_raw, gain_k).astype(jnp.bfloat16)
        forward_keys_all = lax.all_gather(forward_key_rot, "dp", axis=0, tiled=True)
        forward_values_all = lax.all_gather(forward_value_raw, "dp", axis=0, tiled=True)
        forward_allowed = (key_pos[None, :] <= positions[:, None]) & (
            own_segs[:, None] == doc_row[None, :]
        )
        forward_attn, forward_log_total = attend(
            forward_query_rot, forward_keys_all, forward_values_all, forward_allowed, head_size
        )
        forward_mixed = layer_in + lax.psum(dot_last(forward_attn, w_o), "tensor")
        forward_normed_mlp = rms_scale(forward_mixed, gain_mlp).astype(jnp.bfloat16)
        forward_gate_raw = dot_plain(forward_normed_mlp, w_g)
        forward_up_raw = dot_plain(forward_normed_mlp, w_u)
        forward_activated = swiglu(forward_gate_raw, forward_up_raw).astype(jnp.bfloat16)
        layer_out = forward_mixed + lax.psum(dot_last(forward_activated, w_d), "tensor")
        forward_stored = (
            layer_in,
            forward_normed,
            forward_queries,
            forward_key_raw,
            forward_query_rot,
            forward_key_rot,
            forward_value_raw,
            forward_attn,
            forward_log_total,
            forward_mixed,
            forward_normed_mlp,
            forward_gate_raw,
            forward_up_raw,
            forward_activated,
            forward_allowed,
        )
        layer_out, stored = (layer_out, forward_stored)
        outgoing = layer_out.astype(jnp.bfloat16)
        stored_steps.append(stored)
        outgoing_steps.append(outgoing)
        if step_index < batch_count:
            arrived = shifted(outgoing, "section", 1)
    section_out = jnp.stack(
        [
            jnp.where(section_first, outgoing_steps[batch_index], outgoing_steps[batch_index + 1])
            for batch_index in range(batch_count)
        ]
    )
    back_arrived = jnp.zeros((row_count, model_width), jnp.bfloat16)
    grad_steps = []
    totals = None
    norm_totals = None
    for step_index in range(batch_count + 1):
        early_batch = min(batch_count - step_index, batch_count - 1)
        late_batch = max(batch_count - 1 - step_index, 0)
        stored = jax.tree.map(
            lambda a, b: jnp.where(section_first, a, b),
            stored_steps[early_batch],
            stored_steps[late_batch + 1],
        )
        valid = jnp.where(
            section_first,
            jnp.float32(1.0 if step_index >= 1 else 0.0),
            jnp.float32(1.0 if step_index < batch_count else 0.0),
        )
        grad_out = (
            jnp.where(
                section_first,
                back_arrived.astype(jnp.float32),
                cotangent[late_batch].astype(jnp.float32),
            )
            * valid
        )
        (
            backward_layer_in,
            normed,
            queries,
            key_raw,
            query_rot,
            key_rot,
            value_raw,
            attn,
            log_total,
            mixed,
            normed_mlp,
            gate_raw,
            up_raw,
            activated,
            allowed,
        ) = stored[:15]
        keys_all = lax.all_gather(key_rot, "dp", axis=0, tiled=True)
        values_all = lax.all_gather(value_raw, "dp", axis=0, tiled=True)
        mlp_grad = grad_out.astype(jnp.bfloat16)
        act_grad = dot_plain(mlp_grad, w_d)
        grad_wd = dot_first(mlp_grad, activated)
        unused, swiglu_back = jax.vjp(swiglu, gate_raw, up_raw)
        gate_grad, up_grad = swiglu_back(act_grad)
        gate_grad = gate_grad.astype(jnp.bfloat16)
        up_grad = up_grad.astype(jnp.bfloat16)
        grad_wg = dot_first(normed_mlp, gate_grad)
        grad_wu = dot_first(normed_mlp, up_grad)
        normed_mlp_grad = lax.psum(
            (dot_last(gate_grad, w_g) + dot_last(up_grad, w_u)).astype(jnp.bfloat16), "tensor"
        ).astype(jnp.float32)
        unused, mlp_norm_back = jax.vjp(rms_scale, mixed, gain_mlp)
        mixed_part, grad_gain_mlp = mlp_norm_back(normed_mlp_grad)
        mixed_grad = grad_out + mixed_part
        branch_low = mixed_grad.astype(jnp.bfloat16)
        attn_grad = dot_plain(branch_low, w_o).astype(jnp.bfloat16)
        grad_wo = dot_first(branch_low, attn)
        query_back, key_back, value_back = attend_back(
            query_rot, keys_all, values_all, allowed, log_total, attn_grad, head_size
        )
        backward_key_total = lax.psum_scatter(
            key_back.astype(jnp.bfloat16), "dp", scatter_dimension=0, tiled=True
        ).astype(jnp.float32)
        value_total = lax.psum_scatter(
            value_back.astype(jnp.bfloat16), "dp", scatter_dimension=0, tiled=True
        )
        unused, key_rope_back = jax.vjp(rope_query, key_raw, gain_k)
        key_gradient, grad_gain_k = key_rope_back(backward_key_total)
        key_gradient = key_gradient.astype(jnp.bfloat16)
        unused, query_rope_back = jax.vjp(rope_query, queries, gain_q)
        query_grad, grad_gain_q = query_rope_back(query_back)
        query_grad = query_grad.astype(jnp.bfloat16)
        grad_wq = dot_first(normed, query_grad)
        grad_wk = dot_first(normed, key_gradient)
        grad_wv = dot_first(normed, value_total)
        normed_grad = lax.psum(
            (
                dot_last(query_grad, w_q) + dot_last(key_gradient, w_k) + dot_last(value_total, w_v)
            ).astype(jnp.bfloat16),
            "tensor",
        ).astype(jnp.float32)
        unused, attn_norm_back = jax.vjp(rms_scale, backward_layer_in, gain_attn)
        input_part, grad_gain_attn = attn_norm_back(normed_grad)
        weight_part = (
            grad_wq,
            grad_wk,
            grad_wv,
            grad_wo,
            grad_wg,
            grad_wu,
            grad_wd,
            grad_gain_attn,
            grad_gain_mlp,
        )
        input_grad, weight_part, norm_part = (
            mixed_grad + input_part,
            weight_part,
            (grad_gain_q, grad_gain_k),
        )
        outgoing = input_grad.astype(jnp.bfloat16)
        grad_steps.append(outgoing)
        if step_index < batch_count:
            back_arrived = shifted(outgoing, "section", -1)
        totals = (
            weight_part if totals is None else tuple((a + b for a, b in zip(totals, weight_part)))
        )
        norm_totals = (
            norm_part
            if norm_totals is None
            else tuple((a + b for a, b in zip(norm_totals, norm_part)))
        )
    shards = jax.tree.map(
        lambda part: part.astype(jnp.float32),
        lax.psum_scatter(as_sent(totals), "dp", scatter_dimension=0, tiled=True),
    )
    query_total, key_total = lax.psum(norm_totals, ("tensor", "dp"))
    input_grads = jnp.stack(
        [
            jnp.where(
                section_first,
                grad_steps[batch_count - batch_index],
                grad_steps[batch_count - 1 - batch_index],
            )
            for batch_index in range(batch_count)
        ]
    )
    return (
        (section_out[None], input_grads[None])
        + tuple((member[None] for member in shards))
        + (query_total[None], key_total[None])
    )


def paired(x, axis, flip):
    count = lax.axis_size(axis)
    return lax.ppermute(x, axis, [(i, i ^ flip) for i in range(count)])


def ring_order(count):
    return list(range(0, count, 2)) + list(range(count - 1, 0, -2))


def ring(x, by):
    order = ring_order(lax.axis_size("dp"))
    count = len(order)
    pairs = []
    for core, step in ((0, by), (1, -by)):
        for i in range(count):
            pairs.append((core * count + order[i], core * count + order[(i + step) % count]))
    return lax.ppermute(x, ("tensor", "dp"), pairs)


def received_order(count):
    half = count // 2
    return [(0, False)] + [(s, lag) for s in range(1, half) for lag in (False, True)] + [(half, False)]


def near_chunks(count):
    return 2 * (count // 2 - 2) + 1


def gate(value, token):
    return lax.optimization_barrier((value, token))[0]


def whole_vmem(count):
    return [pl.BlockSpec(memory_space=pltpu.VMEM)] * count


def joined(pieces):
    rows = sum(piece.shape[0] for piece in pieces)
    width = pieces[0].shape[1]

    def kernel(*refs):
        at = 0
        for ref in refs[:-1]:
            refs[-1][at : at + ref.shape[0], :] = ref[...]
            at += ref.shape[0]

    return pl.pallas_call(
        kernel,
        out_shape=jax.ShapeDtypeStruct((rows, width), pieces[0].dtype),
        in_specs=whole_vmem(len(pieces)),
        out_specs=pl.BlockSpec(memory_space=pltpu.VMEM),
        cost_estimate=pl.CostEstimate(flops=0, bytes_accessed=4 * rows * width, transcendentals=0),
    )(*pieces)


def gather_ring(chunk):
    count = lax.axis_size("dp")
    half = count // 2
    lead, lag = chunk, paired(chunk, "tensor", 1)
    chunks, token = [chunk], None
    for step in range(1, half + 1):
        lead = ring(lead, 1)
        chunks.append(lead)
        if step < half:
            lag = ring(lag, 1)
            chunks.append(lag)
        if step == half - 1:
            token = lead
    cut = near_chunks(count)
    near, far = joined(gate(chunks[:cut], token)), joined(chunks[cut:])
    return [near, far, paired(near, "tensor", 1), paired(far, "tensor", 1)], token


def multiplied(parts, weight):
    return jnp.concatenate(parts, axis=0), by_parts(parts, weight)


def by_parts(parts, weight):
    return jnp.concatenate([dot_plain(part, weight) for part in parts], axis=0)


def product_scattered(act, weight):
    count = lax.axis_size("dp")
    half = count // 2
    side = act.shape[0] // 2
    rows = side // count
    near = near_chunks(count) * rows
    far_sum = dot_last(act[side + near :], weight).astype(jnp.bfloat16)
    near_sum = dot_last(act[side : side + near], weight).astype(jnp.bfloat16)
    own = dot_last(act[:side], weight)
    far_sum = paired(far_sum, "tensor", 1)
    near_sum = paired(near_sum, "tensor", 1)
    spots = {key: i * rows for i, key in enumerate(received_order(count))}

    def part(hops, lag):
        at = spots[hops, lag]
        extra = far_sum[at - near :][:rows] if at >= near else near_sum[at : at + rows]
        return own[at : at + rows] + extra.astype(jnp.float32)

    def hop(value, hops, lag):
        total = part(hops, lag)
        if value is not None:
            total = total + value.astype(jnp.float32)
        return ring(total.astype(jnp.bfloat16), -1)

    lead = lag = token = None
    for hops in range(half, 0, -1):
        lead = hop(lead, hops, False)
        if hops < half:
            lag = hop(lag, hops, True)
        if hops == half - 1:
            token = lead
    across = paired(lag, "tensor", 1)
    return part(0, False) + lead.astype(jnp.float32) + across.astype(jnp.float32), token


def place_rows(blocks, flags, widths):
    count = len(blocks)
    rows, total = blocks[0].shape
    part = rows // 2

    def kernel(flags_ref, *refs):
        for s in range(count):
            left = 0
            for out, width in zip(refs[count:], widths):
                for half in range(2):
                    at = pl.multiple_of((flags_ref[0] ^ s) * part + half * count * part, part)
                    top = half * part
                    out[pl.ds(at, part), :] = refs[s][top : top + part, left : left + width]
                left += width

    size = 2 * count * rows * total
    return pl.pallas_call(
        kernel,
        out_shape=[jax.ShapeDtypeStruct((count * rows, w), blocks[0].dtype) for w in widths],
        in_specs=[pl.BlockSpec(memory_space=pltpu.SMEM)] + whole_vmem(count),
        out_specs=whole_vmem(len(widths)),
        cost_estimate=pl.CostEstimate(flops=0, bytes_accessed=2 * size, transcendentals=0),
    )(flags, *blocks)


def place_columns(first, second, flags, widths, shared):
    count = len(first)
    rows = first[0].shape[0]
    columns = [w * count // (2 if wide else 1) for w, wide in zip(widths, shared)]
    total = sum(columns)

    def kernel(flags_ref, *refs):
        kept, sent = refs[2 * count :]

        def fill(out, blocks):
            left = base = 0
            for width, wide, room in zip(widths, shared, columns):
                for s in range(0, count, 2 if wide else 1):
                    index = flags_ref[0] ^ s
                    at = base + (index // 2 if wide else index) * width
                    value = blocks[s][:, left : left + width]
                    if wide:
                        value = value.astype(jnp.float32) + blocks[s + 1][
                            :, left : left + width
                        ].astype(jnp.float32)
                    out[:, pl.ds(pl.multiple_of(at, 128), width)] = value.astype(out.dtype)
                left += width
                base += room

        @pl.when(flags_ref[1] == 0)
        def _():
            fill(kept, refs[:count])
            fill(sent, refs[count : 2 * count])

        @pl.when(flags_ref[1] != 0)
        def _():
            fill(sent, refs[:count])
            fill(kept, refs[count : 2 * count])

    return pl.pallas_call(
        kernel,
        out_shape=[jax.ShapeDtypeStruct((rows, total), first[0].dtype)] * 2,
        in_specs=[pl.BlockSpec(memory_space=pltpu.SMEM)] + whole_vmem(2 * count),
        out_specs=whole_vmem(2),
        cost_estimate=pl.CostEstimate(
            flops=0, bytes_accessed=4 * count * rows * sum(widths) * 2, transcendentals=0
        ),
    )(flags, *first, *second)


def head_attend(query, key, value, allowed):
    scores = dot_last(query, key) * query.shape[1] ** (-0.5)
    scores = jnp.where(allowed, scores, MASKED)
    highest = jnp.max(scores, axis=-1, keepdims=True)
    weights = jnp.exp(scores - highest)
    total = jnp.sum(weights, axis=-1, keepdims=True)
    probs = (weights / total).astype(jnp.bfloat16)
    return dot_plain(probs, value).astype(jnp.bfloat16), highest + jnp.log(total)


def head_attend_back(query, key, value, allowed, log_total, grad):
    scale = query.shape[1] ** (-0.5)
    scores = jnp.where(allowed, dot_last(query, key) * scale, MASKED)
    probs = jnp.exp(scores - log_total)
    prob_grad = dot_last(grad, value)
    delta = jnp.sum(probs * prob_grad, axis=-1, keepdims=True)
    score_grad = (probs * (prob_grad - delta)).astype(jnp.bfloat16)
    return (
        dot_plain(score_grad, key) * scale,
        dot_first(score_grad, query) * scale,
        dot_first(probs.astype(jnp.bfloat16), grad),
    )


def per_device(
    inputs,
    cotangent,
    segments,
    w_query,
    key_weight,
    value_weight,
    w_output,
    w_gate,
    w_up,
    w_down,
    attn_gain,
    mlp_gain,
    query_gain,
    key_gain,
):
    count = lax.axis_size("dp")
    plane = lax.axis_index("section")
    me = lax.axis_index("dp")
    core = lax.axis_index("tensor")
    flags = jnp.stack([me, plane]).astype(jnp.int32)
    model_width = inputs.shape[2]
    rows = inputs.shape[1] // 2
    head_size = query_gain.shape[1]
    ff_width = w_gate.shape[2] // count
    group_size = w_query.shape[2] // key_weight.shape[2]
    gain_width = attn_gain.shape[1]

    def by_layer(own):
        theirs = paired(own, "section", 1)
        first = plane == 0
        return [jnp.where(first, own, theirs), jnp.where(first, theirs, own)]

    part = gain_width // 2

    def halved(array):
        wide = array.reshape(-1, count, 2, part)
        return jnp.swapaxes(wide, 1, 2).reshape(array.shape)

    def unhalved(array):
        wide = array.reshape(-1, 2, count, part)
        return jnp.swapaxes(wide, 1, 2).reshape(array.shape)

    def own_rows(array):
        own = lax.dynamic_slice(array, (plane, core * rows, 0), (1, rows, model_width))[0]
        return halved(own)

    gains = jnp.concatenate([attn_gain[0], mlp_gain[0], query_gain[0], key_gain[0]])
    gains = jnp.concatenate(by_layer(gains.astype(jnp.float32)))
    docs = lax.dynamic_index_in_dim(segments, plane, 0, keepdims=False).astype(jnp.float32)
    note = jnp.concatenate([gains, docs])
    notes = jnp.stack([note] + [paired(note, "dp", s) for s in range(1, count)])
    notes = jnp.concatenate(
        [lax.dynamic_slice_in_dim(notes, me ^ j, 1, axis=0) for j in range(count)], axis=0
    )
    per_layer = gains.shape[0] // 2
    layer_gains = []
    for layer in range(2):
        at = layer * per_layer
        layer_gains.append(
            (
                halved(notes[:, at : at + gain_width].reshape(-1)),
                halved(notes[:, at + gain_width : at + 2 * gain_width].reshape(-1)),
                gains[at + 2 * gain_width : at + 2 * gain_width + head_size],
                gains[at + 2 * gain_width + head_size : at + per_layer],
            )
        )
    doc_table = notes[:, 2 * per_layer :].reshape(count, 2, rows)

    place = jnp.where(me % 2 == 0, me // 2, count - 1 - me // 2)
    docs_parts, pos_parts = ([], []), ([], [])
    away = 2 * core - 1
    for at in range(2):
        for hops, lag in received_order(count):
            side = core if lag == bool(at) else 1 - core
            spot = (place + (away if at == 0 else -away) * hops + count) % count
            owner = jnp.where(spot < count // 2, 2 * spot, 2 * (count - 1 - spot) + 1)
            block = lax.dynamic_index_in_dim(doc_table, owner, 0, keepdims=False)
            docs_parts[at].append(lax.dynamic_index_in_dim(block, side, 0, keepdims=False))
            start = owner * 2 * rows + side * rows
            pos_parts[at].append(start + jnp.arange(rows, dtype=jnp.int32))
    docs_all = jnp.concatenate(docs_parts[0] + docs_parts[1])
    positions = jnp.concatenate(pos_parts[0] + pos_parts[1])
    allowed = (positions[None, :] <= positions[:, None]) & (docs_all[:, None] == docs_all[None, :])
    cosine, sine_table = rope_tables(positions, head_size)
    rope = partial(rotate_norm, cosine=cosine, sine_table=sine_table)

    def cut(pieces):
        def block(to):
            return jnp.concatenate(
                [
                    lax.dynamic_slice_in_dim(array, (to // share) * width, width, axis=1)
                    for array, width, share in pieces
                ],
                axis=1,
            )

        return [block(me ^ s) for s in range(count)]

    def turn(blocks):
        return [blocks[0]] + [paired(blocks[s], "dp", s) for s in range(1, count)]

    def both_layers(blocks, widths):
        sets = []
        for placed in place_rows(blocks, flags, widths):
            facing = paired(placed, "section", 1)
            sets.append([jnp.where(plane == layer, placed, facing) for layer in range(2)])
        return sets

    pieces_of = {
        "qk": ((w_query[0], head_size, 1), (key_weight[0], head_size, group_size)),
        "vo": ((value_weight[0], head_size, group_size), (w_output[0], head_size, 1)),
        "g": ((w_gate[0], ff_width, 1),),
        "u": ((w_up[0], ff_width, 1),),
        "d": ((w_down[0], ff_width, 1),),
    }
    sliced = {name: cut(pieces) for name, pieces in pieces_of.items()}
    turned, weights = {}, {}

    def attention(raw, value, layer):
        _, _, gain_q, gain_k = layer_gains[layer]
        queries, key_raw = raw[:, :head_size], raw[:, head_size:]
        value = value.astype(jnp.bfloat16)
        query_rot = rope(queries, gain_q).astype(jnp.bfloat16)
        key_rot = rope(key_raw, gain_k).astype(jnp.bfloat16)
        attn, log_total = head_attend(query_rot, key_rot, value, allowed)
        return attn, (queries, key_raw, value, query_rot, key_rot, log_total)

    def forward(layer_in, layer):
        gain_attn, gain_mlp, _, _ = layer_gains[layer]
        if layer == 0:
            turned["qk"] = turn(sliced["qk"])
            parts, token = gather_ring(layer_in.astype(jnp.bfloat16))
            raw_in = joined(parts).astype(jnp.float32)
            weights["qk"] = both_layers(turned["qk"], (2 * head_size,))[0]
            turned["vo"] = turn(gate(sliced["vo"], turned["qk"]))
            weights["v"], weights["o"] = both_layers(turned["vo"], (head_size, head_size))
            turned["g"] = turn(gate(sliced["g"], turned["vo"]))
            normed = rms_scale(raw_in, gain_attn).astype(jnp.bfloat16)
            raw = dot_plain(normed, weights["qk"][0])
            value = dot_plain(normed, weights["v"][0])
        else:
            chunk = rms_scale(layer_in, gain_attn).astype(jnp.bfloat16)
            parts, token = gather_ring(chunk)
            normed, raw = multiplied(parts, weights["qk"][layer])
            value = by_parts(parts, weights["v"][layer])
        attn, kept = attention(raw, value, layer)
        if layer == 0:
            weights["g"] = both_layers(gate(turned["g"], attn), (ff_width,))[0]
            turned["u"] = turn(gate(sliced["u"], turned["g"]))
            extra = None
        else:
            cotangent_rows = own_rows(cotangent)
            extra, token = gather_ring(gate(cotangent_rows, raw))
            attn = gate(attn, token)
        summed, token = product_scattered(attn, weights["o"][layer])
        mixed = layer_in + summed
        if layer == 0:
            weights["u"] = both_layers(gate(turned["u"], mixed), (ff_width,))[0]
            turned["d"] = turn(gate(sliced["d"], turned["u"]))
            weights["gu"] = [
                jnp.concatenate([weights["g"][i], weights["u"][i]], axis=1) for i in range(2)
            ]
        parts, token = gather_ring(rms_scale(mixed, gain_mlp).astype(jnp.bfloat16))
        if layer == 0:
            weights["d"] = both_layers(gate(turned["d"], parts[1]), (ff_width,))[0]
        normed_mlp, raw_mlp = multiplied(parts, weights["gu"][layer])
        gate_raw, up_raw = raw_mlp[:, :ff_width], raw_mlp[:, ff_width:]
        activated = swiglu(gate_raw, up_raw).astype(jnp.bfloat16)
        summed, token = product_scattered(activated, weights["d"][layer])
        stored = (layer_in, normed, kept, attn, mixed, normed_mlp, gate_raw, up_raw, activated)
        return mixed + summed, stored, extra

    def halves(grad):
        span = grad.shape[0] // 2
        sent = lax.dynamic_slice_in_dim(grad, (1 - plane) * span, span, axis=0)
        kept = lax.dynamic_slice_in_dim(grad, plane * span, span, axis=0)
        return kept, paired(sent.astype(jnp.bfloat16), "section", 1)

    last_turn = []

    def returned(pair, token):
        kept, taken = pair
        if token is not None:
            taken = gate(taken, token)
        total = (kept + taken.astype(jnp.float32)).astype(jnp.bfloat16)
        blocks = [lax.dynamic_slice_in_dim(total, (me ^ s) * part, part, axis=0) for s in range(count)]
        if last_turn:
            blocks = gate(blocks, last_turn[-1])
        last_turn.append(turn(blocks))
        return last_turn[-1]

    def backward(gathered, grad_out, stored, layer, back):
        layer_in, normed, kept, attn, mixed, normed_mlp, gate_raw, up_raw, activated = stored
        queries, key_raw, value, query_rot, key_rot, log_total = kept
        gain_attn, gain_mlp, gain_q, gain_k = layer_gains[layer]
        out_low, act_grad = multiplied(gathered, weights["d"][layer])
        unused, swiglu_back = jax.vjp(swiglu, gate_raw, up_raw)
        gate_grad, up_grad = swiglu_back(act_grad)
        raw_grad = jnp.concatenate([gate_grad, up_grad], axis=1).astype(jnp.bfloat16)
        summed, token = product_scattered(raw_grad, weights["gu"][layer])
        sums = {}
        sums["d"] = halves(dot_first(out_low, activated))
        sums["gu"] = halves(dot_first(normed_mlp, raw_grad))
        back["d"] = returned(sums["d"], token)
        unused, mlp_norm_back = jax.vjp(rms_scale, mixed, gain_mlp)
        mixed_part, grad_gain_mlp = mlp_norm_back(summed)
        mixed_grad = grad_out + mixed_part
        parts, token = gather_ring(mixed_grad.astype(jnp.bfloat16))
        branch_low, attn_grad = multiplied(parts, weights["o"][layer])
        back["gu"] = returned(sums["gu"], parts[0])
        query_back, key_back, value_back = head_attend_back(
            query_rot, key_rot, value, allowed, log_total, attn_grad.astype(jnp.bfloat16)
        )
        unused, key_rope_back = jax.vjp(rope, key_raw, gain_k)
        key_grad, grad_gain_k = key_rope_back(key_back)
        unused, query_rope_back = jax.vjp(rope, queries, gain_q)
        query_grad, grad_gain_q = query_rope_back(query_back)
        qkv_grad = jnp.concatenate([query_grad, key_grad, value_back], axis=1).astype(jnp.bfloat16)
        summed, token = product_scattered(qkv_grad, weights["qkv"][layer])
        grad_attn = [dot_first(normed, qkv_grad), dot_first(branch_low, attn)]
        sums["attn"] = halves(jnp.concatenate(grad_attn, axis=1))
        unused, attn_norm_back = jax.vjp(rms_scale, layer_in, gain_attn)
        input_part, grad_gain_attn = attn_norm_back(summed)
        small = (grad_gain_attn, grad_gain_mlp, grad_gain_q, grad_gain_k)
        points = (mixed_grad, branch_low, qkv_grad)
        return mixed_grad + input_part, sums["attn"], small, points

    out_first, stored_first, _ = forward(own_rows(inputs).astype(jnp.float32), 0)
    out_first = out_first.astype(jnp.bfloat16)
    weights["qkv"] = [
        jnp.concatenate([weights["qk"][i], weights["v"][i]], axis=1) for i in range(2)
    ]
    out_second, stored_second, gathered = forward(out_first.astype(jnp.float32), 1)
    out_second = out_second.astype(jnp.bfloat16)
    back_second, back_first = {}, {}
    grad_second, late, small_second, points = backward(
        gathered, own_rows(cotangent).astype(jnp.float32), stored_second, 1, back_second
    )
    grad_second = grad_second.astype(jnp.bfloat16)
    gathered, token = gather_ring(grad_second)
    back_second["attn"] = returned(late, token)
    grad_first, late, small_first, points = backward(
        gathered, grad_second.astype(jnp.float32), stored_first, 0, back_first
    )
    grad_first = grad_first.astype(jnp.bfloat16)
    back_first["attn"] = returned(late, None)

    def by_section(first, second):
        first, second = unhalved(first), unhalved(second)
        kept = jnp.where(plane == 0, first, second)
        taken = paired(jnp.where(plane == 0, second, first), "section", 1)
        both = jnp.where(plane == 0, jnp.stack([kept, taken]), jnp.stack([taken, kept]))
        facing = paired(both, "tensor", 1)
        return jnp.where(
            core == 0,
            jnp.concatenate([both, facing], axis=1),
            jnp.concatenate([facing, both], axis=1),
        )[None]

    section_out = by_section(out_first, out_second)
    input_grads = by_section(grad_first, grad_second)

    def owned(name, widths, shared, token):
        firsts = back_first[name] if token is None else gate(back_first[name], token)
        kept, sent = place_columns(firsts, back_second[name], flags, widths, shared)
        taken = paired(sent, "section", 1)
        both = jnp.where(
            plane == 0,
            jnp.concatenate([kept, taken], axis=0),
            jnp.concatenate([taken, kept], axis=0),
        )
        return both.astype(jnp.float32)

    _, branch_point, summed_point = points
    ff_total = w_gate.shape[2]
    grad_d = owned("d", (ff_width,), (False,), branch_point)
    grad_gu = owned("gu", (ff_width,) * 2, (False,) * 2, summed_point)
    grad_attn = owned("attn", (head_size,) * 4, (False, True, True, False), None)
    edges = [0]
    for array in (w_query, key_weight, value_weight, w_output):
        edges.append(edges[-1] + array.shape[2])
    attn_grads = [grad_attn[:, a:b] for a, b in zip(edges, edges[1:])]
    mlp_grads = (grad_gu[:, :ff_total], grad_gu[:, ff_total:], grad_d)

    rows_of = jnp.concatenate(
        [
            part.reshape(count, -1)
            for small in (small_first, small_second)
            for part in (
                unhalved(small[0]),
                unhalved(small[1]),
                jnp.tile(small[2], count),
                jnp.tile(small[3], count),
            )
        ],
        axis=1,
    )

    def row(to):
        return lax.dynamic_index_in_dim(rows_of, to, 0, keepdims=False)

    gain_sum = row(me)
    for s in range(1, count):
        gain_sum = gain_sum + paired(row(me ^ s), "dp", s)
    gain_sum = gain_sum + paired(gain_sum, "tensor", 1)
    gain_sum = gain_sum + paired(gain_sum, "section", 1)
    mine = jnp.where(plane == 0, gain_sum[:per_layer], gain_sum[per_layer:])
    grad_gain_attn = mine[:gain_width]
    grad_gain_mlp = mine[gain_width : 2 * gain_width]
    grad_gain_q = mine[2 * gain_width : 2 * gain_width + head_size]
    grad_gain_k = mine[2 * gain_width + head_size :]
    shards = (
        attn_grads[0], attn_grads[1], attn_grads[2], attn_grads[3],
        mlp_grads[0], mlp_grads[1], mlp_grads[2],
        grad_gain_attn, grad_gain_mlp, grad_gain_q, grad_gain_k,
    )
    return (section_out, input_grads) + tuple(part[None] for part in shards)


def fits(mesh):
    sizes = dict(mesh.shape)
    return sizes["dp"] == 8 and sizes["tensor"] == 2 and sizes["section"] == 2


def solution(mesh):
    return jax.shard_map(
        per_device if fits(mesh) else per_device_wide,
        mesh=mesh,
        in_specs=(
            P(None, "dp", None),
            P(None, "dp", None),
            P(None, "dp"),
            P("section", "dp", "tensor"),
            P("section", "dp", "tensor"),
            P("section", "dp", "tensor"),
            P("section", "dp", "tensor"),
            P("section", "dp", "tensor"),
            P("section", "dp", "tensor"),
            P("section", "dp", "tensor"),
            P("section", "dp"),
            P("section", "dp"),
            P("section", None),
            P("section", None),
        ),
        out_specs=(
            P("section", None, "dp", None),
            P("section", None, "dp", None),
            P("section", "dp", "tensor"),
            P("section", "dp", "tensor"),
            P("section", "dp", "tensor"),
            P("section", "dp", "tensor"),
            P("section", "dp", "tensor"),
            P("section", "dp", "tensor"),
            P("section", "dp", "tensor"),
            P("section", "dp"),
            P("section", "dp"),
            P("section", None),
            P("section", None),
        ),
        check_vma=False,
    )
```

```python
from functools import partial

import jax
import jax.numpy as jnp
from jax import lax
from jax.experimental import pallas as pl
from jax.experimental.pallas import tpu as pltpu
from jax.sharding import PartitionSpec as P


EPSILON = 1e-06
MASKED = -1e30


def shifted(x, axis, by):
    count = lax.axis_size(axis)
    pairs = [(i, i + by) for i in range(count) if 0 <= i + by < count]
    return lax.ppermute(x, axis, pairs)


def as_sent(x):

    def short(part):
        return part.astype(jnp.bfloat16) if part.dtype == jnp.float32 else part

    return jax.tree.map(short, x)


def dot_plain(left, right):
    return jnp.dot(left, right, preferred_element_type=jnp.float32)


def dot_last(left, right):
    return lax.dot_general(
        left, right, (((1,), (1,)), ((), ())), preferred_element_type=jnp.float32
    )


def dot_first(left, right):
    return lax.dot_general(
        left, right, (((0,), (0,)), ((), ())), preferred_element_type=jnp.float32
    )


def rms_scale(values, norm_gain):
    return (
        values * lax.rsqrt(jnp.mean(values * values, axis=-1, keepdims=True) + EPSILON) * norm_gain
    )


def swiglu(gate_raw, up_raw):
    return jax.nn.silu(gate_raw) * up_raw


def rope_tables(positions, head_size):
    half_size = head_size // 2
    freqs = jnp.power(
        jnp.float32(1000000.0), -jnp.arange(half_size, dtype=jnp.float32) * 2.0 / head_size
    )
    angles = positions.astype(jnp.float32)[:, None] * freqs[None, :]
    angles = jnp.concatenate([angles, angles], axis=-1)
    return (jnp.cos(angles), jnp.sin(angles))


def rotate_norm(raw_proj, norm_gain, cosine, sine_table):
    head_size = norm_gain.shape[0]
    token_count = raw_proj.shape[0]
    heads = raw_proj.reshape(token_count, -1, head_size)
    normed = rms_scale(heads, norm_gain)
    half_size = head_size // 2
    turned = jnp.concatenate([-normed[..., half_size:], normed[..., :half_size]], axis=-1)
    rotated = normed * cosine[:, None, :] + turned * sine_table[:, None, :]
    return rotated.reshape(token_count, -1)


def scores_for(queries, keys_all, allowed, head_size):
    row_count = queries.shape[0]
    kv_heads = keys_all.shape[1] // head_size
    group_size = queries.shape[1] // keys_all.shape[1]
    query_heads = queries.reshape(row_count, kv_heads, group_size, head_size)
    key_heads = keys_all.reshape(keys_all.shape[0], kv_heads, head_size)
    scores = jnp.einsum(
        "bngd,snd->ngbs", query_heads, key_heads, preferred_element_type=jnp.float32
    ) * head_size ** (-0.5)
    return (jnp.where(allowed[None, None], scores, MASKED), query_heads, key_heads)


def attend(queries, keys_all, values_all, allowed, head_size):
    scores, _, key_heads = scores_for(queries, keys_all, allowed, head_size)
    highest = jnp.max(scores, axis=-1, keepdims=True)
    weights = jnp.exp(scores - highest)
    total = jnp.sum(weights, axis=-1, keepdims=True)
    probs = (weights / total).astype(jnp.bfloat16)
    value_heads = values_all.reshape(key_heads.shape)
    mixed = jnp.einsum("ngbs,snd->bngd", probs, value_heads, preferred_element_type=jnp.float32)
    return (mixed.reshape(queries.shape[0], -1).astype(jnp.bfloat16), highest + jnp.log(total))


def attend_back(queries, keys_all, values_all, allowed, log_total, attn_grad, head_size):
    scores, query_heads, key_heads = scores_for(queries, keys_all, allowed, head_size)
    probs = jnp.exp(scores - log_total)
    value_heads = values_all.reshape(key_heads.shape)
    grad_heads = attn_grad.reshape(query_heads.shape)
    prob_grad = jnp.einsum(
        "bngd,snd->ngbs", grad_heads, value_heads, preferred_element_type=jnp.float32
    )
    delta = jnp.sum(probs * prob_grad, axis=-1, keepdims=True)
    score_grad = (probs * (prob_grad - delta)).astype(jnp.bfloat16)
    scale = head_size ** (-0.5)
    query_back = jnp.einsum(
        "ngbs,snd->bngd", score_grad, key_heads, preferred_element_type=jnp.float32
    )
    key_back = jnp.einsum(
        "ngbs,bngd->snd", score_grad, query_heads, preferred_element_type=jnp.float32
    )
    value_back = jnp.einsum(
        "ngbs,bngd->snd", probs.astype(jnp.bfloat16), grad_heads, preferred_element_type=jnp.float32
    )
    key_count = keys_all.shape[0]
    return (
        query_back.reshape(queries.shape[0], -1) * scale,
        key_back.reshape(key_count, -1) * scale,
        value_back.reshape(key_count, -1),
    )


def per_device_wide(
    inputs,
    cotangent,
    segments,
    w_query,
    key_weight,
    value_weight,
    w_output,
    w_gate,
    w_up,
    w_down,
    attn_gain,
    mlp_gain,
    query_gain,
    key_gain,
):
    section_first = lax.axis_index("section") == 0
    gathered = (
        lax.all_gather(w_query[0], "dp", axis=0, tiled=True),
        lax.all_gather(key_weight[0], "dp", axis=0, tiled=True),
        lax.all_gather(value_weight[0], "dp", axis=0, tiled=True),
        lax.all_gather(w_output[0], "dp", axis=0, tiled=True),
        lax.all_gather(w_gate[0], "dp", axis=0, tiled=True),
        lax.all_gather(w_up[0], "dp", axis=0, tiled=True),
        lax.all_gather(w_down[0], "dp", axis=0, tiled=True),
        lax.all_gather(attn_gain[0], "dp", axis=0, tiled=True),
        lax.all_gather(mlp_gain[0], "dp", axis=0, tiled=True),
    )
    w_q, w_k, w_v, w_o, w_g, w_u, w_d = gathered[:7]
    gain_attn = gathered[7].astype(jnp.float32)
    gain_mlp = gathered[8].astype(jnp.float32)
    gain_q = query_gain[0].astype(jnp.float32)
    gain_k = key_gain[0].astype(jnp.float32)
    head_size = gain_q.shape[0]
    doc_table = lax.all_gather(segments, "dp", axis=1, tiled=True)
    batch_count, row_count, model_width = inputs.shape
    token_count = doc_table.shape[1]
    positions = lax.axis_index("dp") * row_count + jnp.arange(row_count, dtype=jnp.int32)
    key_pos = jnp.arange(token_count, dtype=jnp.int32)
    cosine, sine_table = rope_tables(positions, head_size)
    rope_query = partial(rotate_norm, cosine=cosine, sine_table=sine_table)
    arrived = jnp.zeros((row_count, model_width), jnp.bfloat16)
    stored_steps, outgoing_steps = ([], [])
    for step_index in range(batch_count + 1):
        early = min(step_index, batch_count - 1)
        late = max(step_index - 1, 0)
        layer_in = jnp.where(
            section_first, inputs[early].astype(jnp.float32), arrived.astype(jnp.float32)
        )
        own_segs = jnp.where(section_first, segments[early], segments[late])
        doc_row = jnp.where(section_first, doc_table[early], doc_table[late])
        forward_normed = rms_scale(layer_in, gain_attn).astype(jnp.bfloat16)
        forward_queries = dot_plain(forward_normed, w_q)
        forward_key_raw = dot_plain(forward_normed, w_k)
        forward_value_raw = dot_plain(forward_normed, w_v).astype(jnp.bfloat16)
        forward_query_rot = rope_query(forward_queries, gain_q).astype(jnp.bfloat16)
        forward_key_rot = rope_query(forward_key_raw, gain_k).astype(jnp.bfloat16)
        forward_keys_all = lax.all_gather(forward_key_rot, "dp", axis=0, tiled=True)
        forward_values_all = lax.all_gather(forward_value_raw, "dp", axis=0, tiled=True)
        forward_allowed = (key_pos[None, :] <= positions[:, None]) & (
            own_segs[:, None] == doc_row[None, :]
        )
        forward_attn, forward_log_total = attend(
            forward_query_rot, forward_keys_all, forward_values_all, forward_allowed, head_size
        )
        forward_mixed = layer_in + lax.psum(dot_last(forward_attn, w_o), "tensor")
        forward_normed_mlp = rms_scale(forward_mixed, gain_mlp).astype(jnp.bfloat16)
        forward_gate_raw = dot_plain(forward_normed_mlp, w_g)
        forward_up_raw = dot_plain(forward_normed_mlp, w_u)
        forward_activated = swiglu(forward_gate_raw, forward_up_raw).astype(jnp.bfloat16)
        layer_out = forward_mixed + lax.psum(dot_last(forward_activated, w_d), "tensor")
        forward_stored = (
            layer_in,
            forward_normed,
            forward_queries,
            forward_key_raw,
            forward_query_rot,
            forward_key_rot,
            forward_value_raw,
            forward_attn,
            forward_log_total,
            forward_mixed,
            forward_normed_mlp,
            forward_gate_raw,
            forward_up_raw,
            forward_activated,
            forward_allowed,
        )
        layer_out, stored = (layer_out, forward_stored)
        outgoing = layer_out.astype(jnp.bfloat16)
        stored_steps.append(stored)
        outgoing_steps.append(outgoing)
        if step_index < batch_count:
            arrived = shifted(outgoing, "section", 1)
    section_out = jnp.stack(
        [
            jnp.where(section_first, outgoing_steps[batch_index], outgoing_steps[batch_index + 1])
            for batch_index in range(batch_count)
        ]
    )
    back_arrived = jnp.zeros((row_count, model_width), jnp.bfloat16)
    grad_steps = []
    totals = None
    norm_totals = None
    for step_index in range(batch_count + 1):
        early_batch = min(batch_count - step_index, batch_count - 1)
        late_batch = max(batch_count - 1 - step_index, 0)
        stored = jax.tree.map(
            lambda a, b: jnp.where(section_first, a, b),
            stored_steps[early_batch],
            stored_steps[late_batch + 1],
        )
        valid = jnp.where(
            section_first,
            jnp.float32(1.0 if step_index >= 1 else 0.0),
            jnp.float32(1.0 if step_index < batch_count else 0.0),
        )
        grad_out = (
            jnp.where(
                section_first,
                back_arrived.astype(jnp.float32),
                cotangent[late_batch].astype(jnp.float32),
            )
            * valid
        )
        (
            backward_layer_in,
            normed,
            queries,
            key_raw,
            query_rot,
            key_rot,
            value_raw,
            attn,
            log_total,
            mixed,
            normed_mlp,
            gate_raw,
            up_raw,
            activated,
            allowed,
        ) = stored[:15]
        keys_all = lax.all_gather(key_rot, "dp", axis=0, tiled=True)
        values_all = lax.all_gather(value_raw, "dp", axis=0, tiled=True)
        mlp_grad = grad_out.astype(jnp.bfloat16)
        act_grad = dot_plain(mlp_grad, w_d)
        grad_wd = dot_first(mlp_grad, activated)
        unused, swiglu_back = jax.vjp(swiglu, gate_raw, up_raw)
        gate_grad, up_grad = swiglu_back(act_grad)
        gate_grad = gate_grad.astype(jnp.bfloat16)
        up_grad = up_grad.astype(jnp.bfloat16)
        grad_wg = dot_first(normed_mlp, gate_grad)
        grad_wu = dot_first(normed_mlp, up_grad)
        normed_mlp_grad = lax.psum(
            (dot_last(gate_grad, w_g) + dot_last(up_grad, w_u)).astype(jnp.bfloat16), "tensor"
        ).astype(jnp.float32)
        unused, mlp_norm_back = jax.vjp(rms_scale, mixed, gain_mlp)
        mixed_part, grad_gain_mlp = mlp_norm_back(normed_mlp_grad)
        mixed_grad = grad_out + mixed_part
        branch_low = mixed_grad.astype(jnp.bfloat16)
        attn_grad = dot_plain(branch_low, w_o).astype(jnp.bfloat16)
        grad_wo = dot_first(branch_low, attn)
        query_back, key_back, value_back = attend_back(
            query_rot, keys_all, values_all, allowed, log_total, attn_grad, head_size
        )
        backward_key_total = lax.psum_scatter(
            key_back.astype(jnp.bfloat16), "dp", scatter_dimension=0, tiled=True
        ).astype(jnp.float32)
        value_total = lax.psum_scatter(
            value_back.astype(jnp.bfloat16), "dp", scatter_dimension=0, tiled=True
        )
        unused, key_rope_back = jax.vjp(rope_query, key_raw, gain_k)
        key_gradient, grad_gain_k = key_rope_back(backward_key_total)
        key_gradient = key_gradient.astype(jnp.bfloat16)
        unused, query_rope_back = jax.vjp(rope_query, queries, gain_q)
        query_grad, grad_gain_q = query_rope_back(query_back)
        query_grad = query_grad.astype(jnp.bfloat16)
        grad_wq = dot_first(normed, query_grad)
        grad_wk = dot_first(normed, key_gradient)
        grad_wv = dot_first(normed, value_total)
        normed_grad = lax.psum(
            (
                dot_last(query_grad, w_q) + dot_last(key_gradient, w_k) + dot_last(value_total, w_v)
            ).astype(jnp.bfloat16),
            "tensor",
        ).astype(jnp.float32)
        unused, attn_norm_back = jax.vjp(rms_scale, backward_layer_in, gain_attn)
        input_part, grad_gain_attn = attn_norm_back(normed_grad)
        weight_part = (
            grad_wq,
            grad_wk,
            grad_wv,
            grad_wo,
            grad_wg,
            grad_wu,
            grad_wd,
            grad_gain_attn,
            grad_gain_mlp,
        )
        input_grad, weight_part, norm_part = (
            mixed_grad + input_part,
            weight_part,
            (grad_gain_q, grad_gain_k),
        )
        outgoing = input_grad.astype(jnp.bfloat16)
        grad_steps.append(outgoing)
        if step_index < batch_count:
            back_arrived = shifted(outgoing, "section", -1)
        totals = (
            weight_part if totals is None else tuple((a + b for a, b in zip(totals, weight_part)))
        )
        norm_totals = (
            norm_part
            if norm_totals is None
            else tuple((a + b for a, b in zip(norm_totals, norm_part)))
        )
    shards = jax.tree.map(
        lambda part: part.astype(jnp.float32),
        lax.psum_scatter(as_sent(totals), "dp", scatter_dimension=0, tiled=True),
    )
    query_total, key_total = lax.psum(norm_totals, ("tensor", "dp"))
    input_grads = jnp.stack(
        [
            jnp.where(
                section_first,
                grad_steps[batch_count - batch_index],
                grad_steps[batch_count - 1 - batch_index],
            )
            for batch_index in range(batch_count)
        ]
    )
    return (
        (section_out[None], input_grads[None])
        + tuple((member[None] for member in shards))
        + (query_total[None], key_total[None])
    )


def paired(x, axis, flip):
    count = lax.axis_size(axis)
    return lax.ppermute(x, axis, [(i, i ^ flip) for i in range(count)])


def ring_order(count):
    return list(range(0, count, 2)) + list(range(count - 1, 0, -2))


def ring(x, by):
    order = ring_order(lax.axis_size("dp"))
    count = len(order)
    pairs = []
    for core, step in ((0, by), (1, -by)):
        for i in range(count):
            pairs.append((core * count + order[i], core * count + order[(i + step) % count]))
    return lax.ppermute(x, ("tensor", "dp"), pairs)


def received_order(count):
    half = count // 2
    return [(0, False)] + [(s, lag) for s in range(1, half) for lag in (False, True)] + [(half, False)]


def near_chunks(count):
    return 2 * (count // 2 - 2) + 1


def gate(value, token):
    return lax.optimization_barrier((value, token))[0]


def whole_vmem(count):
    return [pl.BlockSpec(memory_space=pltpu.VMEM)] * count


def joined(pieces):
    rows = sum(piece.shape[0] for piece in pieces)
    width = pieces[0].shape[1]

    def kernel(*refs):
        at = 0
        for ref in refs[:-1]:
            refs[-1][at : at + ref.shape[0], :] = ref[...]
            at += ref.shape[0]

    return pl.pallas_call(
        kernel,
        out_shape=jax.ShapeDtypeStruct((rows, width), pieces[0].dtype),
        in_specs=whole_vmem(len(pieces)),
        out_specs=pl.BlockSpec(memory_space=pltpu.VMEM),
        cost_estimate=pl.CostEstimate(flops=0, bytes_accessed=4 * rows * width, transcendentals=0),
    )(*pieces)


def gather_ring(chunk):
    count = lax.axis_size("dp")
    half = count // 2
    lead, lag = chunk, paired(chunk, "tensor", 1)
    chunks, token = [chunk], None
    for step in range(1, half + 1):
        lead = ring(lead, 1)
        chunks.append(lead)
        if step < half:
            lag = ring(lag, 1)
            chunks.append(lag)
        if step == half - 1:
            token = lead
    cut = near_chunks(count)
    near, far = joined(gate(chunks[:cut], token)), joined(chunks[cut:])
    return [near, far, paired(near, "tensor", 1), paired(far, "tensor", 1)], token


def multiplied(parts, weight):
    return jnp.concatenate(parts, axis=0), by_parts(parts, weight)


def by_parts(parts, weight):
    return jnp.concatenate([dot_plain(part, weight) for part in parts], axis=0)


def product_scattered(act, weight):
    count = lax.axis_size("dp")
    half = count // 2
    side = act.shape[0] // 2
    rows = side // count
    near = near_chunks(count) * rows
    far_sum = dot_last(act[side + near :], weight).astype(jnp.bfloat16)
    near_sum = dot_last(act[side : side + near], weight).astype(jnp.bfloat16)
    own = dot_last(act[:side], weight)
    far_sum = paired(far_sum, "tensor", 1)
    near_sum = paired(near_sum, "tensor", 1)
    spots = {key: i * rows for i, key in enumerate(received_order(count))}

    def part(hops, lag):
        at = spots[hops, lag]
        extra = far_sum[at - near :][:rows] if at >= near else near_sum[at : at + rows]
        return own[at : at + rows] + extra.astype(jnp.float32)

    def hop(value, hops, lag):
        total = part(hops, lag)
        if value is not None:
            total = total + value.astype(jnp.float32)
        return ring(total.astype(jnp.bfloat16), -1)

    lead = lag = token = None
    for hops in range(half, 0, -1):
        lead = hop(lead, hops, False)
        if hops < half:
            lag = hop(lag, hops, True)
        if hops == half - 1:
            token = lead
    across = paired(lag, "tensor", 1)
    return part(0, False) + lead.astype(jnp.float32) + across.astype(jnp.float32), token


def place_rows(blocks, flags, widths):
    count = len(blocks)
    rows, total = blocks[0].shape
    part = rows // 2

    def kernel(flags_ref, *refs):
        for s in range(count):
            left = 0
            for out, width in zip(refs[count:], widths):
                for half in range(2):
                    at = pl.multiple_of((flags_ref[0] ^ s) * part + half * count * part, part)
                    top = half * part
                    out[pl.ds(at, part), :] = refs[s][top : top + part, left : left + width]
                left += width

    size = 2 * count * rows * total
    return pl.pallas_call(
        kernel,
        out_shape=[jax.ShapeDtypeStruct((count * rows, w), blocks[0].dtype) for w in widths],
        in_specs=[pl.BlockSpec(memory_space=pltpu.SMEM)] + whole_vmem(count),
        out_specs=whole_vmem(len(widths)),
        cost_estimate=pl.CostEstimate(flops=0, bytes_accessed=2 * size, transcendentals=0),
    )(flags, *blocks)


def place_columns(first, second, flags, widths, shared, skip):
    count = len(first)
    rows = first[0].shape[0]
    columns = [w * count // (2 if wide else 1) for w, wide in zip(widths, shared)]
    total = sum(columns)

    def kernel(flags_ref, *refs):
        kept, sent = refs[2 * count :]

        def fill(out, blocks, left):
            base = 0
            for width, wide, room in zip(widths, shared, columns):
                for s in range(0, count, 2 if wide else 1):
                    index = flags_ref[0] ^ s
                    at = base + (index // 2 if wide else index) * width
                    value = blocks[s][:, left : left + width]
                    if wide:
                        value = value.astype(jnp.float32) + blocks[s + 1][
                            :, left : left + width
                        ].astype(jnp.float32)
                    out[:, pl.ds(pl.multiple_of(at, 128), width)] = value.astype(out.dtype)
                left += width
                base += room

        @pl.when(flags_ref[1] == 0)
        def _():
            fill(kept, refs[:count], 0)
            fill(sent, refs[count : 2 * count], skip)

        @pl.when(flags_ref[1] != 0)
        def _():
            fill(sent, refs[:count], 0)
            fill(kept, refs[count : 2 * count], skip)

    return pl.pallas_call(
        kernel,
        out_shape=[jax.ShapeDtypeStruct((rows, total), first[0].dtype)] * 2,
        in_specs=[pl.BlockSpec(memory_space=pltpu.SMEM)] + whole_vmem(2 * count),
        out_specs=whole_vmem(2),
        cost_estimate=pl.CostEstimate(
            flops=0, bytes_accessed=4 * count * rows * sum(widths) * 2, transcendentals=0
        ),
    )(flags, *first, *second)


def head_attend(query, key, value, allowed):
    scores = dot_last(query, key) * query.shape[1] ** (-0.5)
    scores = jnp.where(allowed, scores, MASKED)
    highest = jnp.max(scores, axis=-1, keepdims=True)
    weights = jnp.exp(scores - highest)
    total = jnp.sum(weights, axis=-1, keepdims=True)
    probs = (weights / total).astype(jnp.bfloat16)
    return dot_plain(probs, value).astype(jnp.bfloat16), highest + jnp.log(total)


def head_attend_back(query, key, value, allowed, log_total, grad):
    scale = query.shape[1] ** (-0.5)
    scores = jnp.where(allowed, dot_last(query, key) * scale, MASKED)
    probs = jnp.exp(scores - log_total)
    prob_grad = dot_last(grad, value)
    delta = jnp.sum(probs * prob_grad, axis=-1, keepdims=True)
    score_grad = (probs * (prob_grad - delta)).astype(jnp.bfloat16)
    return (
        dot_plain(score_grad, key) * scale,
        dot_first(score_grad, query) * scale,
        dot_first(probs.astype(jnp.bfloat16), grad),
    )


def per_device(
    inputs,
    cotangent,
    segments,
    w_query,
    key_weight,
    value_weight,
    w_output,
    w_gate,
    w_up,
    w_down,
    attn_gain,
    mlp_gain,
    query_gain,
    key_gain,
):
    count = lax.axis_size("dp")
    plane = lax.axis_index("section")
    me = lax.axis_index("dp")
    core = lax.axis_index("tensor")
    flags = jnp.stack([me, plane]).astype(jnp.int32)
    model_width = inputs.shape[2]
    rows = inputs.shape[1] // 2
    head_size = query_gain.shape[1]
    ff_width = w_gate.shape[2] // count
    group_size = w_query.shape[2] // key_weight.shape[2]
    gain_width = attn_gain.shape[1]

    def by_layer(own):
        theirs = paired(own, "section", 1)
        first = plane == 0
        return [jnp.where(first, own, theirs), jnp.where(first, theirs, own)]

    part = gain_width // 2

    def halved(array):
        wide = array.reshape(-1, count, 2, part)
        return jnp.swapaxes(wide, 1, 2).reshape(array.shape)

    def unhalved(array):
        wide = array.reshape(-1, 2, count, part)
        return jnp.swapaxes(wide, 1, 2).reshape(array.shape)

    def own_rows(array):
        own = lax.dynamic_slice(array, (plane, core * rows, 0), (1, rows, model_width))[0]
        return halved(own)

    gains = jnp.concatenate([attn_gain[0], mlp_gain[0], query_gain[0], key_gain[0]])
    gains = jnp.concatenate(by_layer(gains.astype(jnp.float32)))
    docs = lax.dynamic_index_in_dim(segments, plane, 0, keepdims=False).astype(jnp.float32)
    note = jnp.concatenate([gains, docs])
    notes = jnp.stack([note] + [paired(note, "dp", s) for s in range(1, count)])
    notes = jnp.concatenate(
        [lax.dynamic_slice_in_dim(notes, me ^ j, 1, axis=0) for j in range(count)], axis=0
    )
    per_layer = gains.shape[0] // 2
    layer_gains = []
    for layer in range(2):
        at = layer * per_layer
        layer_gains.append(
            (
                halved(notes[:, at : at + gain_width].reshape(-1)),
                halved(notes[:, at + gain_width : at + 2 * gain_width].reshape(-1)),
                gains[at + 2 * gain_width : at + 2 * gain_width + head_size],
                gains[at + 2 * gain_width + head_size : at + per_layer],
            )
        )
    doc_table = notes[:, 2 * per_layer :].reshape(count, 2, rows)

    place = jnp.where(me % 2 == 0, me // 2, count - 1 - me // 2)
    docs_parts, pos_parts = ([], []), ([], [])
    away = 2 * core - 1
    for at in range(2):
        for hops, lag in received_order(count):
            side = core if lag == bool(at) else 1 - core
            spot = (place + (away if at == 0 else -away) * hops + count) % count
            owner = jnp.where(spot < count // 2, 2 * spot, 2 * (count - 1 - spot) + 1)
            block = lax.dynamic_index_in_dim(doc_table, owner, 0, keepdims=False)
            docs_parts[at].append(lax.dynamic_index_in_dim(block, side, 0, keepdims=False))
            start = owner * 2 * rows + side * rows
            pos_parts[at].append(start + jnp.arange(rows, dtype=jnp.int32))
    docs_all = jnp.concatenate(docs_parts[0] + docs_parts[1])
    positions = jnp.concatenate(pos_parts[0] + pos_parts[1])
    allowed = (positions[None, :] <= positions[:, None]) & (docs_all[:, None] == docs_all[None, :])
    cosine, sine_table = rope_tables(positions, head_size)
    rope = partial(rotate_norm, cosine=cosine, sine_table=sine_table)

    def cut(pieces):
        def block(to):
            return jnp.concatenate(
                [
                    lax.dynamic_slice_in_dim(array, (to // share) * width, width, axis=1)
                    for array, width, share in pieces
                ],
                axis=1,
            )

        return [block(me ^ s) for s in range(count)]

    def turn(blocks):
        return [blocks[0]] + [paired(blocks[s], "dp", s) for s in range(1, count)]

    def both_layers(blocks, widths):
        sets = []
        for placed in place_rows(blocks, flags, widths):
            facing = paired(placed, "section", 1)
            sets.append([jnp.where(plane == layer, placed, facing) for layer in range(2)])
        return sets

    pieces_of = {
        "qk": ((w_query[0], head_size, 1), (key_weight[0], head_size, group_size)),
        "vo": ((value_weight[0], head_size, group_size), (w_output[0], head_size, 1)),
        "g": ((w_gate[0], ff_width, 1),),
        "u": ((w_up[0], ff_width, 1),),
        "d": ((w_down[0], ff_width, 1),),
    }
    sliced = {name: cut(pieces) for name, pieces in pieces_of.items()}
    turned, weights = {}, {}

    def attention(raw, value, layer):
        _, _, gain_q, gain_k = layer_gains[layer]
        queries, key_raw = raw[:, :head_size], raw[:, head_size:]
        value = value.astype(jnp.bfloat16)
        query_rot = rope(queries, gain_q).astype(jnp.bfloat16)
        key_rot = rope(key_raw, gain_k).astype(jnp.bfloat16)
        attn, log_total = head_attend(query_rot, key_rot, value, allowed)
        return attn, (queries, key_raw, value, query_rot, key_rot, log_total)

    def forward(layer_in, layer):
        gain_attn, gain_mlp, _, _ = layer_gains[layer]
        if layer == 0:
            turned["qk"] = turn(sliced["qk"])
            parts, token = gather_ring(layer_in.astype(jnp.bfloat16))
            raw_in = joined(parts).astype(jnp.float32)
            weights["qk"] = both_layers(turned["qk"], (2 * head_size,))[0]
            turned["vo"] = turn(gate(sliced["vo"], turned["qk"]))
            weights["v"], weights["o"] = both_layers(turned["vo"], (head_size, head_size))
            turned["g"] = turn(gate(sliced["g"], turned["vo"]))
            normed = rms_scale(raw_in, gain_attn).astype(jnp.bfloat16)
            raw = dot_plain(normed, weights["qk"][0])
            value = dot_plain(normed, weights["v"][0])
        else:
            chunk = rms_scale(layer_in, gain_attn).astype(jnp.bfloat16)
            parts, token = gather_ring(chunk)
            normed, raw = multiplied(parts, weights["qk"][layer])
            value = by_parts(parts, weights["v"][layer])
        attn, kept = attention(raw, value, layer)
        if layer == 0:
            turned["u"] = turn(gate(sliced["u"], turned["g"]))
            weights["g"] = both_layers(gate(turned["g"], raw), (ff_width,))[0]
            extra = None
        else:
            cotangent_rows = own_rows(cotangent)
            extra, token = gather_ring(gate(cotangent_rows, raw))
            attn = gate(attn, extra[1])
        summed, token = product_scattered(attn, weights["o"][layer])
        mixed = layer_in + summed
        if layer == 0:
            weights["u"] = both_layers(gate(turned["u"], token), (ff_width,))[0]
            turned["d"] = turn(gate(sliced["d"], turned["u"]))
            weights["gu"] = [
                jnp.concatenate([weights["g"][i], weights["u"][i]], axis=1) for i in range(2)
            ]
        parts, token = gather_ring(rms_scale(mixed, gain_mlp).astype(jnp.bfloat16))
        if layer == 0:
            weights["d"] = both_layers(gate(turned["d"], parts[1]), (ff_width,))[0]
        normed_mlp, raw_mlp = multiplied(parts, weights["gu"][layer])
        gate_raw, up_raw = raw_mlp[:, :ff_width], raw_mlp[:, ff_width:]
        activated = swiglu(gate_raw, up_raw).astype(jnp.bfloat16)
        stored = (layer_in, normed, kept, attn, mixed, normed_mlp, gate_raw, up_raw, activated)

        def finish(after):
            held = activated if after is None else gate(activated, after)
            summed, _ = product_scattered(held, weights["d"][layer])
            return ((mixed + summed).astype(jnp.bfloat16),)

        return finish, stored, extra

    def halves(grad):
        span = grad.shape[0] // 2
        sent = lax.dynamic_slice_in_dim(grad, (1 - plane) * span, span, axis=0)
        kept = lax.dynamic_slice_in_dim(grad, plane * span, span, axis=0)
        return kept, paired(sent.astype(jnp.bfloat16), "section", 1)

    last_turn = []

    def returned(pair, token):
        kept, taken = pair
        if token is not None:
            taken = gate(taken, token)
        total = (kept + taken.astype(jnp.float32)).astype(jnp.bfloat16)
        blocks = [lax.dynamic_slice_in_dim(total, (me ^ s) * part, part, axis=0) for s in range(count)]
        if last_turn:
            blocks = gate(blocks, last_turn[-1])
        last_turn.append(turn(blocks))
        return last_turn[-1]

    def backward(gathered, grad_out, stored, layer, back, late):
        layer_in, normed, kept, attn, mixed, normed_mlp, gate_raw, up_raw, activated = stored
        queries, key_raw, value, query_rot, key_rot, log_total = kept
        gain_attn, gain_mlp, gain_q, gain_k = layer_gains[layer]
        out_low, act_grad = multiplied(gathered, weights["d"][layer])
        unused, swiglu_back = jax.vjp(swiglu, gate_raw, up_raw)
        gate_grad, up_grad = swiglu_back(act_grad)
        raw_grad = jnp.concatenate([gate_grad, up_grad], axis=1).astype(jnp.bfloat16)
        summed, token = product_scattered(raw_grad, weights["gu"][layer])
        sums = {}
        sums["d"] = halves(dot_first(out_low, activated))
        sums["gu"] = halves(dot_first(normed_mlp, raw_grad))
        unused, mlp_norm_back = jax.vjp(rms_scale, mixed, gain_mlp)
        mixed_part, grad_gain_mlp = mlp_norm_back(summed)
        mixed_grad = grad_out + mixed_part
        back["d"] = returned(sums["d"], mixed_grad)
        parts, token = gather_ring(mixed_grad.astype(jnp.bfloat16))
        branch_low, attn_grad = multiplied(parts, weights["o"][layer])
        if late is not None:
            late = partial(late, attn_grad)
        back["gu"] = returned(sums["gu"], parts[1])
        query_back, key_back, value_back = head_attend_back(
            query_rot, key_rot, value, allowed, log_total, attn_grad.astype(jnp.bfloat16)
        )
        unused, key_rope_back = jax.vjp(rope, key_raw, gain_k)
        key_grad, grad_gain_k = key_rope_back(key_back)
        unused, query_rope_back = jax.vjp(rope, queries, gain_q)
        query_grad, grad_gain_q = query_rope_back(query_back)
        qkv_grad = jnp.concatenate([query_grad, key_grad, value_back], axis=1).astype(jnp.bfloat16)
        if late is not None:
            late = late()
            qkv_grad = gate(qkv_grad, late[0])
        summed, token = product_scattered(qkv_grad, weights["qkv"][layer])
        two = 2 * head_size
        grad_vo = [dot_first(normed, qkv_grad[:, two:]), dot_first(branch_low, attn)]
        grad_vo = jnp.concatenate(grad_vo, axis=1)
        grad_qk = dot_first(normed, qkv_grad[:, :two])
        if layer == 0:
            sums = (halves(grad_qk), halves(grad_vo))
        else:
            sums = halves(jnp.concatenate([grad_qk, grad_vo], axis=1))
        unused, attn_norm_back = jax.vjp(rms_scale, layer_in, gain_attn)
        input_part, grad_gain_attn = attn_norm_back(summed)
        small = (grad_gain_attn, grad_gain_mlp, grad_gain_q, grad_gain_k)
        points = (branch_low, token)
        return mixed_grad + input_part, sums, small, points, late

    finish, stored_first, _ = forward(own_rows(inputs).astype(jnp.float32), 0)
    out_first = finish(None)[0]
    weights["qkv"] = [
        jnp.concatenate([weights["qk"][i], weights["v"][i]], axis=1) for i in range(2)
    ]
    finish, stored_second, gathered = forward(out_first.astype(jnp.float32), 1)
    back_second, back_first = {}, {}
    grad_second, waiting, small_second, points, last = backward(
        gathered, own_rows(cotangent).astype(jnp.float32), stored_second, 1, back_second, finish
    )
    out_second = last[0]
    grad_second = grad_second.astype(jnp.bfloat16)
    gathered, _ = gather_ring(grad_second)
    back_second["attn"] = returned(waiting, gathered[1])
    grad_first, waiting, small_first, points, last = backward(
        gathered, grad_second.astype(jnp.float32), stored_first, 0, back_first, None
    )
    grad_first = grad_first.astype(jnp.bfloat16)
    back_first["qk"] = returned(waiting[0], None)
    back_first["vo"] = returned(waiting[1], None)

    def by_section(first, second):
        first, second = unhalved(first), unhalved(second)
        kept = jnp.where(plane == 0, first, second)
        taken = paired(jnp.where(plane == 0, second, first), "section", 1)
        both = jnp.where(plane == 0, jnp.stack([kept, taken]), jnp.stack([taken, kept]))
        facing = paired(both, "tensor", 1)
        return jnp.where(
            core == 0,
            jnp.concatenate([both, facing], axis=1),
            jnp.concatenate([facing, both], axis=1),
        )[None]

    section_out = by_section(out_first, out_second)
    input_grads = by_section(grad_first, grad_second)

    def owned(name, widths, shared, token, other=None, skip=0):
        firsts = back_first[name] if token is None else gate(back_first[name], token)
        seconds = back_second[other or name]
        kept, sent = place_columns(firsts, seconds, flags, widths, shared, skip)
        taken = paired(sent, "section", 1)
        both = jnp.where(
            plane == 0,
            jnp.concatenate([kept, taken], axis=0),
            jnp.concatenate([taken, kept], axis=0),
        )
        return both.astype(jnp.float32)

    branch_point, summed_point = points
    ff_total = w_gate.shape[2]
    grad_d = owned("d", (ff_width,), (False,), branch_point)
    grad_gu = owned("gu", (ff_width,) * 2, (False,) * 2, summed_point)
    grad_qk = owned("qk", (head_size,) * 2, (False, True), None, "attn")
    grad_vo = owned("vo", (head_size,) * 2, (True, False), None, "attn", 2 * head_size)
    q_total, v_total = w_query.shape[2], value_weight.shape[2]
    attn_grads = (
        grad_qk[:, :q_total], grad_qk[:, q_total:], grad_vo[:, :v_total], grad_vo[:, v_total:],
    )
    mlp_grads = (grad_gu[:, :ff_total], grad_gu[:, ff_total:], grad_d)

    rows_of = jnp.concatenate(
        [
            part.reshape(count, -1)
            for small in (small_first, small_second)
            for part in (
                unhalved(small[0]),
                unhalved(small[1]),
                jnp.tile(small[2], count),
                jnp.tile(small[3], count),
            )
        ],
        axis=1,
    )

    gain_sum, step = rows_of, count // 2
    while step:
        bit = (me // step) % 2
        gain_sum = gain_sum.reshape(2, step, -1)
        kept = lax.dynamic_index_in_dim(gain_sum, bit, 0, keepdims=False)
        sent = lax.dynamic_index_in_dim(gain_sum, 1 - bit, 0, keepdims=False)
        gain_sum = kept + paired(sent, "dp", step)
        step //= 2
    gain_sum = gain_sum.reshape(-1)
    gain_sum = gain_sum + paired(gain_sum, "tensor", 1)
    gain_sum = gain_sum + paired(gain_sum, "section", 1)
    mine = jnp.where(plane == 0, gain_sum[:per_layer], gain_sum[per_layer:])
    grad_gain_attn = mine[:gain_width]
    grad_gain_mlp = mine[gain_width : 2 * gain_width]
    grad_gain_q = mine[2 * gain_width : 2 * gain_width + head_size]
    grad_gain_k = mine[2 * gain_width + head_size :]
    shards = (
        attn_grads[0], attn_grads[1], attn_grads[2], attn_grads[3],
        mlp_grads[0], mlp_grads[1], mlp_grads[2],
        grad_gain_attn, grad_gain_mlp, grad_gain_q, grad_gain_k,
    )
    return (section_out, input_grads) + tuple(part[None] for part in shards)


def fits(mesh):
    sizes = dict(mesh.shape)
    return sizes["dp"] == 8 and sizes["tensor"] == 2 and sizes["section"] == 2


def solution(mesh):
    return jax.shard_map(
        per_device if fits(mesh) else per_device_wide,
        mesh=mesh,
        in_specs=(
            P(None, "dp", None),
            P(None, "dp", None),
            P(None, "dp"),
            P("section", "dp", "tensor"),
            P("section", "dp", "tensor"),
            P("section", "dp", "tensor"),
            P("section", "dp", "tensor"),
            P("section", "dp", "tensor"),
            P("section", "dp", "tensor"),
            P("section", "dp", "tensor"),
            P("section", "dp"),
            P("section", "dp"),
            P("section", None),
            P("section", None),
        ),
        out_specs=(
            P("section", None, "dp", None),
            P("section", None, "dp", None),
            P("section", "dp", "tensor"),
            P("section", "dp", "tensor"),
            P("section", "dp", "tensor"),
            P("section", "dp", "tensor"),
            P("section", "dp", "tensor"),
            P("section", "dp", "tensor"),
            P("section", "dp", "tensor"),
            P("section", "dp"),
            P("section", "dp"),
            P("section", None),
            P("section", None),
        ),
        check_vma=False,
    )
```

```python
from functools import partial

import jax
import jax.numpy as jnp
from jax import lax
from jax.experimental import pallas as pl
from jax.experimental.pallas import tpu as pltpu
from jax.sharding import PartitionSpec as P


SECTION, TENSOR, DP = "section", "tensor", "dp"
EPSILON = 1e-06
MASKED = -1e30


def shifted(x, axis, by):
    count = lax.axis_size(axis)
    pairs = [(i, i + by) for i in range(count) if 0 <= i + by < count]
    return lax.ppermute(x, axis, pairs)


def as_sent(x):

    def short(part):
        return part.astype(jnp.bfloat16) if part.dtype == jnp.float32 else part

    return jax.tree.map(short, x)


def dot_plain(left, right):
    return jnp.dot(left, right, preferred_element_type=jnp.float32)


def dot_last(left, right):
    return lax.dot_general(
        left, right, (((1,), (1,)), ((), ())), preferred_element_type=jnp.float32
    )


def dot_first(left, right):
    return lax.dot_general(
        left, right, (((0,), (0,)), ((), ())), preferred_element_type=jnp.float32
    )


def rms_scale(values, norm_gain):
    return (
        values * lax.rsqrt(jnp.mean(values * values, axis=-1, keepdims=True) + EPSILON) * norm_gain
    )


def swiglu(gate_raw, up_raw):
    return jax.nn.silu(gate_raw) * up_raw


def rope_tables(positions, head_size):
    half_size = head_size // 2
    freqs = jnp.power(
        jnp.float32(1000000.0), -jnp.arange(half_size, dtype=jnp.float32) * 2.0 / head_size
    )
    angles = positions.astype(jnp.float32)[:, None] * freqs[None, :]
    angles = jnp.concatenate([angles, angles], axis=-1)
    return (jnp.cos(angles), jnp.sin(angles))


def rotate_norm(raw_proj, norm_gain, cosine, sine_table):
    head_size = norm_gain.shape[0]
    token_count = raw_proj.shape[0]
    heads = raw_proj.reshape(token_count, -1, head_size)
    normed = rms_scale(heads, norm_gain)
    half_size = head_size // 2
    turned = jnp.concatenate([-normed[..., half_size:], normed[..., :half_size]], axis=-1)
    rotated = normed * cosine[:, None, :] + turned * sine_table[:, None, :]
    return rotated.reshape(token_count, -1)


def scores_for(queries, keys_all, allowed, head_size):
    row_count = queries.shape[0]
    kv_heads = keys_all.shape[1] // head_size
    group_size = queries.shape[1] // keys_all.shape[1]
    query_heads = queries.reshape(row_count, kv_heads, group_size, head_size)
    key_heads = keys_all.reshape(keys_all.shape[0], kv_heads, head_size)
    scores = jnp.einsum(
        "bngd,snd->ngbs", query_heads, key_heads, preferred_element_type=jnp.float32
    ) * head_size ** (-0.5)
    return (jnp.where(allowed[None, None], scores, MASKED), query_heads, key_heads)


def attend(queries, keys_all, values_all, allowed, head_size):
    scores, _, key_heads = scores_for(queries, keys_all, allowed, head_size)
    highest = jnp.max(scores, axis=-1, keepdims=True)
    weights = jnp.exp(scores - highest)
    total = jnp.sum(weights, axis=-1, keepdims=True)
    probs = (weights / total).astype(jnp.bfloat16)
    value_heads = values_all.reshape(key_heads.shape)
    mixed = jnp.einsum("ngbs,snd->bngd", probs, value_heads, preferred_element_type=jnp.float32)
    return (mixed.reshape(queries.shape[0], -1).astype(jnp.bfloat16), highest + jnp.log(total))


def attend_back(queries, keys_all, values_all, allowed, log_total, attn_grad, head_size):
    scores, query_heads, key_heads = scores_for(queries, keys_all, allowed, head_size)
    probs = jnp.exp(scores - log_total)
    value_heads = values_all.reshape(key_heads.shape)
    grad_heads = attn_grad.reshape(query_heads.shape)
    prob_grad = jnp.einsum(
        "bngd,snd->ngbs", grad_heads, value_heads, preferred_element_type=jnp.float32
    )
    delta = jnp.sum(probs * prob_grad, axis=-1, keepdims=True)
    score_grad = (probs * (prob_grad - delta)).astype(jnp.bfloat16)
    scale = head_size ** (-0.5)
    query_back = jnp.einsum(
        "ngbs,snd->bngd", score_grad, key_heads, preferred_element_type=jnp.float32
    )
    key_back = jnp.einsum(
        "ngbs,bngd->snd", score_grad, query_heads, preferred_element_type=jnp.float32
    )
    value_back = jnp.einsum(
        "ngbs,bngd->snd", probs.astype(jnp.bfloat16), grad_heads, preferred_element_type=jnp.float32
    )
    key_count = keys_all.shape[0]
    return (
        query_back.reshape(queries.shape[0], -1) * scale,
        key_back.reshape(key_count, -1) * scale,
        value_back.reshape(key_count, -1),
    )


def per_device_wide(
    inputs,
    cotangent,
    segments,
    w_query,
    key_weight,
    value_weight,
    w_output,
    w_gate,
    w_up,
    w_down,
    attn_gain,
    mlp_gain,
    query_gain,
    key_gain,
):
    section_first = lax.axis_index(SECTION) == 0
    gathered = (
        lax.all_gather(w_query[0], DP, axis=0, tiled=True),
        lax.all_gather(key_weight[0], DP, axis=0, tiled=True),
        lax.all_gather(value_weight[0], DP, axis=0, tiled=True),
        lax.all_gather(w_output[0], DP, axis=0, tiled=True),
        lax.all_gather(w_gate[0], DP, axis=0, tiled=True),
        lax.all_gather(w_up[0], DP, axis=0, tiled=True),
        lax.all_gather(w_down[0], DP, axis=0, tiled=True),
        lax.all_gather(attn_gain[0], DP, axis=0, tiled=True),
        lax.all_gather(mlp_gain[0], DP, axis=0, tiled=True),
    )
    w_q, w_k, w_v, w_o, w_g, w_u, w_d = gathered[:7]
    gain_attn = gathered[7].astype(jnp.float32)
    gain_mlp = gathered[8].astype(jnp.float32)
    gain_q = query_gain[0].astype(jnp.float32)
    gain_k = key_gain[0].astype(jnp.float32)
    head_size = gain_q.shape[0]
    doc_table = lax.all_gather(segments, DP, axis=1, tiled=True)
    batch_count, row_count, model_width = inputs.shape
    token_count = doc_table.shape[1]
    positions = lax.axis_index(DP) * row_count + jnp.arange(row_count, dtype=jnp.int32)
    key_pos = jnp.arange(token_count, dtype=jnp.int32)
    cosine, sine_table = rope_tables(positions, head_size)
    rope_query = partial(rotate_norm, cosine=cosine, sine_table=sine_table)
    arrived = jnp.zeros((row_count, model_width), jnp.bfloat16)
    stored_steps, outgoing_steps = ([], [])
    for step_index in range(batch_count + 1):
        early = min(step_index, batch_count - 1)
        late = max(step_index - 1, 0)
        layer_in = jnp.where(
            section_first, inputs[early].astype(jnp.float32), arrived.astype(jnp.float32)
        )
        own_segs = jnp.where(section_first, segments[early], segments[late])
        doc_row = jnp.where(section_first, doc_table[early], doc_table[late])
        forward_normed = rms_scale(layer_in, gain_attn).astype(jnp.bfloat16)
        forward_queries = dot_plain(forward_normed, w_q)
        forward_key_raw = dot_plain(forward_normed, w_k)
        forward_value_raw = dot_plain(forward_normed, w_v).astype(jnp.bfloat16)
        forward_query_rot = rope_query(forward_queries, gain_q).astype(jnp.bfloat16)
        forward_key_rot = rope_query(forward_key_raw, gain_k).astype(jnp.bfloat16)
        forward_keys_all = lax.all_gather(forward_key_rot, DP, axis=0, tiled=True)
        forward_values_all = lax.all_gather(forward_value_raw, DP, axis=0, tiled=True)
        forward_allowed = (key_pos[None, :] <= positions[:, None]) & (
            own_segs[:, None] == doc_row[None, :]
        )
        forward_attn, forward_log_total = attend(
            forward_query_rot, forward_keys_all, forward_values_all, forward_allowed, head_size
        )
        forward_mixed = layer_in + lax.psum(dot_last(forward_attn, w_o), TENSOR)
        forward_normed_mlp = rms_scale(forward_mixed, gain_mlp).astype(jnp.bfloat16)
        forward_gate_raw = dot_plain(forward_normed_mlp, w_g)
        forward_up_raw = dot_plain(forward_normed_mlp, w_u)
        forward_activated = swiglu(forward_gate_raw, forward_up_raw).astype(jnp.bfloat16)
        layer_out = forward_mixed + lax.psum(dot_last(forward_activated, w_d), TENSOR)
        forward_stored = (
            layer_in,
            forward_normed,
            forward_queries,
            forward_key_raw,
            forward_query_rot,
            forward_key_rot,
            forward_value_raw,
            forward_attn,
            forward_log_total,
            forward_mixed,
            forward_normed_mlp,
            forward_gate_raw,
            forward_up_raw,
            forward_activated,
            forward_allowed,
        )
        layer_out, stored = (layer_out, forward_stored)
        outgoing = layer_out.astype(jnp.bfloat16)
        stored_steps.append(stored)
        outgoing_steps.append(outgoing)
        if step_index < batch_count:
            arrived = shifted(outgoing, SECTION, 1)
    section_out = jnp.stack(
        [
            jnp.where(section_first, outgoing_steps[batch_index], outgoing_steps[batch_index + 1])
            for batch_index in range(batch_count)
        ]
    )
    back_arrived = jnp.zeros((row_count, model_width), jnp.bfloat16)
    grad_steps = []
    totals = None
    norm_totals = None
    for step_index in range(batch_count + 1):
        early_batch = min(batch_count - step_index, batch_count - 1)
        late_batch = max(batch_count - 1 - step_index, 0)
        stored = jax.tree.map(
            lambda a, b: jnp.where(section_first, a, b),
            stored_steps[early_batch],
            stored_steps[late_batch + 1],
        )
        valid = jnp.where(
            section_first,
            jnp.float32(1.0 if step_index >= 1 else 0.0),
            jnp.float32(1.0 if step_index < batch_count else 0.0),
        )
        grad_out = (
            jnp.where(
                section_first,
                back_arrived.astype(jnp.float32),
                cotangent[late_batch].astype(jnp.float32),
            )
            * valid
        )
        (
            backward_layer_in,
            normed,
            queries,
            key_raw,
            query_rot,
            key_rot,
            value_raw,
            attn,
            log_total,
            mixed,
            normed_mlp,
            gate_raw,
            up_raw,
            activated,
            allowed,
        ) = stored[:15]
        keys_all = lax.all_gather(key_rot, DP, axis=0, tiled=True)
        values_all = lax.all_gather(value_raw, DP, axis=0, tiled=True)
        mlp_grad = grad_out.astype(jnp.bfloat16)
        act_grad = dot_plain(mlp_grad, w_d)
        grad_wd = dot_first(mlp_grad, activated)
        unused, swiglu_back = jax.vjp(swiglu, gate_raw, up_raw)
        gate_grad, up_grad = swiglu_back(act_grad)
        gate_grad = gate_grad.astype(jnp.bfloat16)
        up_grad = up_grad.astype(jnp.bfloat16)
        grad_wg = dot_first(normed_mlp, gate_grad)
        grad_wu = dot_first(normed_mlp, up_grad)
        normed_mlp_grad = lax.psum(
            (dot_last(gate_grad, w_g) + dot_last(up_grad, w_u)).astype(jnp.bfloat16), TENSOR
        ).astype(jnp.float32)
        unused, mlp_norm_back = jax.vjp(rms_scale, mixed, gain_mlp)
        mixed_part, grad_gain_mlp = mlp_norm_back(normed_mlp_grad)
        mixed_grad = grad_out + mixed_part
        branch_low = mixed_grad.astype(jnp.bfloat16)
        attn_grad = dot_plain(branch_low, w_o).astype(jnp.bfloat16)
        grad_wo = dot_first(branch_low, attn)
        query_back, key_back, value_back = attend_back(
            query_rot, keys_all, values_all, allowed, log_total, attn_grad, head_size
        )
        backward_key_total = lax.psum_scatter(
            key_back.astype(jnp.bfloat16), DP, scatter_dimension=0, tiled=True
        ).astype(jnp.float32)
        value_total = lax.psum_scatter(
            value_back.astype(jnp.bfloat16), DP, scatter_dimension=0, tiled=True
        )
        unused, key_rope_back = jax.vjp(rope_query, key_raw, gain_k)
        key_gradient, grad_gain_k = key_rope_back(backward_key_total)
        key_gradient = key_gradient.astype(jnp.bfloat16)
        unused, query_rope_back = jax.vjp(rope_query, queries, gain_q)
        query_grad, grad_gain_q = query_rope_back(query_back)
        query_grad = query_grad.astype(jnp.bfloat16)
        grad_wq = dot_first(normed, query_grad)
        grad_wk = dot_first(normed, key_gradient)
        grad_wv = dot_first(normed, value_total)
        normed_grad = lax.psum(
            (
                dot_last(query_grad, w_q) + dot_last(key_gradient, w_k) + dot_last(value_total, w_v)
            ).astype(jnp.bfloat16),
            TENSOR,
        ).astype(jnp.float32)
        unused, attn_norm_back = jax.vjp(rms_scale, backward_layer_in, gain_attn)
        input_part, grad_gain_attn = attn_norm_back(normed_grad)
        weight_part = (
            grad_wq,
            grad_wk,
            grad_wv,
            grad_wo,
            grad_wg,
            grad_wu,
            grad_wd,
            grad_gain_attn,
            grad_gain_mlp,
        )
        input_grad, weight_part, norm_part = (
            mixed_grad + input_part,
            weight_part,
            (grad_gain_q, grad_gain_k),
        )
        outgoing = input_grad.astype(jnp.bfloat16)
        grad_steps.append(outgoing)
        if step_index < batch_count:
            back_arrived = shifted(outgoing, SECTION, -1)
        totals = (
            weight_part if totals is None else tuple((a + b for a, b in zip(totals, weight_part)))
        )
        norm_totals = (
            norm_part
            if norm_totals is None
            else tuple((a + b for a, b in zip(norm_totals, norm_part)))
        )
    shards = jax.tree.map(
        lambda part: part.astype(jnp.float32),
        lax.psum_scatter(as_sent(totals), DP, scatter_dimension=0, tiled=True),
    )
    query_total, key_total = lax.psum(norm_totals, (TENSOR, DP))
    input_grads = jnp.stack(
        [
            jnp.where(
                section_first,
                grad_steps[batch_count - batch_index],
                grad_steps[batch_count - 1 - batch_index],
            )
            for batch_index in range(batch_count)
        ]
    )
    return (
        (section_out[None], input_grads[None])
        + tuple((member[None] for member in shards))
        + (query_total[None], key_total[None])
    )


def paired(x, axis, flip):
    count = lax.axis_size(axis)
    return lax.ppermute(x, axis, [(i, i ^ flip) for i in range(count)])


def ring_order(count):
    return list(range(0, count, 2)) + list(range(count - 1, 0, -2))


def ring(x, by):
    order = ring_order(lax.axis_size(DP))
    count = len(order)
    pairs = []
    for core, step in ((0, by), (1, -by)):
        for i in range(count):
            pairs.append((core * count + order[i], core * count + order[(i + step) % count]))
    return lax.ppermute(x, (TENSOR, DP), pairs)


def received_order(count):
    half = count // 2
    return [(0, False)] + [(s, lag) for s in range(1, half) for lag in (False, True)] + [(half, False)]


def near_chunks(count):
    return 2 * (count // 2 - 2) + 1


def gate(value, token):
    return lax.optimization_barrier((value, token))[0]


def whole_vmem(count):
    return [pl.BlockSpec(memory_space=pltpu.VMEM)] * count


def joined(pieces):
    rows = sum(piece.shape[0] for piece in pieces)
    width = pieces[0].shape[1]

    def kernel(*refs):
        at = 0
        for ref in refs[:-1]:
            refs[-1][at : at + ref.shape[0], :] = ref[...]
            at += ref.shape[0]

    return pl.pallas_call(
        kernel,
        out_shape=jax.ShapeDtypeStruct((rows, width), pieces[0].dtype),
        in_specs=whole_vmem(len(pieces)),
        out_specs=pl.BlockSpec(memory_space=pltpu.VMEM),
        cost_estimate=pl.CostEstimate(flops=0, bytes_accessed=4 * rows * width, transcendentals=0),
    )(*pieces)


def gather_ring(chunk):
    count = lax.axis_size(DP)
    half = count // 2
    lead, lag = chunk, paired(chunk, TENSOR, 1)
    chunks, token = [chunk], None
    for step in range(1, half + 1):
        lead = ring(lead, 1)
        chunks.append(lead)
        if step < half:
            lag = ring(lag, 1)
            chunks.append(lag)
        if step == half - 1:
            token = lead
    cut = near_chunks(count)
    near, far = joined(gate(chunks[:cut], token)), joined(chunks[cut:])
    return [near, far, paired(near, TENSOR, 1), paired(far, TENSOR, 1)], token


def multiplied(parts, weight):
    return jnp.concatenate(parts, axis=0), by_parts(parts, weight)


def by_parts(parts, weight):
    return jnp.concatenate([dot_plain(part, weight) for part in parts], axis=0)


def product_scattered(act, weight):
    count = lax.axis_size(DP)
    half = count // 2
    side = act.shape[0] // 2
    rows = side // count
    near = near_chunks(count) * rows
    far_sum = dot_last(act[side + near :], weight).astype(jnp.bfloat16)
    near_sum = dot_last(act[side : side + near], weight).astype(jnp.bfloat16)
    own = dot_last(act[:side], weight)
    far_sum = paired(far_sum, TENSOR, 1)
    near_sum = paired(near_sum, TENSOR, 1)
    spots = {key: i * rows for i, key in enumerate(received_order(count))}

    def part(hops, lag):
        at = spots[hops, lag]
        extra = far_sum[at - near :][:rows] if at >= near else near_sum[at : at + rows]
        return own[at : at + rows] + extra.astype(jnp.float32)

    def hop(value, hops, lag):
        total = part(hops, lag)
        if value is not None:
            total = total + value.astype(jnp.float32)
        return ring(total.astype(jnp.bfloat16), -1)

    lead = lag = token = None
    for hops in range(half, 0, -1):
        lead = hop(lead, hops, False)
        if hops < half:
            lag = hop(lag, hops, True)
        if hops == half:
            token = lead
    across = paired(lag, TENSOR, 1)
    return part(0, False) + lead.astype(jnp.float32) + across.astype(jnp.float32), token


def place_rows(blocks, flags, widths):
    count = len(blocks)
    rows, total = blocks[0].shape
    part = rows // 2

    def kernel(flags_ref, *refs):
        for s in range(count):
            left = 0
            for out, width in zip(refs[count:], widths):
                for half in range(2):
                    at = pl.multiple_of((flags_ref[0] ^ s) * part + half * count * part, part)
                    top = half * part
                    out[pl.ds(at, part), :] = refs[s][top : top + part, left : left + width]
                left += width

    size = 2 * count * rows * total
    return pl.pallas_call(
        kernel,
        out_shape=[jax.ShapeDtypeStruct((count * rows, w), blocks[0].dtype) for w in widths],
        in_specs=[pl.BlockSpec(memory_space=pltpu.SMEM)] + whole_vmem(count),
        out_specs=whole_vmem(len(widths)),
        cost_estimate=pl.CostEstimate(flops=0, bytes_accessed=2 * size, transcendentals=0),
    )(flags, *blocks)


def packed(pairs, flags, count):
    rows = pairs[0][0].shape[0] // count
    widths = [kept.shape[1] for kept, _ in pairs]

    def kernel(flags_ref, *refs):
        ins, outs = refs[: 2 * len(pairs)], refs[2 * len(pairs) :]
        for s, out in enumerate(outs):
            at = pl.ds(pl.multiple_of((flags_ref[0] ^ s) * rows, rows), rows)
            left = 0
            for i, width in enumerate(widths):
                value = ins[2 * i][at, :].astype(jnp.float32)
                value += ins[2 * i + 1][at, :].astype(jnp.float32)
                out[:, left : left + width] = value.astype(out.dtype)
                left += width

    operands = [array for pair in pairs for array in pair]
    size = 2 * count * rows * sum(widths)
    return pl.pallas_call(
        kernel,
        out_shape=[jax.ShapeDtypeStruct((rows, sum(widths)), jnp.bfloat16)] * count,
        in_specs=[pl.BlockSpec(memory_space=pltpu.SMEM)] + whole_vmem(len(operands)),
        out_specs=whole_vmem(count),
        cost_estimate=pl.CostEstimate(flops=0, bytes_accessed=3 * size, transcendentals=0),
    )(flags, *operands)


def place_columns(first, second, flags, widths, shared, skip):
    count = len(first)
    rows = first[0].shape[0]
    columns = [w * count // (2 if wide else 1) for w, wide in zip(widths, shared)]
    total = sum(columns)

    def kernel(flags_ref, *refs):
        kept, sent = refs[2 * count :]

        def fill(out, blocks, left):
            base = 0
            for width, wide, room in zip(widths, shared, columns):
                for s in range(0, count, 2 if wide else 1):
                    index = flags_ref[0] ^ s
                    at = base + (index // 2 if wide else index) * width
                    value = blocks[s][:, left : left + width]
                    if wide:
                        value = value.astype(jnp.float32) + blocks[s + 1][
                            :, left : left + width
                        ].astype(jnp.float32)
                    out[:, pl.ds(pl.multiple_of(at, 128), width)] = value.astype(out.dtype)
                left += width
                base += room

        @pl.when(flags_ref[1] == 0)
        def _():
            fill(kept, refs[:count], 0)
            fill(sent, refs[count : 2 * count], skip)

        @pl.when(flags_ref[1] != 0)
        def _():
            fill(sent, refs[:count], 0)
            fill(kept, refs[count : 2 * count], skip)

    return pl.pallas_call(
        kernel,
        out_shape=[jax.ShapeDtypeStruct((rows, total), first[0].dtype)] * 2,
        in_specs=[pl.BlockSpec(memory_space=pltpu.SMEM)] + whole_vmem(2 * count),
        out_specs=whole_vmem(2),
        cost_estimate=pl.CostEstimate(
            flops=0, bytes_accessed=4 * count * rows * sum(widths) * 2, transcendentals=0
        ),
    )(flags, *first, *second)


def head_attend(query, key, value, allowed):
    scores = dot_last(query, key) * query.shape[1] ** (-0.5)
    scores = jnp.where(allowed, scores, MASKED)
    highest = jnp.max(scores, axis=-1, keepdims=True)
    weights = jnp.exp(scores - highest)
    total = jnp.sum(weights, axis=-1, keepdims=True)
    probs = (weights / total).astype(jnp.bfloat16)
    return dot_plain(probs, value).astype(jnp.bfloat16), highest + jnp.log(total)


def head_attend_back(query, key, value, allowed, log_total, grad):
    scale = query.shape[1] ** (-0.5)
    scores = jnp.where(allowed, dot_last(query, key) * scale, MASKED)
    probs = jnp.exp(scores - log_total)
    prob_grad = dot_last(grad, value)
    delta = jnp.sum(probs * prob_grad, axis=-1, keepdims=True)
    score_grad = (probs * (prob_grad - delta)).astype(jnp.bfloat16)
    return (
        dot_plain(score_grad, key) * scale,
        dot_first(score_grad, query) * scale,
        dot_first(probs.astype(jnp.bfloat16), grad),
    )


def per_device(
    inputs,
    cotangent,
    segments,
    w_query,
    key_weight,
    value_weight,
    w_output,
    w_gate,
    w_up,
    w_down,
    attn_gain,
    mlp_gain,
    query_gain,
    key_gain,
):
    count = lax.axis_size(DP)
    plane = lax.axis_index(SECTION)
    me = lax.axis_index(DP)
    core = lax.axis_index(TENSOR)
    flags = jnp.stack([me, plane]).astype(jnp.int32)
    model_width = inputs.shape[2]
    rows = inputs.shape[1] // 2
    head_size = query_gain.shape[1]
    ff_width = w_gate.shape[2] // count
    group_size = w_query.shape[2] // key_weight.shape[2]
    gain_width = attn_gain.shape[1]

    def by_layer(own):
        theirs = paired(own, SECTION, 1)
        first = plane == 0
        return [jnp.where(first, own, theirs), jnp.where(first, theirs, own)]

    part = gain_width // 2

    def halved(array):
        wide = array.reshape(-1, count, 2, part)
        return jnp.swapaxes(wide, 1, 2).reshape(array.shape)

    def unhalved(array):
        wide = array.reshape(-1, 2, count, part)
        return jnp.swapaxes(wide, 1, 2).reshape(array.shape)

    def own_rows(array):
        own = lax.dynamic_slice(array, (plane, core * rows, 0), (1, rows, model_width))[0]
        return halved(own)

    gains = jnp.concatenate([attn_gain[0], mlp_gain[0], query_gain[0], key_gain[0]])
    gains = jnp.concatenate(by_layer(gains.astype(jnp.float32)))
    docs = lax.dynamic_index_in_dim(segments, plane, 0, keepdims=False).astype(jnp.float32)
    note = jnp.concatenate([gains, docs])
    notes = jnp.stack([note] + [paired(note, DP, s) for s in range(1, count)])
    notes = jnp.concatenate(
        [lax.dynamic_slice_in_dim(notes, me ^ j, 1, axis=0) for j in range(count)], axis=0
    )
    per_layer = gains.shape[0] // 2
    layer_gains = []
    for layer in range(2):
        at = layer * per_layer
        layer_gains.append(
            (
                halved(notes[:, at : at + gain_width].reshape(-1)),
                halved(notes[:, at + gain_width : at + 2 * gain_width].reshape(-1)),
                gains[at + 2 * gain_width : at + 2 * gain_width + head_size],
                gains[at + 2 * gain_width + head_size : at + per_layer],
            )
        )
    doc_table = notes[:, 2 * per_layer :].reshape(count, 2, rows)

    place = jnp.where(me % 2 == 0, me // 2, count - 1 - me // 2)
    docs_parts, pos_parts = ([], []), ([], [])
    away = 2 * core - 1
    for at in range(2):
        for hops, lag in received_order(count):
            side = core if lag == bool(at) else 1 - core
            spot = (place + (away if at == 0 else -away) * hops + count) % count
            owner = jnp.where(spot < count // 2, 2 * spot, 2 * (count - 1 - spot) + 1)
            block = lax.dynamic_index_in_dim(doc_table, owner, 0, keepdims=False)
            docs_parts[at].append(lax.dynamic_index_in_dim(block, side, 0, keepdims=False))
            start = owner * 2 * rows + side * rows
            pos_parts[at].append(start + jnp.arange(rows, dtype=jnp.int32))
    docs_all = jnp.concatenate(docs_parts[0] + docs_parts[1])
    positions = jnp.concatenate(pos_parts[0] + pos_parts[1])
    allowed = (positions[None, :] <= positions[:, None]) & (docs_all[:, None] == docs_all[None, :])
    cosine, sine_table = rope_tables(positions, head_size)
    rope = partial(rotate_norm, cosine=cosine, sine_table=sine_table)

    def cut(pieces):
        def block(to):
            return jnp.concatenate(
                [
                    lax.dynamic_slice_in_dim(
                        array, (to // share) * stride + skip, width, axis=1
                    )
                    for array, width, share, stride, skip in pieces
                ],
                axis=1,
            )

        return [block(me ^ s) for s in range(count)]

    def turn(blocks):
        moved = [blocks[0]]
        for s in range(1, count):
            moved.append(paired(blocks[s], DP, s))
        return moved

    def both_layers(blocks, widths):
        sets = []
        for placed in place_rows(blocks, flags, widths):
            facing = paired(placed, SECTION, 1)
            sets.append([jnp.where(plane == layer, placed, facing) for layer in range(2)])
        return sets

    wide = ff_width * 2 // 3

    def heads(array, share):
        return (array[0], head_size, share, head_size, 0)

    def hidden(array, width, skip):
        return (array[0], width, 1, ff_width, skip)

    sliced = {
        "qk": cut((heads(w_query, 1), heads(key_weight, group_size))),
        "vo": cut((heads(value_weight, group_size), heads(w_output, 1))),
        "g": cut((hidden(w_gate, ff_width, 0),)),
        "u": cut((hidden(w_up, ff_width, 0),)),
        "d": cut((hidden(w_down, wide, 0),)),
        "e": cut((hidden(w_down, ff_width - wide, wide),)),
    }
    turned, weights = {}, {}

    def attention(raw, value, layer):
        _, _, gain_q, gain_k = layer_gains[layer]
        queries, key_raw = raw[:, :head_size], raw[:, head_size:]
        value = value.astype(jnp.bfloat16)
        query_rot = rope(queries, gain_q).astype(jnp.bfloat16)
        key_rot = rope(key_raw, gain_k).astype(jnp.bfloat16)
        attn, log_total = head_attend(query_rot, key_rot, value, allowed)
        return attn, (queries, key_raw, value, query_rot, key_rot, log_total)

    def forward(layer_in, layer):
        gain_attn, gain_mlp, _, _ = layer_gains[layer]
        if layer == 0:
            turned["qk"] = turn(sliced["qk"])
            parts, token = gather_ring(layer_in.astype(jnp.bfloat16))
            raw_in = joined(parts).astype(jnp.float32)
            weights["qk"] = both_layers(turned["qk"], (2 * head_size,))[0]
            turned["vo"] = turn(gate(sliced["vo"], turned["qk"]))
            weights["v"], weights["o"] = both_layers(turned["vo"], (head_size, head_size))
            turned["g"] = turn(gate(sliced["g"], turned["vo"]))
            normed = rms_scale(raw_in, gain_attn).astype(jnp.bfloat16)
            raw = dot_plain(normed, weights["qk"][0])
            value = dot_plain(normed, weights["v"][0])
        else:
            chunk = rms_scale(layer_in, gain_attn).astype(jnp.bfloat16)
            parts, token = gather_ring(chunk)
            normed, raw = multiplied(parts, weights["qk"][layer])
            value = by_parts(parts, weights["v"][layer])
        attn, kept = attention(raw, value, layer)
        if layer == 0:
            turned["u"] = turn(gate(sliced["u"], turned["g"]))
            weights["g"] = both_layers(gate(turned["g"], raw), (ff_width,))[0]
            extra = None
        else:
            cotangent_rows = own_rows(cotangent)
            extra, token = gather_ring(gate(cotangent_rows, raw))
            attn = gate(attn, extra[1])
        summed, token = product_scattered(attn, weights["o"][layer])
        mixed = layer_in + summed
        if layer == 0:
            weights["u"] = both_layers(gate(turned["u"], token), (ff_width,))[0]
            turned["d"] = turn(gate(sliced["d"], turned["u"]))
            turned["e"] = turn(gate(sliced["e"], turned["d"]))
            weights["gu"] = [
                jnp.concatenate([weights["g"][i], weights["u"][i]], axis=1) for i in range(2)
            ]
        parts, token = gather_ring(rms_scale(mixed, gain_mlp).astype(jnp.bfloat16))
        if layer == 0:
            weights["d"] = both_layers(gate(turned["d"], token), (wide,))[0]
            weights["e"] = both_layers(gate(turned["e"], parts[1]), (ff_width - wide,))[0]
            weights["d"] = [
                jnp.concatenate([weights["d"][i], weights["e"][i]], axis=1) for i in range(2)
            ]
        normed_mlp, raw_mlp = multiplied(parts, weights["gu"][layer])
        gate_raw, up_raw = raw_mlp[:, :ff_width], raw_mlp[:, ff_width:]
        activated = swiglu(gate_raw, up_raw).astype(jnp.bfloat16)
        stored = (layer_in, normed, kept, attn, mixed, normed_mlp, gate_raw, up_raw, activated)

        def finish(after):
            held = activated if after is None else gate(activated, after)
            summed, _ = product_scattered(held, weights["d"][layer])
            return ((mixed + summed).astype(jnp.bfloat16),)

        return finish, stored, extra

    def halves(grad):
        span = grad.shape[0] // 2
        sent = lax.dynamic_slice_in_dim(grad, (1 - plane) * span, span, axis=0)
        kept = lax.dynamic_slice_in_dim(grad, plane * span, span, axis=0).astype(jnp.bfloat16)
        return kept, paired(sent.astype(jnp.bfloat16), SECTION, 1)

    turns = []

    def returned(pairs, token):
        if token is not None:
            pairs = [(kept, gate(taken, token)) for kept, taken in pairs]
        if len(turns) > 1:
            pairs = [(kept, gate(taken, turns[-2])) for kept, taken in pairs]
        turns.append(turn(packed(pairs, flags, count)))
        return turns[-1]

    def backward(gathered, grad_out, stored, layer, back, late):
        layer_in, normed, kept, attn, mixed, normed_mlp, gate_raw, up_raw, activated = stored
        queries, key_raw, value, query_rot, key_rot, log_total = kept
        gain_attn, gain_mlp, gain_q, gain_k = layer_gains[layer]
        if late is not None:
            late = late(None)
        out_low, act_grad = multiplied(gathered, weights["d"][layer])
        unused, swiglu_back = jax.vjp(swiglu, gate_raw, up_raw)
        gate_grad, up_grad = swiglu_back(act_grad)
        raw_grad = jnp.concatenate([gate_grad, up_grad], axis=1).astype(jnp.bfloat16)
        summed, token = product_scattered(raw_grad, weights["gu"][layer])
        sums = {}
        sums["d"] = halves(dot_first(out_low, activated))
        sums["gu"] = halves(dot_first(normed_mlp, raw_grad))
        unused, mlp_norm_back = jax.vjp(rms_scale, mixed, gain_mlp)
        mixed_part, grad_gain_mlp = mlp_norm_back(summed)
        mixed_grad = grad_out + mixed_part
        parts, token = gather_ring(mixed_grad.astype(jnp.bfloat16))
        attn_grad = by_parts(parts, weights["o"][layer])
        back["mlp"] = returned((sums["gu"], sums["d"]), parts[1])
        query_back, key_back, value_back = head_attend_back(
            query_rot, key_rot, value, allowed, log_total, attn_grad.astype(jnp.bfloat16)
        )
        unused, key_rope_back = jax.vjp(rope, key_raw, gain_k)
        key_grad, grad_gain_k = key_rope_back(key_back)
        unused, query_rope_back = jax.vjp(rope, queries, gain_q)
        query_grad, grad_gain_q = query_rope_back(query_back)
        qkv_grad = jnp.concatenate([query_grad, key_grad, value_back], axis=1).astype(jnp.bfloat16)
        summed, token = product_scattered(qkv_grad, weights["qkv"][layer])
        grad_o, top = 0.0, 0
        for rows_part in parts:
            span = rows_part.shape[0]
            grad_o = grad_o + dot_first(rows_part, attn[top : top + span])
            top += span
        grad_attn = jnp.concatenate([dot_first(normed, qkv_grad), grad_o], axis=1)
        sums = halves(grad_attn)
        unused, attn_norm_back = jax.vjp(rms_scale, layer_in, gain_attn)
        input_part, grad_gain_attn = attn_norm_back(summed)
        small = (grad_gain_attn, grad_gain_mlp, grad_gain_q, grad_gain_k)
        points = token
        return mixed_grad + input_part, sums, small, points, late

    finish, stored_first, _ = forward(own_rows(inputs).astype(jnp.float32), 0)
    out_first = finish(None)[0]
    weights["qkv"] = [
        jnp.concatenate([weights["qk"][i], weights["v"][i]], axis=1) for i in range(2)
    ]
    finish, stored_second, gathered = forward(out_first.astype(jnp.float32), 1)
    back_second, back_first = {}, {}
    grad_second, waiting, small_second, points, last = backward(
        gathered, own_rows(cotangent).astype(jnp.float32), stored_second, 1, back_second, finish
    )
    out_second = last[0]
    grad_second = grad_second.astype(jnp.bfloat16)
    gathered, _ = gather_ring(grad_second)
    back_second["attn"] = returned((waiting,), gathered[1])
    grad_first, waiting, small_first, points, last = backward(
        gathered, grad_second.astype(jnp.float32), stored_first, 0, back_first, None
    )
    grad_first = grad_first.astype(jnp.bfloat16)
    back_first["attn"] = returned((waiting,), None)

    def by_section(first, second):
        first, second = unhalved(first), unhalved(second)
        kept = jnp.where(plane == 0, first, second)
        taken = paired(jnp.where(plane == 0, second, first), SECTION, 1)
        both = jnp.where(plane == 0, jnp.stack([kept, taken]), jnp.stack([taken, kept]))
        facing = paired(both, TENSOR, 1)
        whole = jnp.where(
            core == 0,
            jnp.concatenate([both, facing], axis=1),
            jnp.concatenate([facing, both], axis=1),
        )
        return whole[None], facing

    section_out, _ = by_section(out_first, out_second)
    input_grads, facing = by_section(grad_first, grad_second)

    def owned(name, widths, shared, token, other=None, skip=0):
        firsts, seconds = back_first[name], back_second[other or name]
        kept, sent = place_columns(firsts, seconds, flags, widths, shared, skip)
        taken = paired(sent, SECTION, 1)
        if token is not None:
            taken = gate(taken, token)
        both = jnp.where(
            plane == 0,
            jnp.concatenate([kept, taken], axis=0),
            jnp.concatenate([taken, kept], axis=0),
        )
        return both.astype(jnp.float32)

    ff_total = w_gate.shape[2]
    grad_mlp = owned("mlp", (ff_width,) * 3, (False,) * 3, None)
    grad_attn = owned("attn", (head_size,) * 4, (False, True, True, False), facing)
    edges = [0]
    for array in (w_query, key_weight, value_weight, w_output):
        edges.append(edges[-1] + array.shape[2])
    attn_grads = [grad_attn[:, a:b] for a, b in zip(edges, edges[1:])]
    mlp_grads = [grad_mlp[:, i * ff_total : (i + 1) * ff_total] for i in range(3)]

    rows_of = jnp.concatenate(
        [
            part.reshape(count, -1)
            for small in (small_first, small_second)
            for part in (
                unhalved(small[0]),
                unhalved(small[1]),
                jnp.tile(small[2], count),
                jnp.tile(small[3], count),
            )
        ],
        axis=1,
    )

    gain_sum, step = rows_of, count // 2
    while step:
        bit = (me // step) % 2
        gain_sum = gain_sum.reshape(2, step, -1)
        kept = lax.dynamic_index_in_dim(gain_sum, bit, 0, keepdims=False)
        sent = lax.dynamic_index_in_dim(gain_sum, 1 - bit, 0, keepdims=False)
        gain_sum = kept + paired(sent, DP, step)
        step //= 2
    gain_sum = gain_sum.reshape(-1)
    gain_sum = gain_sum + paired(gain_sum, TENSOR, 1)
    gain_sum = gain_sum + paired(gain_sum, SECTION, 1)
    mine = jnp.where(plane == 0, gain_sum[:per_layer], gain_sum[per_layer:])
    grad_gain_attn = mine[:gain_width]
    grad_gain_mlp = mine[gain_width : 2 * gain_width]
    grad_gain_q = mine[2 * gain_width : 2 * gain_width + head_size]
    grad_gain_k = mine[2 * gain_width + head_size :]
    shards = (
        attn_grads[0], attn_grads[1], attn_grads[2], attn_grads[3],
        mlp_grads[0], mlp_grads[1], mlp_grads[2],
        grad_gain_attn, grad_gain_mlp, grad_gain_q, grad_gain_k,
    )
    return (section_out, input_grads) + tuple(part[None] for part in shards)


def fits(mesh):
    sizes = dict(mesh.shape)
    return sizes[DP] == 8 and sizes[TENSOR] == 2 and sizes[SECTION] == 2


def solution(mesh):
    return jax.shard_map(
        per_device if fits(mesh) else per_device_wide,
        mesh=mesh,
        in_specs=(
            P(None, DP, None),
            P(None, DP, None),
            P(None, DP),
            P(SECTION, DP, TENSOR),
            P(SECTION, DP, TENSOR),
            P(SECTION, DP, TENSOR),
            P(SECTION, DP, TENSOR),
            P(SECTION, DP, TENSOR),
            P(SECTION, DP, TENSOR),
            P(SECTION, DP, TENSOR),
            P(SECTION, DP),
            P(SECTION, DP),
            P(SECTION, None),
            P(SECTION, None),
        ),
        out_specs=(
            P(SECTION, None, DP, None),
            P(SECTION, None, DP, None),
            P(SECTION, DP, TENSOR),
            P(SECTION, DP, TENSOR),
            P(SECTION, DP, TENSOR),
            P(SECTION, DP, TENSOR),
            P(SECTION, DP, TENSOR),
            P(SECTION, DP, TENSOR),
            P(SECTION, DP, TENSOR),
            P(SECTION, DP),
            P(SECTION, DP),
            P(SECTION, None),
            P(SECTION, None),
        ),
        check_vma=False,
    )
```

```python
from functools import partial

import jax
import jax.numpy as jnp
from jax import lax
from jax.experimental import pallas as pl
from jax.experimental.pallas import tpu as pltpu
from jax.sharding import PartitionSpec as P


SECTION, TENSOR, DP = "section", "tensor", "dp"
EPSILON = 1e-06
MASKED = -1e30


def shifted(x, axis, by):
    count = lax.axis_size(axis)
    pairs = [(i, i + by) for i in range(count) if 0 <= i + by < count]
    return lax.ppermute(x, axis, pairs)


def as_sent(x):

    def short(part):
        return part.astype(jnp.bfloat16) if part.dtype == jnp.float32 else part

    return jax.tree.map(short, x)


def dot_plain(left, right):
    return jnp.dot(left, right, preferred_element_type=jnp.float32)


def dot_last(left, right):
    return lax.dot_general(
        left, right, (((1,), (1,)), ((), ())), preferred_element_type=jnp.float32
    )


def dot_first(left, right):
    return lax.dot_general(
        left, right, (((0,), (0,)), ((), ())), preferred_element_type=jnp.float32
    )


def rms_scale(values, norm_gain):
    return (
        values * lax.rsqrt(jnp.mean(values * values, axis=-1, keepdims=True) + EPSILON) * norm_gain
    )


def swiglu(gate_raw, up_raw):
    return jax.nn.silu(gate_raw) * up_raw


def rope_tables(positions, head_size):
    half_size = head_size // 2
    freqs = jnp.power(
        jnp.float32(1000000.0), -jnp.arange(half_size, dtype=jnp.float32) * 2.0 / head_size
    )
    angles = positions.astype(jnp.float32)[:, None] * freqs[None, :]
    angles = jnp.concatenate([angles, angles], axis=-1)
    return (jnp.cos(angles), jnp.sin(angles))


def rotate_norm(raw_proj, norm_gain, cosine, sine_table):
    head_size = norm_gain.shape[0]
    token_count = raw_proj.shape[0]
    heads = raw_proj.reshape(token_count, -1, head_size)
    normed = rms_scale(heads, norm_gain)
    half_size = head_size // 2
    turned = jnp.concatenate([-normed[..., half_size:], normed[..., :half_size]], axis=-1)
    rotated = normed * cosine[:, None, :] + turned * sine_table[:, None, :]
    return rotated.reshape(token_count, -1)


def scores_for(queries, keys_all, allowed, head_size):
    row_count = queries.shape[0]
    kv_heads = keys_all.shape[1] // head_size
    group_size = queries.shape[1] // keys_all.shape[1]
    query_heads = queries.reshape(row_count, kv_heads, group_size, head_size)
    key_heads = keys_all.reshape(keys_all.shape[0], kv_heads, head_size)
    scores = jnp.einsum(
        "bngd,snd->ngbs", query_heads, key_heads, preferred_element_type=jnp.float32
    ) * head_size ** (-0.5)
    return (jnp.where(allowed[None, None], scores, MASKED), query_heads, key_heads)


def attend(queries, keys_all, values_all, allowed, head_size):
    scores, _, key_heads = scores_for(queries, keys_all, allowed, head_size)
    highest = jnp.max(scores, axis=-1, keepdims=True)
    weights = jnp.exp(scores - highest)
    total = jnp.sum(weights, axis=-1, keepdims=True)
    probs = (weights / total).astype(jnp.bfloat16)
    value_heads = values_all.reshape(key_heads.shape)
    mixed = jnp.einsum("ngbs,snd->bngd", probs, value_heads, preferred_element_type=jnp.float32)
    return (mixed.reshape(queries.shape[0], -1).astype(jnp.bfloat16), highest + jnp.log(total))


def attend_back(queries, keys_all, values_all, allowed, log_total, attn_grad, head_size):
    scores, query_heads, key_heads = scores_for(queries, keys_all, allowed, head_size)
    probs = jnp.exp(scores - log_total)
    value_heads = values_all.reshape(key_heads.shape)
    grad_heads = attn_grad.reshape(query_heads.shape)
    prob_grad = jnp.einsum(
        "bngd,snd->ngbs", grad_heads, value_heads, preferred_element_type=jnp.float32
    )
    delta = jnp.sum(probs * prob_grad, axis=-1, keepdims=True)
    score_grad = (probs * (prob_grad - delta)).astype(jnp.bfloat16)
    scale = head_size ** (-0.5)
    query_back = jnp.einsum(
        "ngbs,snd->bngd", score_grad, key_heads, preferred_element_type=jnp.float32
    )
    key_back = jnp.einsum(
        "ngbs,bngd->snd", score_grad, query_heads, preferred_element_type=jnp.float32
    )
    value_back = jnp.einsum(
        "ngbs,bngd->snd", probs.astype(jnp.bfloat16), grad_heads, preferred_element_type=jnp.float32
    )
    key_count = keys_all.shape[0]
    return (
        query_back.reshape(queries.shape[0], -1) * scale,
        key_back.reshape(key_count, -1) * scale,
        value_back.reshape(key_count, -1),
    )


def per_device_wide(
    inputs,
    cotangent,
    segments,
    w_query,
    key_weight,
    value_weight,
    w_output,
    w_gate,
    w_up,
    w_down,
    attn_gain,
    mlp_gain,
    query_gain,
    key_gain,
):
    section_first = lax.axis_index(SECTION) == 0
    gathered = (
        lax.all_gather(w_query[0], DP, axis=0, tiled=True),
        lax.all_gather(key_weight[0], DP, axis=0, tiled=True),
        lax.all_gather(value_weight[0], DP, axis=0, tiled=True),
        lax.all_gather(w_output[0], DP, axis=0, tiled=True),
        lax.all_gather(w_gate[0], DP, axis=0, tiled=True),
        lax.all_gather(w_up[0], DP, axis=0, tiled=True),
        lax.all_gather(w_down[0], DP, axis=0, tiled=True),
        lax.all_gather(attn_gain[0], DP, axis=0, tiled=True),
        lax.all_gather(mlp_gain[0], DP, axis=0, tiled=True),
    )
    w_q, w_k, w_v, w_o, w_g, w_u, w_d = gathered[:7]
    gain_attn = gathered[7].astype(jnp.float32)
    gain_mlp = gathered[8].astype(jnp.float32)
    gain_q = query_gain[0].astype(jnp.float32)
    gain_k = key_gain[0].astype(jnp.float32)
    head_size = gain_q.shape[0]
    doc_table = lax.all_gather(segments, DP, axis=1, tiled=True)
    batch_count, row_count, model_width = inputs.shape
    token_count = doc_table.shape[1]
    positions = lax.axis_index(DP) * row_count + jnp.arange(row_count, dtype=jnp.int32)
    key_pos = jnp.arange(token_count, dtype=jnp.int32)
    cosine, sine_table = rope_tables(positions, head_size)
    rope_query = partial(rotate_norm, cosine=cosine, sine_table=sine_table)
    arrived = jnp.zeros((row_count, model_width), jnp.bfloat16)
    stored_steps, outgoing_steps = ([], [])
    for step_index in range(batch_count + 1):
        early = min(step_index, batch_count - 1)
        late = max(step_index - 1, 0)
        layer_in = jnp.where(
            section_first, inputs[early].astype(jnp.float32), arrived.astype(jnp.float32)
        )
        own_segs = jnp.where(section_first, segments[early], segments[late])
        doc_row = jnp.where(section_first, doc_table[early], doc_table[late])
        forward_normed = rms_scale(layer_in, gain_attn).astype(jnp.bfloat16)
        forward_queries = dot_plain(forward_normed, w_q)
        forward_key_raw = dot_plain(forward_normed, w_k)
        forward_value_raw = dot_plain(forward_normed, w_v).astype(jnp.bfloat16)
        forward_query_rot = rope_query(forward_queries, gain_q).astype(jnp.bfloat16)
        forward_key_rot = rope_query(forward_key_raw, gain_k).astype(jnp.bfloat16)
        forward_keys_all = lax.all_gather(forward_key_rot, DP, axis=0, tiled=True)
        forward_values_all = lax.all_gather(forward_value_raw, DP, axis=0, tiled=True)
        forward_allowed = (key_pos[None, :] <= positions[:, None]) & (
            own_segs[:, None] == doc_row[None, :]
        )
        forward_attn, forward_log_total = attend(
            forward_query_rot, forward_keys_all, forward_values_all, forward_allowed, head_size
        )
        forward_mixed = layer_in + lax.psum(dot_last(forward_attn, w_o), TENSOR)
        forward_normed_mlp = rms_scale(forward_mixed, gain_mlp).astype(jnp.bfloat16)
        forward_gate_raw = dot_plain(forward_normed_mlp, w_g)
        forward_up_raw = dot_plain(forward_normed_mlp, w_u)
        forward_activated = swiglu(forward_gate_raw, forward_up_raw).astype(jnp.bfloat16)
        layer_out = forward_mixed + lax.psum(dot_last(forward_activated, w_d), TENSOR)
        forward_stored = (
            layer_in,
            forward_normed,
            forward_queries,
            forward_key_raw,
            forward_query_rot,
            forward_key_rot,
            forward_value_raw,
            forward_attn,
            forward_log_total,
            forward_mixed,
            forward_normed_mlp,
            forward_gate_raw,
            forward_up_raw,
            forward_activated,
            forward_allowed,
        )
        layer_out, stored = (layer_out, forward_stored)
        outgoing = layer_out.astype(jnp.bfloat16)
        stored_steps.append(stored)
        outgoing_steps.append(outgoing)
        if step_index < batch_count:
            arrived = shifted(outgoing, SECTION, 1)
    section_out = jnp.stack(
        [
            jnp.where(section_first, outgoing_steps[batch_index], outgoing_steps[batch_index + 1])
            for batch_index in range(batch_count)
        ]
    )
    back_arrived = jnp.zeros((row_count, model_width), jnp.bfloat16)
    grad_steps = []
    totals = None
    norm_totals = None
    for step_index in range(batch_count + 1):
        early_batch = min(batch_count - step_index, batch_count - 1)
        late_batch = max(batch_count - 1 - step_index, 0)
        stored = jax.tree.map(
            lambda a, b: jnp.where(section_first, a, b),
            stored_steps[early_batch],
            stored_steps[late_batch + 1],
        )
        valid = jnp.where(
            section_first,
            jnp.float32(1.0 if step_index >= 1 else 0.0),
            jnp.float32(1.0 if step_index < batch_count else 0.0),
        )
        grad_out = (
            jnp.where(
                section_first,
                back_arrived.astype(jnp.float32),
                cotangent[late_batch].astype(jnp.float32),
            )
            * valid
        )
        (
            backward_layer_in,
            normed,
            queries,
            key_raw,
            query_rot,
            key_rot,
            value_raw,
            attn,
            log_total,
            mixed,
            normed_mlp,
            gate_raw,
            up_raw,
            activated,
            allowed,
        ) = stored[:15]
        keys_all = lax.all_gather(key_rot, DP, axis=0, tiled=True)
        values_all = lax.all_gather(value_raw, DP, axis=0, tiled=True)
        mlp_grad = grad_out.astype(jnp.bfloat16)
        act_grad = dot_plain(mlp_grad, w_d)
        grad_wd = dot_first(mlp_grad, activated)
        unused, swiglu_back = jax.vjp(swiglu, gate_raw, up_raw)
        gate_grad, up_grad = swiglu_back(act_grad)
        gate_grad = gate_grad.astype(jnp.bfloat16)
        up_grad = up_grad.astype(jnp.bfloat16)
        grad_wg = dot_first(normed_mlp, gate_grad)
        grad_wu = dot_first(normed_mlp, up_grad)
        normed_mlp_grad = lax.psum(
            (dot_last(gate_grad, w_g) + dot_last(up_grad, w_u)).astype(jnp.bfloat16), TENSOR
        ).astype(jnp.float32)
        unused, mlp_norm_back = jax.vjp(rms_scale, mixed, gain_mlp)
        mixed_part, grad_gain_mlp = mlp_norm_back(normed_mlp_grad)
        mixed_grad = grad_out + mixed_part
        branch_low = mixed_grad.astype(jnp.bfloat16)
        attn_grad = dot_plain(branch_low, w_o).astype(jnp.bfloat16)
        grad_wo = dot_first(branch_low, attn)
        query_back, key_back, value_back = attend_back(
            query_rot, keys_all, values_all, allowed, log_total, attn_grad, head_size
        )
        backward_key_total = lax.psum_scatter(
            key_back.astype(jnp.bfloat16), DP, scatter_dimension=0, tiled=True
        ).astype(jnp.float32)
        value_total = lax.psum_scatter(
            value_back.astype(jnp.bfloat16), DP, scatter_dimension=0, tiled=True
        )
        unused, key_rope_back = jax.vjp(rope_query, key_raw, gain_k)
        key_gradient, grad_gain_k = key_rope_back(backward_key_total)
        key_gradient = key_gradient.astype(jnp.bfloat16)
        unused, query_rope_back = jax.vjp(rope_query, queries, gain_q)
        query_grad, grad_gain_q = query_rope_back(query_back)
        query_grad = query_grad.astype(jnp.bfloat16)
        grad_wq = dot_first(normed, query_grad)
        grad_wk = dot_first(normed, key_gradient)
        grad_wv = dot_first(normed, value_total)
        normed_grad = lax.psum(
            (
                dot_last(query_grad, w_q) + dot_last(key_gradient, w_k) + dot_last(value_total, w_v)
            ).astype(jnp.bfloat16),
            TENSOR,
        ).astype(jnp.float32)
        unused, attn_norm_back = jax.vjp(rms_scale, backward_layer_in, gain_attn)
        input_part, grad_gain_attn = attn_norm_back(normed_grad)
        weight_part = (
            grad_wq,
            grad_wk,
            grad_wv,
            grad_wo,
            grad_wg,
            grad_wu,
            grad_wd,
            grad_gain_attn,
            grad_gain_mlp,
        )
        input_grad, weight_part, norm_part = (
            mixed_grad + input_part,
            weight_part,
            (grad_gain_q, grad_gain_k),
        )
        outgoing = input_grad.astype(jnp.bfloat16)
        grad_steps.append(outgoing)
        if step_index < batch_count:
            back_arrived = shifted(outgoing, SECTION, -1)
        totals = (
            weight_part if totals is None else tuple((a + b for a, b in zip(totals, weight_part)))
        )
        norm_totals = (
            norm_part
            if norm_totals is None
            else tuple((a + b for a, b in zip(norm_totals, norm_part)))
        )
    shards = jax.tree.map(
        lambda part: part.astype(jnp.float32),
        lax.psum_scatter(as_sent(totals), DP, scatter_dimension=0, tiled=True),
    )
    query_total, key_total = lax.psum(norm_totals, (TENSOR, DP))
    input_grads = jnp.stack(
        [
            jnp.where(
                section_first,
                grad_steps[batch_count - batch_index],
                grad_steps[batch_count - 1 - batch_index],
            )
            for batch_index in range(batch_count)
        ]
    )
    return (
        (section_out[None], input_grads[None])
        + tuple((member[None] for member in shards))
        + (query_total[None], key_total[None])
    )


def paired(x, axis, flip):
    count = lax.axis_size(axis)
    return lax.ppermute(x, axis, [(i, i ^ flip) for i in range(count)])


def ring_order(count):
    return list(range(0, count, 2)) + list(range(count - 1, 0, -2))


def ring(x, by):
    order = ring_order(lax.axis_size(DP))
    count = len(order)
    pairs = []
    for core, step in ((0, by), (1, -by)):
        for i in range(count):
            pairs.append((core * count + order[i], core * count + order[(i + step) % count]))
    return lax.ppermute(x, (TENSOR, DP), pairs)


def received_order(count):
    half = count // 2
    return [(0, False)] + [(s, lag) for s in range(1, half) for lag in (False, True)] + [(half, False)]


def near_chunks(count):
    return 2 * (count // 2 - 2) + 1


def gate(value, token):
    return lax.optimization_barrier((value, token))[0]


def whole_vmem(count):
    return [pl.BlockSpec(memory_space=pltpu.VMEM)] * count


def joined(pieces):
    rows = sum(piece.shape[0] for piece in pieces)
    width = pieces[0].shape[1]

    def kernel(*refs):
        at = 0
        for ref in refs[:-1]:
            refs[-1][at : at + ref.shape[0], :] = ref[...]
            at += ref.shape[0]

    return pl.pallas_call(
        kernel,
        out_shape=jax.ShapeDtypeStruct((rows, width), pieces[0].dtype),
        in_specs=whole_vmem(len(pieces)),
        out_specs=pl.BlockSpec(memory_space=pltpu.VMEM),
        cost_estimate=pl.CostEstimate(flops=0, bytes_accessed=4 * rows * width, transcendentals=0),
    )(*pieces)


def gather_ring(chunk):
    count = lax.axis_size(DP)
    half = count // 2
    lead, lag = chunk, paired(chunk, TENSOR, 1)
    chunks, token = [chunk], None
    for step in range(1, half + 1):
        lead = ring(lead, 1)
        chunks.append(lead)
        if step < half:
            lag = ring(lag, 1)
            chunks.append(lag)
        if step == half - 1:
            token = lead
    cut = near_chunks(count)
    near, far = joined(gate(chunks[:cut], token)), joined(chunks[cut:])
    return [near, far, paired(near, TENSOR, 1), paired(far, TENSOR, 1)], token


def multiplied(parts, weight):
    return jnp.concatenate(parts, axis=0), by_parts(parts, weight)


def by_parts(parts, weight):
    return jnp.concatenate([dot_plain(part, weight) for part in parts], axis=0)


def product_scattered(act, weight):
    count = lax.axis_size(DP)
    half = count // 2
    side = act.shape[0] // 2
    rows = side // count
    near = near_chunks(count) * rows
    far_sum = dot_last(act[side + near :], weight).astype(jnp.bfloat16)
    near_sum = dot_last(act[side : side + near], weight).astype(jnp.bfloat16)
    own = dot_last(act[:side], weight)
    far_sum = paired(far_sum, TENSOR, 1)
    near_sum = paired(near_sum, TENSOR, 1)
    spots = {key: i * rows for i, key in enumerate(received_order(count))}

    def part(hops, lag):
        at = spots[hops, lag]
        extra = far_sum[at - near :][:rows] if at >= near else near_sum[at : at + rows]
        return own[at : at + rows] + extra.astype(jnp.float32)

    def hop(value, hops, lag):
        total = part(hops, lag)
        if value is not None:
            total = total + value.astype(jnp.float32)
        return ring(total.astype(jnp.bfloat16), -1)

    lead = lag = token = None
    for hops in range(half, 0, -1):
        lead = hop(lead, hops, False)
        if hops < half:
            lag = hop(lag, hops, True)
        if hops == half:
            token = lead
    across = paired(lag, TENSOR, 1)
    return part(0, False) + lead.astype(jnp.float32) + across.astype(jnp.float32), token


def place_rows(blocks, flags, widths):
    count = len(blocks)
    rows, total = blocks[0].shape
    part = rows // 2

    def kernel(flags_ref, *refs):
        for s in range(count):
            left = 0
            for out, width in zip(refs[count:], widths):
                for half in range(2):
                    at = pl.multiple_of((flags_ref[0] ^ s) * part + half * count * part, part)
                    top = half * part
                    out[pl.ds(at, part), :] = refs[s][top : top + part, left : left + width]
                left += width

    size = 2 * count * rows * total
    return pl.pallas_call(
        kernel,
        out_shape=[jax.ShapeDtypeStruct((count * rows, w), blocks[0].dtype) for w in widths],
        in_specs=[pl.BlockSpec(memory_space=pltpu.SMEM)] + whole_vmem(count),
        out_specs=whole_vmem(len(widths)),
        cost_estimate=pl.CostEstimate(flops=0, bytes_accessed=2 * size, transcendentals=0),
    )(flags, *blocks)


def packed(pairs, flags, count):
    rows = pairs[0][0].shape[0] // count
    widths = [kept.shape[1] for kept, _ in pairs]

    def kernel(flags_ref, *refs):
        ins, outs = refs[: 2 * len(pairs)], refs[2 * len(pairs) :]
        for s, out in enumerate(outs):
            at = pl.ds(pl.multiple_of((flags_ref[0] ^ s) * rows, rows), rows)
            left = 0
            for i, width in enumerate(widths):
                value = ins[2 * i][at, :].astype(jnp.float32)
                value += ins[2 * i + 1][at, :].astype(jnp.float32)
                out[:, left : left + width] = value.astype(out.dtype)
                left += width

    operands = [array for pair in pairs for array in pair]
    size = 2 * count * rows * sum(widths)
    return pl.pallas_call(
        kernel,
        out_shape=[jax.ShapeDtypeStruct((rows, sum(widths)), jnp.bfloat16)] * count,
        in_specs=[pl.BlockSpec(memory_space=pltpu.SMEM)] + whole_vmem(len(operands)),
        out_specs=whole_vmem(count),
        cost_estimate=pl.CostEstimate(flops=0, bytes_accessed=3 * size, transcendentals=0),
    )(flags, *operands)


def place_columns(first, second, flags, widths, shared, skip):
    count = len(first)
    rows = first[0].shape[0]
    columns = [w * count // (2 if wide else 1) for w, wide in zip(widths, shared)]
    total = sum(columns)

    def kernel(flags_ref, *refs):
        kept, sent = refs[2 * count :]

        def fill(out, blocks, left):
            base = 0
            for width, wide, room in zip(widths, shared, columns):
                for s in range(0, count, 2 if wide else 1):
                    index = flags_ref[0] ^ s
                    at = base + (index // 2 if wide else index) * width
                    value = blocks[s][:, left : left + width]
                    if wide:
                        value = value.astype(jnp.float32) + blocks[s + 1][
                            :, left : left + width
                        ].astype(jnp.float32)
                    out[:, pl.ds(pl.multiple_of(at, 128), width)] = value.astype(out.dtype)
                left += width
                base += room

        @pl.when(flags_ref[1] == 0)
        def _():
            fill(kept, refs[:count], 0)
            fill(sent, refs[count : 2 * count], skip)

        @pl.when(flags_ref[1] != 0)
        def _():
            fill(sent, refs[:count], 0)
            fill(kept, refs[count : 2 * count], skip)

    return pl.pallas_call(
        kernel,
        out_shape=[jax.ShapeDtypeStruct((rows, total), first[0].dtype)] * 2,
        in_specs=[pl.BlockSpec(memory_space=pltpu.SMEM)] + whole_vmem(2 * count),
        out_specs=whole_vmem(2),
        cost_estimate=pl.CostEstimate(
            flops=0, bytes_accessed=4 * count * rows * sum(widths) * 2, transcendentals=0
        ),
    )(flags, *first, *second)


def head_attend(query, key, value, allowed):
    scores = dot_last(query, key) * query.shape[1] ** (-0.5)
    scores = jnp.where(allowed, scores, MASKED)
    highest = jnp.max(scores, axis=-1, keepdims=True)
    weights = jnp.exp(scores - highest)
    total = jnp.sum(weights, axis=-1, keepdims=True)
    probs = (weights / total).astype(jnp.bfloat16)
    return dot_plain(probs, value).astype(jnp.bfloat16), highest + jnp.log(total)


def head_attend_back(query, key, value, allowed, log_total, grad):
    scale = query.shape[1] ** (-0.5)
    scores = jnp.where(allowed, dot_last(query, key) * scale, MASKED)
    probs = jnp.exp(scores - log_total)
    prob_grad = dot_last(grad, value)
    delta = jnp.sum(probs * prob_grad, axis=-1, keepdims=True)
    score_grad = (probs * (prob_grad - delta)).astype(jnp.bfloat16)
    return (
        dot_plain(score_grad, key) * scale,
        dot_first(score_grad, query) * scale,
        dot_first(probs.astype(jnp.bfloat16), grad),
    )


def per_device(
    inputs,
    cotangent,
    segments,
    w_query,
    key_weight,
    value_weight,
    w_output,
    w_gate,
    w_up,
    w_down,
    attn_gain,
    mlp_gain,
    query_gain,
    key_gain,
):
    count = lax.axis_size(DP)
    plane = lax.axis_index(SECTION)
    me = lax.axis_index(DP)
    core = lax.axis_index(TENSOR)
    flags = jnp.stack([me, plane]).astype(jnp.int32)
    model_width = inputs.shape[2]
    rows = inputs.shape[1] // 2
    head_size = query_gain.shape[1]
    ff_width = w_gate.shape[2] // count
    group_size = w_query.shape[2] // key_weight.shape[2]
    gain_width = attn_gain.shape[1]

    def by_layer(own):
        theirs = paired(own, SECTION, 1)
        first = plane == 0
        return [jnp.where(first, own, theirs), jnp.where(first, theirs, own)]

    part = gain_width // 2

    def halved(array):
        wide = array.reshape(-1, count, 2, part)
        return jnp.swapaxes(wide, 1, 2).reshape(array.shape)

    def unhalved(array):
        wide = array.reshape(-1, 2, count, part)
        return jnp.swapaxes(wide, 1, 2).reshape(array.shape)

    def own_rows(array):
        own = lax.dynamic_slice(array, (plane, core * rows, 0), (1, rows, model_width))[0]
        return halved(own)

    gains = jnp.concatenate([attn_gain[0], mlp_gain[0], query_gain[0], key_gain[0]])
    gains = jnp.concatenate(by_layer(gains.astype(jnp.float32)))
    docs = lax.dynamic_index_in_dim(segments, plane, 0, keepdims=False).astype(jnp.float32)
    note = jnp.concatenate([gains, docs])
    notes = jnp.stack([note] + [paired(note, DP, s) for s in range(1, count)])
    notes = jnp.concatenate(
        [lax.dynamic_slice_in_dim(notes, me ^ j, 1, axis=0) for j in range(count)], axis=0
    )
    per_layer = gains.shape[0] // 2
    layer_gains = []
    for layer in range(2):
        at = layer * per_layer
        layer_gains.append(
            (
                halved(notes[:, at : at + gain_width].reshape(-1)),
                halved(notes[:, at + gain_width : at + 2 * gain_width].reshape(-1)),
                gains[at + 2 * gain_width : at + 2 * gain_width + head_size],
                gains[at + 2 * gain_width + head_size : at + per_layer],
            )
        )
    doc_table = notes[:, 2 * per_layer :].reshape(count, 2, rows)

    place = jnp.where(me % 2 == 0, me // 2, count - 1 - me // 2)
    docs_parts, pos_parts = ([], []), ([], [])
    away = 2 * core - 1
    for at in range(2):
        for hops, lag in received_order(count):
            side = core if lag == bool(at) else 1 - core
            spot = (place + (away if at == 0 else -away) * hops + count) % count
            owner = jnp.where(spot < count // 2, 2 * spot, 2 * (count - 1 - spot) + 1)
            block = lax.dynamic_index_in_dim(doc_table, owner, 0, keepdims=False)
            docs_parts[at].append(lax.dynamic_index_in_dim(block, side, 0, keepdims=False))
            start = owner * 2 * rows + side * rows
            pos_parts[at].append(start + jnp.arange(rows, dtype=jnp.int32))
    docs_all = jnp.concatenate(docs_parts[0] + docs_parts[1])
    positions = jnp.concatenate(pos_parts[0] + pos_parts[1])
    allowed = (positions[None, :] <= positions[:, None]) & (docs_all[:, None] == docs_all[None, :])
    cosine, sine_table = rope_tables(positions, head_size)
    rope = partial(rotate_norm, cosine=cosine, sine_table=sine_table)

    def cut(pieces):
        def block(to):
            return jnp.concatenate(
                [
                    lax.dynamic_slice_in_dim(
                        array, (to // share) * stride + skip, width, axis=1
                    )
                    for array, width, share, stride, skip in pieces
                ],
                axis=1,
            )

        return [block(me ^ s) for s in range(count)]

    def turn(blocks):
        moved = [blocks[0]]
        for s in range(1, count):
            moved.append(paired(blocks[s], DP, s))
        return moved

    def both_layers(blocks, widths):
        sets = []
        for placed in place_rows(blocks, flags, widths):
            facing = paired(placed, SECTION, 1)
            sets.append([jnp.where(plane == layer, placed, facing) for layer in range(2)])
        return sets

    wide = ff_width * 2 // 3

    def heads(array, share):
        return (array[0], head_size, share, head_size, 0)

    def hidden(array, width, skip):
        return (array[0], width, 1, ff_width, skip)

    sliced = {
        "qk": cut((heads(w_query, 1), heads(key_weight, group_size))),
        "vo": cut((heads(value_weight, group_size), heads(w_output, 1))),
        "g": cut((hidden(w_gate, ff_width, 0),)),
        "u": cut((hidden(w_up, ff_width, 0),)),
        "d": cut((hidden(w_down, wide, 0),)),
        "e": cut((hidden(w_down, ff_width - wide, wide),)),
    }
    turned, weights = {}, {}

    def attention(raw, value, layer):
        _, _, gain_q, gain_k = layer_gains[layer]
        queries, key_raw = raw[:, :head_size], raw[:, head_size:]
        value = value.astype(jnp.bfloat16)
        query_rot = rope(queries, gain_q).astype(jnp.bfloat16)
        key_rot = rope(key_raw, gain_k).astype(jnp.bfloat16)
        attn, log_total = head_attend(query_rot, key_rot, value, allowed)
        return attn, (queries, key_raw, value, query_rot, key_rot, log_total)

    def forward(layer_in, layer):
        gain_attn, gain_mlp, _, _ = layer_gains[layer]
        if layer == 0:
            turned["qk"] = turn(sliced["qk"])
            parts, token = gather_ring(layer_in.astype(jnp.bfloat16))
            raw_in = joined(parts).astype(jnp.float32)
            weights["qk"] = both_layers(turned["qk"], (2 * head_size,))[0]
            turned["vo"] = turn(gate(sliced["vo"], turned["qk"]))
            weights["v"], weights["o"] = both_layers(turned["vo"], (head_size, head_size))
            turned["g"] = turn(gate(sliced["g"], turned["vo"]))
            normed = rms_scale(raw_in, gain_attn).astype(jnp.bfloat16)
            raw = dot_plain(normed, weights["qk"][0])
            value = dot_plain(normed, weights["v"][0])
        else:
            chunk = rms_scale(layer_in, gain_attn).astype(jnp.bfloat16)
            parts, token = gather_ring(chunk)
            normed, raw = multiplied(parts, weights["qk"][layer])
            value = by_parts(parts, weights["v"][layer])
        attn, kept = attention(raw, value, layer)
        if layer == 0:
            turned["u"] = turn(gate(sliced["u"], turned["g"]))
            weights["g"] = both_layers(gate(turned["g"], raw), (ff_width,))[0]
            extra = None
        else:
            cotangent_rows = own_rows(cotangent)
            extra, token = gather_ring(gate(cotangent_rows, raw))
            attn = gate(attn, extra[1])
        summed, token = product_scattered(attn, weights["o"][layer])
        mixed = layer_in + summed
        if layer == 0:
            weights["u"] = both_layers(gate(turned["u"], token), (ff_width,))[0]
            turned["d"] = turn(gate(sliced["d"], turned["u"]))
            turned["e"] = turn(gate(sliced["e"], turned["d"]))
            weights["gu"] = [
                jnp.concatenate([weights["g"][i], weights["u"][i]], axis=1) for i in range(2)
            ]
        parts, token = gather_ring(rms_scale(mixed, gain_mlp).astype(jnp.bfloat16))
        if layer == 0:
            weights["d"] = both_layers(gate(turned["d"], token), (wide,))[0]
            weights["e"] = both_layers(gate(turned["e"], parts[1]), (ff_width - wide,))[0]
            weights["d"] = [
                jnp.concatenate([weights["d"][i], weights["e"][i]], axis=1) for i in range(2)
            ]
        normed_mlp, raw_mlp = multiplied(parts, weights["gu"][layer])
        gate_raw, up_raw = raw_mlp[:, :ff_width], raw_mlp[:, ff_width:]
        activated = swiglu(gate_raw, up_raw).astype(jnp.bfloat16)
        stored = (layer_in, normed, kept, attn, mixed, normed_mlp, gate_raw, up_raw, activated)

        def finish(after):
            held = activated if after is None else gate(activated, after)
            summed, _ = product_scattered(held, weights["d"][layer])
            return ((mixed + summed).astype(jnp.bfloat16),)

        return finish, stored, extra

    def halves(grad):
        span = grad.shape[0] // 2
        sent = lax.dynamic_slice_in_dim(grad, (1 - plane) * span, span, axis=0)
        kept = lax.dynamic_slice_in_dim(grad, plane * span, span, axis=0).astype(jnp.bfloat16)
        return kept, paired(sent.astype(jnp.bfloat16), SECTION, 1)

    turns = []

    def returned(pairs, token):
        if token is not None:
            pairs = [(kept, gate(taken, token)) for kept, taken in pairs]
        if len(turns) > 1:
            pairs = [(kept, gate(taken, turns[-2])) for kept, taken in pairs]
        turns.append(turn(packed(pairs, flags, count)))
        return turns[-1]

    def backward(gathered, grad_out, stored, layer, back, late):
        layer_in, normed, kept, attn, mixed, normed_mlp, gate_raw, up_raw, activated = stored
        queries, key_raw, value, query_rot, key_rot, log_total = kept
        gain_attn, gain_mlp, gain_q, gain_k = layer_gains[layer]
        if late is not None:
            late = late(None)
        out_low, act_grad = multiplied(gathered, weights["d"][layer])
        unused, swiglu_back = jax.vjp(swiglu, gate_raw, up_raw)
        gate_grad, up_grad = swiglu_back(act_grad)
        raw_grad = jnp.concatenate([gate_grad, up_grad], axis=1).astype(jnp.bfloat16)
        summed, token = product_scattered(raw_grad, weights["gu"][layer])
        sums = {}
        sums["d"] = halves(dot_first(out_low, activated))
        sums["gu"] = halves(dot_first(normed_mlp, raw_grad))
        unused, mlp_norm_back = jax.vjp(rms_scale, mixed, gain_mlp)
        mixed_part, grad_gain_mlp = mlp_norm_back(summed)
        mixed_grad = grad_out + mixed_part
        parts, token = gather_ring(mixed_grad.astype(jnp.bfloat16))
        attn_grad = by_parts(parts, weights["o"][layer])
        back["mlp"] = returned((sums["gu"], sums["d"]), parts[1])
        query_back, key_back, value_back = head_attend_back(
            query_rot, key_rot, value, allowed, log_total, attn_grad.astype(jnp.bfloat16)
        )
        unused, key_rope_back = jax.vjp(rope, key_raw, gain_k)
        key_grad, grad_gain_k = key_rope_back(key_back)
        unused, query_rope_back = jax.vjp(rope, queries, gain_q)
        query_grad, grad_gain_q = query_rope_back(query_back)
        qkv_grad = jnp.concatenate([query_grad, key_grad, value_back], axis=1).astype(jnp.bfloat16)
        summed, token = product_scattered(qkv_grad, weights["qkv"][layer])
        grad_o, top = 0.0, 0
        for rows_part in parts:
            span = rows_part.shape[0]
            grad_o = grad_o + dot_first(rows_part, attn[top : top + span])
            top += span
        grad_attn = jnp.concatenate([dot_first(normed, qkv_grad), grad_o], axis=1)
        sums = halves(grad_attn)
        unused, attn_norm_back = jax.vjp(rms_scale, layer_in, gain_attn)
        input_part, grad_gain_attn = attn_norm_back(summed)
        small = (grad_gain_attn, grad_gain_mlp, grad_gain_q, grad_gain_k)
        points = token
        return mixed_grad + input_part, sums, small, points, late

    finish, stored_first, _ = forward(own_rows(inputs).astype(jnp.float32), 0)
    out_first = finish(None)[0]
    weights["qkv"] = [
        jnp.concatenate([weights["qk"][i], weights["v"][i]], axis=1) for i in range(2)
    ]
    finish, stored_second, gathered = forward(out_first.astype(jnp.float32), 1)
    back_second, back_first = {}, {}
    grad_second, waiting, small_second, points, last = backward(
        gathered, own_rows(cotangent).astype(jnp.float32), stored_second, 1, back_second, finish
    )
    out_second = last[0]
    grad_second = grad_second.astype(jnp.bfloat16)
    gathered, _ = gather_ring(grad_second)
    back_second["attn"] = returned((waiting,), gathered[1])
    grad_first, waiting, small_first, points, last = backward(
        gathered, grad_second.astype(jnp.float32), stored_first, 0, back_first, None
    )
    grad_first = grad_first.astype(jnp.bfloat16)
    back_first["attn"] = returned((waiting,), None)

    def by_section(first, second):
        first, second = unhalved(first), unhalved(second)
        kept = jnp.where(plane == 0, first, second)
        taken = paired(jnp.where(plane == 0, second, first), SECTION, 1)
        both = jnp.where(plane == 0, jnp.stack([kept, taken]), jnp.stack([taken, kept]))
        facing = paired(both, TENSOR, 1)
        whole = jnp.where(
            core == 0,
            jnp.concatenate([both, facing], axis=1),
            jnp.concatenate([facing, both], axis=1),
        )
        return whole[None], facing

    section_out, _ = by_section(out_first, out_second)
    input_grads, facing = by_section(grad_first, grad_second)

    def owned(name, widths, shared, token):
        firsts, seconds = back_first[name], back_second[name]
        kept, sent = place_columns(firsts, seconds, flags, widths, shared, 0)
        taken = paired(sent, SECTION, 1)
        if token is not None:
            taken = gate(taken, token)
        whole, left = [], 0
        for width, wide in zip(widths, shared):
            right = left + width * count // (2 if wide else 1)
            mine, theirs = kept[:, left:right], taken[:, left:right]
            halves_up = jnp.concatenate([mine, theirs], axis=0)
            halves_down = jnp.concatenate([theirs, mine], axis=0)
            whole.append(jnp.where(plane == 0, halves_up, halves_down).astype(jnp.float32))
            left = right
        return whole

    mlp_grads = owned("mlp", (ff_width,) * 3, (False,) * 3, None)
    attn_grads = owned("attn", (head_size,) * 4, (False, True, True, False), facing)

    rows_of = jnp.concatenate(
        [
            part.reshape(count, -1)
            for small in (small_first, small_second)
            for part in (
                unhalved(small[0]),
                unhalved(small[1]),
                jnp.tile(small[2], count),
                jnp.tile(small[3], count),
            )
        ],
        axis=1,
    )

    gain_sum, step = rows_of, count // 2
    while step:
        bit = (me // step) % 2
        gain_sum = gain_sum.reshape(2, step, -1)
        kept = lax.dynamic_index_in_dim(gain_sum, bit, 0, keepdims=False)
        sent = lax.dynamic_index_in_dim(gain_sum, 1 - bit, 0, keepdims=False)
        gain_sum = kept + paired(sent, DP, step)
        step //= 2
    gain_sum = gain_sum.reshape(-1)
    gain_sum = gain_sum + paired(gain_sum, TENSOR, 1)
    gain_sum = gain_sum + paired(gain_sum, SECTION, 1)
    mine = jnp.where(plane == 0, gain_sum[:per_layer], gain_sum[per_layer:])
    grad_gain_attn = mine[:gain_width]
    grad_gain_mlp = mine[gain_width : 2 * gain_width]
    grad_gain_q = mine[2 * gain_width : 2 * gain_width + head_size]
    grad_gain_k = mine[2 * gain_width + head_size :]
    shards = (
        attn_grads[0], attn_grads[1], attn_grads[2], attn_grads[3],
        mlp_grads[0], mlp_grads[1], mlp_grads[2],
        grad_gain_attn, grad_gain_mlp, grad_gain_q, grad_gain_k,
    )
    return (section_out, input_grads) + tuple(part[None] for part in shards)


def fits(mesh):
    sizes = dict(mesh.shape)
    return sizes[DP] == 8 and sizes[TENSOR] == 2 and sizes[SECTION] == 2


def solution(mesh):
    return jax.shard_map(
        per_device if fits(mesh) else per_device_wide,
        mesh=mesh,
        in_specs=(
            P(None, DP, None),
            P(None, DP, None),
            P(None, DP),
            P(SECTION, DP, TENSOR),
            P(SECTION, DP, TENSOR),
            P(SECTION, DP, TENSOR),
            P(SECTION, DP, TENSOR),
            P(SECTION, DP, TENSOR),
            P(SECTION, DP, TENSOR),
            P(SECTION, DP, TENSOR),
            P(SECTION, DP),
            P(SECTION, DP),
            P(SECTION, None),
            P(SECTION, None),
        ),
        out_specs=(
            P(SECTION, None, DP, None),
            P(SECTION, None, DP, None),
            P(SECTION, DP, TENSOR),
            P(SECTION, DP, TENSOR),
            P(SECTION, DP, TENSOR),
            P(SECTION, DP, TENSOR),
            P(SECTION, DP, TENSOR),
            P(SECTION, DP, TENSOR),
            P(SECTION, DP, TENSOR),
            P(SECTION, DP),
            P(SECTION, DP),
            P(SECTION, None),
            P(SECTION, None),
        ),
        check_vma=False,
    )
```
